128 devices in a mesh: blk: 64 (over z_hi, x, y, core), feat: 2 (over z_lo).
Axes of the slice: x: 4, y: 4, z: 4 (z_hi: 2, z_lo: 2; z = z_hi * 2 + z_lo), core: 2. Of those that a mesh axis runs over, the one named last changes fastest.
Arguments:
- points: bfloat16 [65536, 64], P('blk', 'feat'), may hold values from -1.5 to 1.5
- vectors: bfloat16 [65536, 64], P('blk', 'feat'), may hold values from -5.5 to 5.5
- lengthscale: float32 [64], replicated, may hold values from 0.5 to 2
- outscale: float32 [1], replicated, may hold values from 0.1 to 0.4
- noise: float32 [1], replicated, may hold values from 0.05 to 0.5
Outputs:
- product: float32 [65536, 64], P('blk', 'feat')
The draws below stay inside these ranges and needn't reach their ends.
All inputs are finite; a program needn't handle non-finite values.
Results may differ from the reference program's by a relative error of at most 0.0026.
Values may be sent and summed in bfloat16 or wider, within the bound.
No kernel may reach another device: no remote copies, remote signals or barrier semaphores. Data moves between devices by JAX's collectives and lax.ppermute only.
A program may use at most 64 MiB of HBM per device.

```python
import math
import jax
import jax.numpy as jnp
from jax import lax

FEATS = 64
VECS = 64
PTS_DEV = 1024
POINTS = 65536


def draw_points(key, part):
    latent_width = FEATS // 4
    key_latent, key_map, key_noise, key_level = jax.random.split(jax.random.fold_in(key, 7), 4)
    spread = (0.5 / (FEATS * 1.35)) ** 0.5
    mapping = jax.random.normal(key_map, (latent_width, FEATS), jnp.float32) * spread
    jitter_level = jnp.exp(jax.random.uniform(key_level, (POINTS, 1), jnp.float32, math.log(0.04), math.log(0.3)))
    latent = jax.random.normal(key_latent, (POINTS, latent_width), jnp.float32)
    jitter = jax.random.normal(key_noise, (POINTS, FEATS), jnp.float32) * jitter_level
    values = jnp.dot(latent, mapping) + jitter
    return jnp.clip(values, -1.5, 1.5).astype(jnp.bfloat16)


def draw_vectors(key, part):
    key_noise, key_sign, key_size = jax.random.split(jax.random.fold_in(key, 11), 3)
    signs = jnp.where(jax.random.bernoulli(key_sign, 0.5, (VECS,)), 1.0, -1.0).astype(jnp.float32)
    offsets = signs * jax.random.uniform(key_size, (VECS,), jnp.float32, 0.75, 1.5)
    spread_part = jnp.clip(jax.random.normal(key_noise, (POINTS, VECS), jnp.float32), -4.0, 4.0)
    return (spread_part + offsets[None, :]).astype(jnp.bfloat16)


def setup_inputs(seed: int = 0) -> dict:
    key_of = jax.random.split(jax.random.key(seed), 6)
    return {
        "points": draw_points(jax.random.fold_in(key_of[5], 71), 0),
        "vectors": draw_vectors(jax.random.fold_in(key_of[5], 71), 0),
        "lengthscale": jnp.clip(jnp.exp(jax.random.uniform(key_of[2], (FEATS,), jnp.float32, math.log(0.5), math.log(2.0))), 0.5, 2.0),
        "outscale": jnp.clip(jnp.exp(jax.random.uniform(key_of[3], (1,), jnp.float32, math.log(0.1), math.log(0.4))), 0.1, 0.4),
        "noise": jnp.clip(jnp.exp(jax.random.uniform(key_of[4], (1,), jnp.float32, math.log(0.05), math.log(0.5))), 0.05, 0.5),
    }


def reference(points, vectors, lengthscale, outscale, noise):
    scaled = (points.astype(jnp.float32) / lengthscale).astype(jnp.bfloat16).astype(jnp.float32)
    norms = jnp.sum(scaled * scaled, axis=1)
    vector_wide = vectors.astype(jnp.float32)
    row_blocks = scaled.reshape(POINTS // PTS_DEV, PTS_DEV, FEATS)
    norm_blocks = norms.reshape(POINTS // PTS_DEV, PTS_DEV)

    def one_block(paired):
        block_rows, block_norms = paired
        inner = jnp.dot(block_rows, scaled.T, precision=lax.Precision.HIGHEST)
        distance = jnp.maximum(block_norms[:, None] + norms[None, :] - 2.0 * inner, 0.0)
        kernel_block = (outscale[0] * jnp.exp(-0.5 * distance)).astype(jnp.bfloat16).astype(jnp.float32)
        return jnp.dot(kernel_block, vector_wide, precision=lax.Precision.HIGHEST)

    result = lax.map(one_block, (row_blocks, norm_blocks)).reshape(POINTS, VECS)
    return result + noise[0] * vector_wide
```

```python
import jax
import jax.numpy as jnp
from jax import lax
from jax.experimental import pallas as pl
from jax.experimental.pallas import tpu as pltpu
from jax.sharding import Mesh, PartitionSpec as P

SIZES = (2, 4, 4, 2, 2)
NAMES = ("zh", "x", "y", "c", "zl")
BLK = ("zh", "x", "y", "c")
COLS = ("zh", "y", "c")
TM = 256
TN = 1024
F32 = jnp.float32
BF16 = jnp.bfloat16


def three_parts(wide):
    hi = wide.astype(BF16).astype(F32)
    mid = (wide - hi).astype(BF16).astype(F32)
    return hi, mid, wide - hi - mid


def with_norms(packed, offset, first, other):
    lane = lax.broadcasted_iota(jnp.int32, packed.shape, 1)
    wide = jnp.where(lane < 64, packed.astype(F32), 0.0)
    half = offset - 0.5 * jnp.sum(wide * wide, axis=1, keepdims=True)
    hi, mid, low = three_parts(half)
    ones = (lane >= other) & (lane < other + 3)
    wide = jnp.where(ones, 1.0, wide)
    wide = jnp.where(lane == first, hi, wide)
    wide = jnp.where(lane == first + 1, mid, wide)
    wide = jnp.where(lane == first + 2, low, wide)
    return wide.astype(BF16)


def kernel_body(amp_ref, rows_ref, cols_ref, out_ref, right_ref, vectors_ref):
    step = pl.program_id(0)
    total = cols_ref.shape[0]

    @pl.when(step == 0)
    def _():
        for at in range(0, total, TN):
            chunk = cols_ref[at : at + TN, :]
            right_ref[at : at + TN, :] = with_norms(chunk, 0.0, 64, 67)
            vectors_ref[:, at : at + TN] = chunk.astype(F32).T[64:, :].astype(BF16)

    rows = rows_ref[0].astype(F32)
    rows = jnp.where((step // 2) % 2 == 1, pltpu.roll(rows, 64, 1), rows)
    left = with_norms(rows, amp_ref[1], 67, 64)
    top = jnp.full((1, 1), amp_ref[0], F32).astype(BF16)
    total_sum = jnp.zeros((64, TM), F32)
    for at in range(0, total, TN):
        exponent = lax.dot_general(
            right_ref[at : at + TN, :], left, (((1,), (1,)), ((), ())), preferred_element_type=F32
        )
        block = jnp.minimum(jnp.exp(exponent).astype(BF16), top)
        total_sum += jnp.dot(vectors_ref[:, at : at + TN], block, preferred_element_type=F32)
    out_ref[0, 0] = total_sum[:32]
    out_ref[0, 1] = total_sum[32:]


def kernel_product(amp, rows, cols):
    groups, half, _ = rows.shape
    per = half // TM
    total = cols.shape[0]
    return pl.pallas_call(
        kernel_body,
        grid=(groups * 2 * per,),
        out_shape=jax.ShapeDtypeStruct((groups, 2, 32, 2 * half), F32),
        in_specs=[
            pl.BlockSpec(memory_space=pltpu.SMEM),
            pl.BlockSpec((1, TM, 128), lambda i: (i // (2 * per), i % per, 0)),
            pl.BlockSpec((total, 128), lambda i: (0, 0)),
        ],
        out_specs=pl.BlockSpec((1, 2, 32, TM), lambda i: (i // (2 * per), 0, 0, i % (2 * per))),
        scratch_shapes=[pltpu.VMEM((total, 128), BF16), pltpu.VMEM((64, total), BF16)],
        compiler_params=pltpu.CompilerParams(vmem_limit_bytes=48 << 20),
        name="rbf_product",
    )(amp, rows, cols)


def per_device(points, vectors, lengthscale, outscale, noise):
    zl = lax.axis_index("zl")
    length_slice = lax.dynamic_slice_in_dim(lengthscale, zl * 32, 32)
    scaled = (points.astype(F32) / length_slice).astype(BF16)
    mine = jnp.concatenate([scaled.T, vectors.T], axis=0)
    both = lax.all_gather(mine, "zl", axis=0, tiled=False)
    whole_points = both[:, :32].reshape(64, 1024)
    whole_vectors = both[:, 32:].reshape(64, 1024)
    rows = jnp.concatenate([whole_points[:, :512].T, whole_points[:, 512:].T], axis=1)
    share = jnp.concatenate([whole_points, whole_vectors], axis=0)
    share = lax.dynamic_slice_in_dim(share, zl * 512, 512, 1).T
    all_rows = lax.all_gather(rows, "x", axis=0, tiled=False)
    all_cols = lax.all_gather(share, COLS, axis=0, tiled=True)
    amp = jnp.concatenate([outscale, jnp.log(outscale)])
    partial = kernel_product(amp, all_rows, all_cols)
    result = lax.psum_scatter(partial.reshape(8, 32, 1024), ("x", "zl"), scatter_dimension=0, tiled=False)
    return result.T + noise[0] * vectors.astype(F32)


def solution(mesh):
    fine = Mesh(mesh.devices.reshape(SIZES), NAMES)
    placed = (P(BLK, "zl"), P(BLK, "zl"), P(), P(), P())
    return jax.shard_map(
        per_device, mesh=fine, in_specs=placed, out_specs=P(BLK, "zl"), check_vma=False
    )
```

```python
import jax
import jax.numpy as jnp
from jax import lax
from jax.experimental import pallas as pl
from jax.experimental.pallas import tpu as pltpu
from jax.sharding import Mesh, PartitionSpec as P

SIZES = (2, 4, 4, 2, 2)
NAMES = ("zh", "x", "y", "c", "zl")
BLK = ("zh", "x", "y", "c")
TM = 512
TN = 1024
F32 = jnp.float32
BF16 = jnp.bfloat16
PARAMS = pltpu.CompilerParams(vmem_limit_bytes=48 << 20)


def three_parts(wide):
    hi = wide.astype(BF16).astype(F32)
    mid = (wide - hi).astype(BF16).astype(F32)
    return hi, mid, wide - hi - mid


def with_norms(wide, offset, first, other):
    lane = lax.broadcasted_iota(jnp.int32, wide.shape, 1)
    wide = jnp.where(lane < 64, wide, 0.0)
    half = offset - 0.5 * jnp.sum(wide * wide, axis=1, keepdims=True)
    hi, mid, low = three_parts(half)
    ones = (lane >= other) & (lane < other + 3)
    wide = jnp.where(ones, 1.0, wide)
    wide = jnp.where(lane == first, hi, wide)
    wide = jnp.where(lane == first + 1, mid, wide)
    wide = jnp.where(lane == first + 2, low, wide)
    return wide.astype(BF16)


def ready_rows(amp, blocks):
    count = len(blocks)

    def body(amp_ref, *refs):
        out_ref = refs[count]
        for k in range(count):
            wide = refs[k][...].astype(F32)
            out_ref[k, :512] = with_norms(wide, amp_ref[1], 67, 64)
            out_ref[k, 512:] = with_norms(pltpu.roll(wide, 64, 1), amp_ref[1], 67, 64)

    return pl.pallas_call(
        body,
        out_shape=jax.ShapeDtypeStruct((count, 1024, 128), BF16),
        in_specs=[pl.BlockSpec(memory_space=pltpu.SMEM)]
        + [pl.BlockSpec(memory_space=pltpu.VMEM)] * count,
        out_specs=pl.BlockSpec(memory_space=pltpu.VMEM),
        compiler_params=PARAMS,
        name="ready_rows",
    )(amp, *blocks)


def ready_cols(blocks):
    count = len(blocks)
    total = sum(b.shape[0] for b in blocks)

    def body(*refs):
        right_ref, vectors_ref = refs[count:]
        at = 0
        for ref in refs[:count]:
            for sub in range(0, ref.shape[0], 512):
                wide = ref[sub : sub + 512, :].astype(F32)
                right_ref[at : at + 512, :] = with_norms(wide, 0.0, 64, 67)
                vectors_ref[:, at : at + 512] = wide.T[64:, :].astype(BF16)
                at += 512

    return pl.pallas_call(
        body,
        out_shape=(
            jax.ShapeDtypeStruct((total, 128), BF16),
            jax.ShapeDtypeStruct((64, total), BF16),
        ),
        in_specs=[pl.BlockSpec(memory_space=pltpu.VMEM)] * count,
        out_specs=(pl.BlockSpec(memory_space=pltpu.VMEM),) * 2,
        compiler_params=PARAMS,
        name="ready_cols",
    )(*blocks)


def tile_sum(amp_ref, left, right_ref, vectors_ref):
    top = jnp.full((1, 1), amp_ref[0], F32).astype(BF16)
    total = right_ref.shape[0]
    result = jnp.zeros((64, left.shape[0]), F32)
    for at in range(0, total, TN):
        exponent = lax.dot_general(
            right_ref[at : at + TN, :], left, (((1,), (1,)), ((), ())), preferred_element_type=F32
        )
        block = jnp.minimum(jnp.exp(exponent).astype(BF16), top)
        result += jnp.dot(vectors_ref[:, at : at + TN], block, preferred_element_type=F32)
    return result


def cost(rows, cols):
    return pl.CostEstimate(flops=rows * cols * 512, transcendentals=rows * cols, bytes_accessed=cols * 384)


def add_tiles(amp, left, right, vectors, before):
    total = right.shape[0]
    per = 1024 // TM
    old = [] if before is None else [before]

    def body(amp_ref, left_ref, right_ref, vectors_ref, *refs):
        value = tile_sum(amp_ref, left_ref[0], right_ref, vectors_ref)
        if old:
            value += refs[0][0]
        refs[-1][0] = value

    acc_spec = pl.BlockSpec((1, 64, TM), lambda i: (i // per, 0, i % per))
    return pl.pallas_call(
        body,
        grid=(4 * per,),
        out_shape=jax.ShapeDtypeStruct((4, 64, 1024), F32),
        in_specs=[
            pl.BlockSpec(memory_space=pltpu.SMEM),
            pl.BlockSpec((1, TM, 128), lambda i: (i // per, i % per, 0)),
            pl.BlockSpec((total, 128), lambda i: (0, 0)),
            pl.BlockSpec((64, total), lambda i: (0, 0)),
        ]
        + [acc_spec] * len(old),
        out_specs=acc_spec,
        compiler_params=PARAMS,
        cost_estimate=cost(4096, total),
        name="add_tiles",
    )(amp, left, right, vectors, *old)


def last_tiles(amp, left, right, vectors, before, group, kept):
    total = right.shape[0]

    def body(amp_ref, left_ref, right_ref, vectors_ref, before_ref, mine_ref, theirs_ref):
        value = tile_sum(amp_ref, left_ref[0], right_ref, vectors_ref) + before_ref[0]
        mine_ref[...] = value[:32].astype(kept)
        theirs_ref[...] = value[32:].astype(BF16)

    out_spec = pl.BlockSpec((32, TM), lambda i: (0, i))
    return pl.pallas_call(
        body,
        grid=(1024 // TM,),
        out_shape=(jax.ShapeDtypeStruct((32, 1024), kept), jax.ShapeDtypeStruct((32, 1024), BF16)),
        in_specs=[
            pl.BlockSpec(memory_space=pltpu.SMEM),
            pl.BlockSpec((1, TM, 128), lambda i: (group, i, 0)),
            pl.BlockSpec((total, 128), lambda i: (0, 0)),
            pl.BlockSpec((64, total), lambda i: (0, 0)),
            pl.BlockSpec((1, 64, TM), lambda i: (group, 0, i)),
        ],
        out_specs=(out_spec, out_spec),
        compiler_params=PARAMS,
        cost_estimate=cost(1024, total),
        name="last_tiles",
    )(amp, left, right, vectors, before)


def shift(value, axis, by):
    size = SIZES[NAMES.index(axis)]
    return lax.ppermute(value, axis, [(i, (i + by) % size) for i in range(size)])


def shift_swap(value, by):
    pairs = [(2 * i + j, 2 * ((i + by) % 4) + 1 - j) for i in range(4) for j in range(2)]
    return lax.ppermute(value, ("x", "zl"), pairs)


def per_device(points, vectors, lengthscale, outscale, noise):
    zl = lax.axis_index("zl")
    length_slice = lax.dynamic_slice_in_dim(lengthscale, zl * 32, 32)
    scaled = (points.astype(F32) / length_slice).astype(BF16).T
    flipped = vectors.T
    amp = jnp.concatenate([outscale, jnp.log(outscale)])

    given = jnp.concatenate(
        [scaled[:, :512], scaled[:, 512:], lax.dynamic_slice_in_dim(flipped, (1 - zl) * 512, 512, 1)], axis=0
    )
    got = shift(given, "zl", 1)
    low = jnp.concatenate([scaled[:, :512], got[:32]], axis=0)
    high = jnp.concatenate([scaled[:, 512:], got[32:64]], axis=0)
    rows = jnp.concatenate([low, high], axis=0).T
    share = jnp.concatenate(
        [
            jnp.where(zl == 0, low, high),
            lax.dynamic_slice_in_dim(flipped, zl * 512, 512, 1),
            got[64:],
        ],
        axis=0,
    ).T

    across = shift(share, "zh", 1)
    beside = shift(share, "c", 1)
    rows_in = [shift(rows, "x", by) for by in (1, -1, 2)]
    near = [shift(share, "y", by) for by in (1, -1, 2)]
    far = [across] + [shift(across, "y", by) for by in (1, -1, 2)]
    near = jnp.concatenate(near, axis=0)
    near_beside = shift(near, "c", 1)
    far = jnp.concatenate(far, axis=0)
    far_beside = shift(far, "c", 1)

    left = ready_rows(amp, [rows] + rows_in)
    acc = add_tiles(amp, left, *ready_cols([share, beside]), None)
    acc = add_tiles(amp, left, *ready_cols([near, near_beside]), acc)
    last = ready_cols([far, far_beside])

    arrived = []
    for group, by in ((3, 2), (1, -1), (2, 1)):
        mine, theirs = last_tiles(amp, left, *last, acc, group, BF16)
        arrived.append(shift(mine, "x", by))
        arrived.append(shift_swap(theirs, by))
    mine, theirs = last_tiles(amp, left, *last, acc, 0, F32)
    arrived.append(shift(theirs, "zl", 1))
    for part in arrived:
        mine = mine + part.astype(F32)
    return mine.T + noise[0] * vectors.astype(F32)


def solution(mesh):
    fine = Mesh(mesh.devices.reshape(SIZES), NAMES)
    placed = (P(BLK, "zl"), P(BLK, "zl"), P(), P(), P())
    return jax.shard_map(
        per_device, mesh=fine, in_specs=placed, out_specs=P(BLK, "zl"), check_vma=False
    )
```

```python
import jax
import jax.numpy as jnp
from jax import lax
from jax.experimental import pallas as pl
from jax.experimental.pallas import tpu as pltpu
from jax.sharding import Mesh, PartitionSpec as P

SIZES = (2, 4, 4, 2, 2)
NAMES = ("zh", "x", "y", "c", "zl")
BLK = ("zh", "x", "y", "c")
TM = 512
TN = 1024
F32 = jnp.float32
BF16 = jnp.bfloat16
PARAMS = pltpu.CompilerParams(vmem_limit_bytes=48 << 20)


def three_parts(wide):
    hi = wide.astype(BF16).astype(F32)
    mid = (wide - hi).astype(BF16).astype(F32)
    return hi, mid, wide - hi - mid


def with_norms(wide, offset, first, other):
    lane = lax.broadcasted_iota(jnp.int32, wide.shape, 1)
    wide = jnp.where(lane < 64, wide, 0.0)
    half = offset - 0.5 * jnp.sum(wide * wide, axis=1, keepdims=True)
    hi, mid, low = three_parts(half)
    ones = (lane >= other) & (lane < other + 3)
    wide = jnp.where(ones, 1.0, wide)
    wide = jnp.where(lane == first, hi, wide)
    wide = jnp.where(lane == first + 1, mid, wide)
    wide = jnp.where(lane == first + 2, low, wide)
    return wide.astype(BF16)


def ready_rows(amp, blocks):
    count = len(blocks)

    def body(amp_ref, *refs):
        out_ref = refs[count]
        for k in range(count):
            wide = refs[k][...].astype(F32)
            out_ref[k, :512] = with_norms(wide, amp_ref[1], 67, 64)
            out_ref[k, 512:] = with_norms(pltpu.roll(wide, 64, 1), amp_ref[1], 67, 64)

    return pl.pallas_call(
        body,
        out_shape=jax.ShapeDtypeStruct((count, 1024, 128), BF16),
        in_specs=[pl.BlockSpec(memory_space=pltpu.SMEM)]
        + [pl.BlockSpec(memory_space=pltpu.VMEM)] * count,
        out_specs=pl.BlockSpec(memory_space=pltpu.VMEM),
        compiler_params=PARAMS,
        name="ready_rows",
    )(amp, *blocks)


def ready_cols(blocks):
    count = len(blocks)
    total = sum(b.shape[0] for b in blocks)

    def body(*refs):
        right_ref, vectors_ref = refs[count:]
        at = 0
        for ref in refs[:count]:
            for sub in range(0, ref.shape[0], 512):
                wide = ref[sub : sub + 512, :].astype(F32)
                right_ref[at : at + 512, :] = with_norms(wide, 0.0, 64, 67)
                vectors_ref[:, at : at + 512] = wide.T[64:, :].astype(BF16)
                at += 512

    return pl.pallas_call(
        body,
        out_shape=(
            jax.ShapeDtypeStruct((total, 128), BF16),
            jax.ShapeDtypeStruct((64, total), BF16),
        ),
        in_specs=[pl.BlockSpec(memory_space=pltpu.VMEM)] * count,
        out_specs=(pl.BlockSpec(memory_space=pltpu.VMEM),) * 2,
        compiler_params=PARAMS,
        name="ready_cols",
    )(*blocks)


def tile_sum(amp_ref, left, pairs):
    top = jnp.full((1, 1), amp_ref[0], F32).astype(BF16)
    result = jnp.zeros((64, left.shape[0]), F32)
    for right_ref, vectors_ref in pairs:
        for at in range(0, right_ref.shape[0], TN):
            exponent = lax.dot_general(
                right_ref[at : at + TN, :], left, (((1,), (1,)), ((), ())), preferred_element_type=F32
            )
            block = jnp.minimum(jnp.exp(exponent).astype(BF16), top)
            result += jnp.dot(vectors_ref[:, at : at + TN], block, preferred_element_type=F32)
    return result


SCALE = 512


def cost(rows, cols):
    return pl.CostEstimate(flops=rows * cols * SCALE, transcendentals=0, bytes_accessed=cols * 384)


def add_tiles(amp, left, right, vectors, before):
    count = left.shape[0]
    total = right.shape[0]
    per = 1024 // TM
    old = [] if before is None else [before]

    def body(amp_ref, left_ref, right_ref, vectors_ref, *refs):
        value = tile_sum(amp_ref, left_ref[0], [(right_ref, vectors_ref)])
        if old:
            value += refs[0][0]
        refs[-1][0] = value

    acc_spec = pl.BlockSpec((1, 64, TM), lambda i: (i // per, 0, i % per))
    return pl.pallas_call(
        body,
        grid=(count * per,),
        out_shape=jax.ShapeDtypeStruct((count, 64, 1024), F32),
        in_specs=[
            pl.BlockSpec(memory_space=pltpu.SMEM),
            pl.BlockSpec((1, TM, 128), lambda i: (i // per, i % per, 0)),
            pl.BlockSpec((total, 128), lambda i: (0, 0)),
            pl.BlockSpec((64, total), lambda i: (0, 0)),
        ]
        + [acc_spec] * len(old),
        out_specs=acc_spec,
        compiler_params=PARAMS,
        cost_estimate=cost(1024 * count, total),
        name="add_tiles",
    )(amp, left, right, vectors, *old)


def last_tiles(amp, left, right, vectors, before):
    count = left.shape[0]
    total = right.shape[0]
    per = 1024 // TM

    def body(amp_ref, left_ref, right_ref, vectors_ref, before_ref, *out_refs):
        value = tile_sum(amp_ref, left_ref[0], [(right_ref, vectors_ref)]) + before_ref[0]
        for k in range(count):

            @pl.when(pl.program_id(0) // per == k)
            def _():
                out_refs[k][...] = value.astype(BF16)

    def place(k):
        return pl.BlockSpec((64, TM), lambda i: (0, jnp.clip(i - k * per, 0, per - 1)))

    return pl.pallas_call(
        body,
        grid=(count * per,),
        out_shape=[jax.ShapeDtypeStruct((64, 1024), BF16)] * count,
        in_specs=[
            pl.BlockSpec(memory_space=pltpu.SMEM),
            pl.BlockSpec((1, TM, 128), lambda i: (i // per, i % per, 0)),
            pl.BlockSpec((total, 128), lambda i: (0, 0)),
            pl.BlockSpec((64, total), lambda i: (0, 0)),
            pl.BlockSpec((1, 64, TM), lambda i: (i // per, 0, i % per)),
        ],
        out_specs=[place(k) for k in range(count)],
        compiler_params=PARAMS,
        cost_estimate=cost(1024 * count, total),
        name="last_tiles",
    )(amp, left, right, vectors, before)


def own_tiles(amp, left, ready):
    flat = [part for pair in ready for part in pair]

    def body(amp_ref, left_ref, *refs):
        pairs = [(refs[2 * k], refs[2 * k + 1]) for k in range(len(ready))]
        refs[-1][...] = tile_sum(amp_ref, left_ref[0], pairs)

    return pl.pallas_call(
        body,
        grid=(1024 // TM,),
        out_shape=jax.ShapeDtypeStruct((64, 1024), F32),
        in_specs=[
            pl.BlockSpec(memory_space=pltpu.SMEM),
            pl.BlockSpec((1, TM, 128), lambda i: (0, i, 0)),
        ]
        + [pl.BlockSpec(part.shape, lambda i: (0, 0)) for part in flat],
        out_specs=pl.BlockSpec((64, TM), lambda i: (0, i)),
        compiler_params=PARAMS,
        cost_estimate=cost(1024, sum(right.shape[0] for right, _ in ready)),
        name="own_tiles",
    )(amp, left, *flat)


def own_last(amp, left, right, vectors, before, arrived):
    count = len(arrived)
    total = right.shape[0]

    def body(amp_ref, left_ref, right_ref, vectors_ref, before_ref, *refs):
        mine_ref, theirs_ref = refs[count:]
        value = tile_sum(amp_ref, left_ref[0], [(right_ref, vectors_ref)]) + before_ref[...]
        for ref in refs[:count]:
            value += ref[...].astype(F32)
        mine_ref[...] = value[:32]
        theirs_ref[...] = value[32:].astype(BF16)

    out_spec = pl.BlockSpec((32, TM), lambda i: (0, i))
    return pl.pallas_call(
        body,
        grid=(1024 // TM,),
        out_shape=(jax.ShapeDtypeStruct((32, 1024), F32), jax.ShapeDtypeStruct((32, 1024), BF16)),
        in_specs=[
            pl.BlockSpec(memory_space=pltpu.SMEM),
            pl.BlockSpec((1, TM, 128), lambda i: (0, i, 0)),
            pl.BlockSpec((total, 128), lambda i: (0, 0)),
            pl.BlockSpec((64, total), lambda i: (0, 0)),
        ]
        + [pl.BlockSpec((64, TM), lambda i: (0, i))] * (count + 1),
        out_specs=(out_spec, out_spec),
        compiler_params=PARAMS,
        cost_estimate=cost(1024, total),
        name="own_last",
    )(amp, left, right, vectors, before, *arrived)


def shift(value, axis, by):
    size = SIZES[NAMES.index(axis)]
    return lax.ppermute(value, axis, [(i, (i + by) % size) for i in range(size)])


def per_device(points, vectors, lengthscale, outscale, noise):
    zl = lax.axis_index("zl")
    length_slice = lax.dynamic_slice_in_dim(lengthscale, zl * 32, 32)
    scaled = (points.astype(F32) / length_slice).astype(BF16).T
    flipped = vectors.T
    amp = jnp.concatenate([outscale, jnp.log(outscale)])

    given = jnp.concatenate(
        [scaled[:, :512], scaled[:, 512:], lax.dynamic_slice_in_dim(flipped, (1 - zl) * 512, 512, 1)], axis=0
    )
    got = shift(given, "zl", 1)
    low = jnp.concatenate([scaled[:, :512], got[:32]], axis=0)
    high = jnp.concatenate([scaled[:, 512:], got[32:64]], axis=0)
    rows = jnp.concatenate([low, high], axis=0).T
    share = jnp.concatenate(
        [
            jnp.where(zl == 0, low, high),
            lax.dynamic_slice_in_dim(flipped, zl * 512, 512, 1),
            got[64:],
        ],
        axis=0,
    ).T

    beside = shift(share, "c", 1)
    near = [shift(share, "y", by) for by in (1, -1, 2)]
    rows_in = [shift(rows, "x", by) for by in (1, -1, 2)]
    near[2], rows_in[0] = lax.optimization_barrier((near[2], rows_in[0]))
    near = jnp.concatenate(near, axis=0)
    near_beside = shift(near, "c", 1)
    far = shift(jnp.concatenate([share, near], axis=0), "zh", 1)
    own_left = ready_rows(amp, [rows])
    left = ready_rows(amp, rows_in)
    ready = [ready_cols([share, beside])]
    acc = add_tiles(amp, left, *ready[0], None)
    ready.append(ready_cols([near, near_beside]))
    acc = add_tiles(amp, left, *ready[1], acc)
    far, acc = lax.optimization_barrier((far, acc))
    far_beside = shift(far, "c", 1)
    ready.append(ready_cols([far]))
    acc = add_tiles(amp, left, *ready[2], acc)
    ready.append(ready_cols([far_beside]))

    sent = last_tiles(amp, left, *ready[3], acc)
    arrived = [shift(part, "x", by) for part, by in zip(sent, (-1, 1, 2))]
    own = own_tiles(amp, own_left, [ready[0], ready[1], ready[2]])
    mine, theirs = own_last(amp, own_left, *ready[3], own, arrived)
    mine = mine + shift(theirs, "zl", 1).astype(F32)
    return mine.T + noise[0] * vectors.astype(F32)


def solution(mesh):
    fine = Mesh(mesh.devices.reshape(SIZES), NAMES)
    placed = (P(BLK, "zl"), P(BLK, "zl"), P(), P(), P())
    return jax.shard_map(
        per_device, mesh=fine, in_specs=placed, out_specs=P(BLK, "zl"), check_vma=False
    )
```

```python
import jax
import jax.numpy as jnp
from jax import lax
from jax.experimental import pallas as pl
from jax.experimental.pallas import tpu as pltpu
from jax.sharding import Mesh, PartitionSpec as P

SIZES = (2, 4, 4, 2, 2)
NAMES = ("zh", "x", "y", "c", "zl")
BLK = ("zh", "x", "y", "c")
TM = 512
TN = 1024
F32 = jnp.float32
BF16 = jnp.bfloat16
PARAMS = pltpu.CompilerParams(vmem_limit_bytes=48 << 20)


def three_parts(wide):
    hi = wide.astype(BF16).astype(F32)
    mid = (wide - hi).astype(BF16).astype(F32)
    return hi, mid, wide - hi - mid


def with_norms(wide, offset, first, other):
    lane = lax.broadcasted_iota(jnp.int32, wide.shape, 1)
    wide = jnp.where(lane < 64, wide, 0.0)
    half = offset - 0.5 * jnp.sum(wide * wide, axis=1, keepdims=True)
    hi, mid, low = three_parts(half)
    ones = (lane >= other) & (lane < other + 3)
    wide = jnp.where(ones, 1.0, wide)
    wide = jnp.where(lane == first, hi, wide)
    wide = jnp.where(lane == first + 1, mid, wide)
    wide = jnp.where(lane == first + 2, low, wide)
    return wide.astype(BF16)


def ready_rows(amp, blocks):
    count = len(blocks)

    def body(amp_ref, *refs):
        out_ref = refs[count]
        for k in range(count):
            wide = refs[k][...].astype(F32)
            out_ref[k, :512] = with_norms(wide, amp_ref[1], 67, 64)
            out_ref[k, 512:] = with_norms(pltpu.roll(wide, 64, 1), amp_ref[1], 67, 64)

    return pl.pallas_call(
        body,
        out_shape=jax.ShapeDtypeStruct((count, 1024, 128), BF16),
        in_specs=[pl.BlockSpec(memory_space=pltpu.SMEM)]
        + [pl.BlockSpec(memory_space=pltpu.VMEM)] * count,
        out_specs=pl.BlockSpec(memory_space=pltpu.VMEM),
        compiler_params=PARAMS,
        name="ready_rows",
    )(amp, *blocks)


def first_pack(zl, points, vectors, lengthscale):
    def body(zl_ref, points_ref, vectors_ref, length_ref, out_ref):
        at = zl_ref[0]
        lane = lax.broadcasted_iota(jnp.int32, (32, 64), 1)
        row = lax.broadcasted_iota(jnp.int32, (32, 64), 0)
        column = jnp.sum(jnp.where(lane == row + 32 * at, length_ref[...], 0.0), axis=1, keepdims=True)
        scaled = (points_ref[...].astype(F32) / column).astype(BF16)
        out_ref[:32] = scaled[:, :512]
        out_ref[32:64] = scaled[:, 512:]
        given = vectors_ref[...].astype(F32)
        out_ref[64:] = jnp.where(at == 0, given[:, 512:], given[:, :512]).astype(BF16)

    return pl.pallas_call(
        body,
        out_shape=jax.ShapeDtypeStruct((96, 512), BF16),
        in_specs=[
            pl.BlockSpec(memory_space=pltpu.SMEM),
            pl.BlockSpec((32, 1024), lambda i: (0, 0)),
            pl.BlockSpec((32, 1024), lambda i: (0, 0)),
            pl.BlockSpec((1, 64), lambda i: (0, 0)),
        ],
        grid=(1,),
        out_specs=pl.BlockSpec((96, 512), lambda i: (0, 0)),
        compiler_params=PARAMS,
        name="first_pack",
    )(zl, points, vectors, lengthscale.reshape(1, 64))


def second_pack(zl, given, got, vectors):
    def body(zl_ref, given_ref, got_ref, vectors_ref, rows_ref, share_ref):
        first = zl_ref[0] == 0
        mine = given_ref[...].astype(F32)
        theirs = got_ref[...].astype(F32)
        both = vectors_ref[...].astype(F32)
        whole = jnp.concatenate([mine[:32], theirs[:32], mine[32:64], theirs[32:64]], axis=0)
        rows_ref[...] = whole.T.astype(BF16)
        picked = jnp.concatenate(
            [
                jnp.where(first, whole[:64], whole[64:]),
                jnp.where(first, both[:, :512], both[:, 512:]),
                theirs[64:],
            ],
            axis=0,
        )
        share_ref[...] = picked.T.astype(BF16)

    packed = jax.ShapeDtypeStruct((512, 128), BF16)
    return pl.pallas_call(
        body,
        out_shape=(packed, packed),
        in_specs=[pl.BlockSpec(memory_space=pltpu.SMEM)] + [pl.BlockSpec(memory_space=pltpu.VMEM)] * 3,
        out_specs=(pl.BlockSpec(memory_space=pltpu.VMEM),) * 2,
        compiler_params=PARAMS,
        name="second_pack",
    )(zl, given, got, vectors)


def one_block(amp_ref, left, right, vectors, top):
    exponent = lax.dot_general(right, left, (((1,), (1,)), ((), ())), preferred_element_type=F32)
    block = jnp.minimum(jnp.exp(exponent).astype(BF16), top)
    return jnp.dot(vectors, block, preferred_element_type=F32)


def amplitude(amp_ref):
    return jnp.full((1, 1), amp_ref[0], F32).astype(BF16)


def tile_sum(amp_ref, left, pairs):
    top = amplitude(amp_ref)
    result = jnp.zeros((64, left.shape[0]), F32)
    for right_ref, vectors_ref in pairs:
        for at in range(0, right_ref.shape[0], TN):
            result += one_block(
                amp_ref, left, right_ref[at : at + TN, :], vectors_ref[:, at : at + TN], top
            )
    return result


def raw_sum(amp_ref, left, raw_refs, right_ref, vectors_ref):
    top = amplitude(amp_ref)
    result = jnp.zeros((64, left.shape[0]), F32)
    at = 0
    for ref in raw_refs:
        for sub in range(0, ref.shape[0], 512):
            wide = ref[sub : sub + 512, :].astype(F32)
            right_ref[at : at + 512, :] = with_norms(wide, 0.0, 64, 67)
            vectors_ref[:, at : at + 512] = wide.T[64:, :].astype(BF16)
            at += 512
            if at % TN == 0:
                back = at - TN
                result += one_block(
                    amp_ref, left, right_ref[back:at, :], vectors_ref[:, back:at], top
                )
    return result


SCALE = 512


def cost(rows, cols):
    return pl.CostEstimate(flops=rows * cols * SCALE, transcendentals=0, bytes_accessed=cols * 384)


def add_tiles(amp, left, raws, before, narrow):
    count = left.shape[0]
    total = sum(raw.shape[0] for raw in raws)
    per = 1024 // TM
    old = [] if before is None else [before]
    sums = count if narrow else 1

    def body(amp_ref, left_ref, *refs):
        raw_refs = refs[: len(raws)]
        before_refs = refs[len(raws) : len(raws) + len(old)]
        sum_refs = refs[len(raws) + len(old) : len(raws) + len(old) + sums]
        right_ref, vectors_ref = refs[-2:]
        step = pl.program_id(0)

        def put(value):
            if before_refs:
                value += before_refs[0][0]
            if not narrow:
                sum_refs[0][0] = value
                return
            for k in range(count):

                @pl.when(step // per == k)
                def _():
                    sum_refs[k][...] = value.astype(BF16)

        @pl.when(step == 0)
        def _():
            put(raw_sum(amp_ref, left_ref[0], raw_refs, right_ref, vectors_ref))

        @pl.when(step > 0)
        def _():
            put(tile_sum(amp_ref, left_ref[0], [(right_ref, vectors_ref)]))

    def place(k):
        return pl.BlockSpec((64, TM), lambda i: (0, jnp.clip(i - k * per, 0, per - 1)))

    acc_spec = pl.BlockSpec((1, 64, TM), lambda i: (i // per, 0, i % per))
    if narrow:
        sum_shapes = [jax.ShapeDtypeStruct((64, 1024), BF16)] * count
        sum_specs = [place(k) for k in range(count)]
    else:
        sum_shapes = [jax.ShapeDtypeStruct((count, 64, 1024), F32)]
        sum_specs = [acc_spec]
    out = pl.pallas_call(
        body,
        grid=(count * per,),
        out_shape=sum_shapes
        + [jax.ShapeDtypeStruct((total, 128), BF16), jax.ShapeDtypeStruct((64, total), BF16)],
        in_specs=[
            pl.BlockSpec(memory_space=pltpu.SMEM),
            pl.BlockSpec((1, TM, 128), lambda i: (i // per, i % per, 0)),
        ]
        + [pl.BlockSpec(raw.shape, lambda i: (0, 0)) for raw in raws]
        + [acc_spec] * len(old),
        out_specs=sum_specs
        + [pl.BlockSpec((total, 128), lambda i: (0, 0)), pl.BlockSpec((64, total), lambda i: (0, 0))],
        compiler_params=PARAMS,
        cost_estimate=cost(1024 * count, total),
        name="add_tiles",
    )(amp, left, *raws, *old)
    return out[:sums], tuple(out[sums:])


def own_tiles(amp, left, ready):
    flat = [part for pair in ready for part in pair]

    def body(amp_ref, left_ref, *refs):
        pairs = [(refs[2 * k], refs[2 * k + 1]) for k in range(len(ready))]
        refs[-1][...] = tile_sum(amp_ref, left_ref[0], pairs)

    return pl.pallas_call(
        body,
        grid=(1024 // TM,),
        out_shape=jax.ShapeDtypeStruct((64, 1024), F32),
        in_specs=[
            pl.BlockSpec(memory_space=pltpu.SMEM),
            pl.BlockSpec((1, TM, 128), lambda i: (0, i, 0)),
        ]
        + [pl.BlockSpec(part.shape, lambda i: (0, 0)) for part in flat],
        out_specs=pl.BlockSpec((64, TM), lambda i: (0, i)),
        compiler_params=PARAMS,
        cost_estimate=cost(1024, sum(right.shape[0] for right, _ in ready)),
        name="own_tiles",
    )(amp, left, *flat)


def own_last(amp, left, right, vectors, before, arrived):
    count = len(arrived)
    total = right.shape[0]

    def body(amp_ref, left_ref, right_ref, vectors_ref, before_ref, *refs):
        mine_ref, theirs_ref = refs[count:]
        value = tile_sum(amp_ref, left_ref[0], [(right_ref, vectors_ref)]) + before_ref[...]
        for ref in refs[:count]:
            value += ref[...].astype(F32)
        mine_ref[...] = value[:32]
        theirs_ref[...] = value[32:]

    out_spec = pl.BlockSpec((32, TM), lambda i: (0, i))
    return pl.pallas_call(
        body,
        grid=(1024 // TM,),
        out_shape=(jax.ShapeDtypeStruct((32, 1024), F32), jax.ShapeDtypeStruct((32, 1024), F32)),
        in_specs=[
            pl.BlockSpec(memory_space=pltpu.SMEM),
            pl.BlockSpec((1, TM, 128), lambda i: (0, i, 0)),
            pl.BlockSpec((total, 128), lambda i: (0, 0)),
            pl.BlockSpec((64, total), lambda i: (0, 0)),
        ]
        + [pl.BlockSpec((64, TM), lambda i: (0, i))] * (count + 1),
        out_specs=(out_spec, out_spec),
        compiler_params=PARAMS,
        cost_estimate=cost(1024, total),
        name="own_last",
    )(amp, left, right, vectors, before, *arrived)


def shift(value, axis, by):
    size = SIZES[NAMES.index(axis)]
    return lax.ppermute(value, axis, [(i, (i + by) % size) for i in range(size)])


def per_device(points, vectors, lengthscale, outscale, noise):
    zl = lax.axis_index("zl").astype(jnp.int32).reshape(1)
    amp = jnp.concatenate([outscale, jnp.log(outscale)])

    given = first_pack(zl, points.T, vectors.T, lengthscale)
    got = shift(given, "zl", 1)
    rows, share = second_pack(zl, given, got, vectors.T)

    near = [shift(share, "y", by) for by in (1, -1, 2)]
    rows_in = [shift(rows, "x", by) for by in (1, -1, 2)]
    beside = shift(share, "c", 1)
    near[2], rows_in[0] = lax.optimization_barrier((near[2], rows_in[0]))
    near = jnp.concatenate(near, axis=0)
    near_beside = shift(near, "c", 1)
    far = shift(jnp.concatenate([share, near], axis=0), "zh", 1)

    own_left = ready_rows(amp, [rows])
    left = ready_rows(amp, rows_in)
    (acc,), ready0 = add_tiles(amp, left, [share, beside], None, False)
    (acc,), ready1 = add_tiles(amp, left, [near, near_beside], acc, False)
    far, acc = lax.optimization_barrier((far, acc))
    far_beside = shift(far, "c", 1)
    (acc,), ready2 = add_tiles(amp, left, [far], acc, False)
    sent, ready3 = add_tiles(amp, left, [far_beside], acc, True)
    arrived = [shift(part, "x", by) for part, by in zip(sent, (-1, 1, 2))]
    own = own_tiles(amp, own_left, [ready0, ready1, ready2])
    mine, theirs = own_last(amp, own_left, *ready3, own, arrived)
    mine = mine + shift(theirs, "zl", 1)
    return mine.T + noise[0] * vectors.astype(F32)


def solution(mesh):
    fine = Mesh(mesh.devices.reshape(SIZES), NAMES)
    placed = (P(BLK, "zl"), P(BLK, "zl"), P(), P(), P())
    return jax.shard_map(
        per_device, mesh=fine, in_specs=placed, out_specs=P(BLK, "zl"), check_vma=False
    )
```

```python
import jax
import jax.numpy as jnp
from jax import lax
from jax.experimental import pallas as pl
from jax.experimental.pallas import tpu as pltpu
from jax.sharding import Mesh, PartitionSpec as P

SIZES = (2, 4, 4, 2, 2)
NAMES = ("zh", "x", "y", "c", "zl")
BLK = ("zh", "x", "y", "c")
TM = 256
TN = 512
STEP = 512
LOG2E = 1.4426950408889634
LIFT = 64.0
F8 = jnp.float8_e4m3fn
F32 = jnp.float32
BF16 = jnp.bfloat16
PARAMS = pltpu.CompilerParams(vmem_limit_bytes=48 << 20)


def parts(wide, lanes_low):
    high = wide.astype(F8).astype(F32)
    return jnp.where(lanes_low, high, wide - high)


def lanes_of(shape):
    return lax.broadcasted_iota(jnp.int32, shape, 1) < 64


def ready_rows(amp, blocks):
    count = len(blocks)

    def body(amp_ref, *refs):
        left_ref, norm_ref = refs[count:]
        low = lanes_of((512, 128))
        for k in range(count):
            wide = refs[k][...].astype(F32)
            flipped = wide.T
            flipped = flipped * flipped
            turned = pltpu.roll(wide, 64, 1)
            for half in range(2):
                at = 512 * half
                same = jnp.where(low, wide, turned) if half == 0 else jnp.where(low, turned, wide)
                both = same * LIFT
                high = both.astype(F8)
                left_ref[k, at : at + 512, :128] = high
                left_ref[k, at : at + 512, 128:] = (both - high.astype(F32)).astype(F8)
                norm = jnp.sum(flipped[64 * half : 64 * half + 64], axis=0, keepdims=True)
                norm_ref[k, :, at : at + 512] = amp_ref[1] - (0.5 * LOG2E) * norm

    return pl.pallas_call(
        body,
        out_shape=(
            jax.ShapeDtypeStruct((count, 1024, 256), F8),
            jax.ShapeDtypeStruct((count, 1, 1024), F32),
        ),
        in_specs=[pl.BlockSpec(memory_space=pltpu.SMEM)]
        + [pl.BlockSpec(memory_space=pltpu.VMEM)] * count,
        out_specs=(pl.BlockSpec(memory_space=pltpu.VMEM),) * 2,
        compiler_params=PARAMS,
        name="ready_rows",
    )(amp, *blocks)


def first_pack(zl, points, vectors, lengthscale):
    def body(zl_ref, points_in, vectors_in, length_in, out_ref, kept_ref, points_ref, vectors_ref, length_ref, sems):
        copies = [
            pltpu.make_async_copy(length_in, length_ref, sems.at[0]),
            pltpu.make_async_copy(points_in, points_ref, sems.at[1]),
            pltpu.make_async_copy(vectors_in, vectors_ref, sems.at[2]),
        ]
        for copy in copies:
            copy.start()
        for copy in copies:
            copy.wait()
        at = zl_ref[0]
        lane = lax.broadcasted_iota(jnp.int32, (32, 64), 1)
        row = lax.broadcasted_iota(jnp.int32, (32, 64), 0)
        column = jnp.sum(jnp.where(lane == row + 32 * at, length_ref[...], 0.0), axis=1, keepdims=True)
        scaled = (points_ref[...].astype(F32) / column).astype(BF16)
        out_ref[:32] = scaled[:, :512]
        out_ref[32:64] = scaled[:, 512:]
        given = vectors_ref[...].astype(F32)
        out_ref[64:] = jnp.where(at == 0, given[:, 512:], given[:, :512]).astype(BF16)
        kept_ref[...] = jnp.where(at == 0, given[:, :512], given[:, 512:]).astype(BF16)

    return pl.pallas_call(
        body,
        out_shape=(jax.ShapeDtypeStruct((96, 512), BF16), jax.ShapeDtypeStruct((32, 512), BF16)),
        in_specs=[pl.BlockSpec(memory_space=pltpu.SMEM)] + [pl.BlockSpec(memory_space=pltpu.HBM)] * 3,
        out_specs=(pl.BlockSpec(memory_space=pltpu.VMEM),) * 2,
        scratch_shapes=[
            pltpu.VMEM((32, 1024), BF16),
            pltpu.VMEM((32, 1024), BF16),
            pltpu.VMEM((1, 64), F32),
            pltpu.SemaphoreType.DMA((3,)),
        ],
        compiler_params=PARAMS,
        name="first_pack",
    )(zl, points, vectors, lengthscale.reshape(1, 64))


def second_pack(zl, given, got, kept):
    def body(zl_ref, given_ref, got_ref, kept_ref, rows_ref, share_ref):
        first = zl_ref[0] == 0
        mine = given_ref[...].astype(F32)
        theirs = got_ref[...].astype(F32)
        whole = jnp.concatenate([mine[:32], theirs[:32], mine[32:64], theirs[32:64]], axis=0)
        rows_ref[...] = whole.T.astype(BF16)
        picked = jnp.concatenate(
            [
                jnp.where(first, whole[:64], whole[64:]),
                kept_ref[...].astype(F32),
                theirs[64:],
            ],
            axis=0,
        )
        share_ref[...] = picked.T.astype(BF16)

    packed = jax.ShapeDtypeStruct((512, 128), BF16)
    return pl.pallas_call(
        body,
        out_shape=(packed, packed),
        in_specs=[pl.BlockSpec(memory_space=pltpu.SMEM)] + [pl.BlockSpec(memory_space=pltpu.VMEM)] * 3,
        out_specs=(pl.BlockSpec(memory_space=pltpu.VMEM),) * 2,
        compiler_params=PARAMS,
        name="second_pack",
    )(zl, given, got, kept)


def one_block(left, row_norm, right, norm, vectors, top):
    inner = lax.dot_general(right, left, (((1,), (1,)), ((), ())), preferred_element_type=F32)
    wide_norm = jnp.concatenate([norm] * (left.shape[0] // 128), axis=1)
    exponent = (inner * (LOG2E / (LIFT * LIFT)) + row_norm) + wide_norm
    block = jnp.minimum(jnp.exp2(exponent).astype(BF16), top)
    return jnp.dot(vectors, block, preferred_element_type=F32)


def amplitude(amp_ref):
    return jnp.full((1, 1), amp_ref[0], F32).astype(BF16)


def tile_sum(amp_ref, left, row_norm, ready_refs):
    top = amplitude(amp_ref)
    sums = []
    for m in range(0, STEP, TM):
        result = jnp.zeros((64, TM), F32)
        for right_ref, norm_ref, vectors_ref in ready_refs:
            for at in range(0, right_ref.shape[0], TN):
                part = slice(at, at + TN)
                result += one_block(
                    left[m : m + TM], row_norm[:, m : m + TM],
                    right_ref[part, :], norm_ref[part, :], vectors_ref[:, part], top,
                )
        sums.append(result)
    return jnp.concatenate(sums, axis=1)


def ready_cols(raw_refs, right_ref, norm_ref, vectors_ref):
    low = lanes_of((512, 128))
    at = 0
    for ref in raw_refs:
        for sub in range(0, ref.shape[0], 512):
            part = slice(at, at + 512)
            wide = ref[sub : sub + 512, :].astype(F32)
            vectors_ref[:, part] = wide.T[64:, :].astype(BF16)
            narrow = parts(jnp.where(low, wide, pltpu.roll(wide, 64, 1)) * LIFT, low).astype(F8)
            right_ref[part, :128] = narrow
            right_ref[part, 128:] = narrow
            own = jnp.where(low, wide, 0.0)
            norm = (-0.5 * LOG2E) * jnp.sum(own * own, axis=1, keepdims=True)
            norm_ref[part, :] = jnp.broadcast_to(norm, (512, 128))
            at += 512


def ready_shapes(total):
    return [
        jax.ShapeDtypeStruct((total, 256), F8),
        jax.ShapeDtypeStruct((total, 128), F32),
        jax.ShapeDtypeStruct((64, total), BF16),
    ]


def whole(arrays):
    return [pl.BlockSpec(a.shape, lambda i: (0, 0)) for a in arrays]


SCALE = 512


def cost(rows, cols):
    return pl.CostEstimate(flops=rows * cols * SCALE, transcendentals=0, bytes_accessed=cols * 384)


def row_specs():
    per = 1024 // STEP
    return [
        pl.BlockSpec(memory_space=pltpu.SMEM),
        pl.BlockSpec((1, STEP, 256), lambda i: (i // per, i % per, 0)),
        pl.BlockSpec((1, 1, STEP), lambda i: (i // per, 0, i % per)),
    ]


def add_tiles(amp, left, raws, before, narrow):
    count = left[0].shape[0]
    total = sum(raw.shape[0] for raw in raws)
    per = 1024 // STEP
    old = [] if before is None else [before]
    sums = count if narrow else 1

    def body(amp_ref, left_ref, row_norm_ref, *refs):
        raw_refs = refs[: len(raws)]
        before_refs = refs[len(raws) : len(raws) + len(old)]
        sum_refs = refs[len(raws) + len(old) : len(raws) + len(old) + sums]
        ready_refs = refs[-3:]
        step = pl.program_id(0)

        @pl.when(step == 0)
        def _():
            ready_cols(raw_refs, *ready_refs)

        value = tile_sum(amp_ref, left_ref[0], row_norm_ref[0], [ready_refs])
        if before_refs:
            value += before_refs[0][0]
        if not narrow:
            sum_refs[0][0] = value
            return
        for k in range(count):

            @pl.when(step // per == k)
            def _():
                sum_refs[k][...] = value.astype(BF16)

    def place(k):
        return pl.BlockSpec((64, STEP), lambda i: (0, jnp.clip(i - k * per, 0, per - 1)))

    acc_spec = pl.BlockSpec((1, 64, STEP), lambda i: (i // per, 0, i % per))
    if narrow:
        sum_shapes = [jax.ShapeDtypeStruct((64, 1024), BF16)] * count
        sum_specs = [place(k) for k in range(count)]
    else:
        sum_shapes = [jax.ShapeDtypeStruct((count, 64, 1024), F32)]
        sum_specs = [acc_spec]
    ready = ready_shapes(total)
    out = pl.pallas_call(
        body,
        grid=(count * per,),
        out_shape=sum_shapes + ready,
        in_specs=row_specs() + whole(raws) + [acc_spec] * len(old),
        out_specs=sum_specs + whole(ready),
        compiler_params=PARAMS,
        cost_estimate=cost(1024 * count, total),
        name="add_tiles",
    )(amp, *left, *raws, *old)
    return out[:sums], tuple(out[sums:])


def own_tiles(amp, left, ready):
    flat = [part for group in ready for part in group]

    def body(amp_ref, left_ref, row_norm_ref, *refs):
        groups = [refs[3 * k : 3 * k + 3] for k in range(len(ready))]
        refs[-1][...] = tile_sum(amp_ref, left_ref[0], row_norm_ref[0], groups)

    return pl.pallas_call(
        body,
        grid=(1024 // STEP,),
        out_shape=jax.ShapeDtypeStruct((64, 1024), F32),
        in_specs=row_specs() + whole(flat),
        out_specs=pl.BlockSpec((64, STEP), lambda i: (0, i)),
        compiler_params=PARAMS,
        cost_estimate=cost(1024, sum(group[0].shape[0] for group in ready)),
        name="own_tiles",
    )(amp, *left, *flat)


def own_last(amp, left, ready, before, arrived):
    count = len(arrived)

    def body(amp_ref, left_ref, row_norm_ref, right_ref, norm_ref, vectors_ref, before_ref, *refs):
        mine_ref, theirs_ref = refs[count:]
        groups = [(right_ref, norm_ref, vectors_ref)]
        value = tile_sum(amp_ref, left_ref[0], row_norm_ref[0], groups) + before_ref[...]
        for ref in refs[:count]:
            value += ref[...].astype(F32)
        mine_ref[...] = value[:32]
        theirs_ref[...] = value[32:]

    out_spec = pl.BlockSpec((32, STEP), lambda i: (0, i))
    half = jax.ShapeDtypeStruct((32, 1024), F32)
    return pl.pallas_call(
        body,
        grid=(1024 // STEP,),
        out_shape=(half, half),
        in_specs=row_specs()
        + whole(ready)
        + [pl.BlockSpec((64, STEP), lambda i: (0, i))] * (count + 1),
        out_specs=(out_spec, out_spec),
        compiler_params=PARAMS,
        cost_estimate=cost(1024, ready[0].shape[0]),
        name="own_last",
    )(amp, *left, *ready, before, *arrived)


def shift(value, axis, by):
    size = SIZES[NAMES.index(axis)]
    return lax.ppermute(value, axis, [(i, (i + by) % size) for i in range(size)])


def per_device(points, vectors, lengthscale, outscale, noise):
    zl = lax.axis_index("zl").astype(jnp.int32).reshape(1)
    amp = jnp.concatenate([outscale, jnp.log(outscale) * LOG2E])

    given, kept = first_pack(zl, points.T, vectors.T, lengthscale)
    got = shift(given, "zl", 1)
    rows, share = second_pack(zl, given, got, kept)

    near = [shift(share, "y", by) for by in (1, -1, 2)]
    rows_in = [shift(rows, "x", by) for by in (1, -1, 2)]
    beside = shift(share, "c", 1)
    own_left = ready_rows(amp, [rows])
    near[2], rows_in[0], own_left = lax.optimization_barrier((near[2], rows_in[0], own_left))
    near = jnp.concatenate(near, axis=0)
    near_beside = shift(near, "c", 1)
    far = shift(jnp.concatenate([share, near], axis=0), "zh", 1)

    left = ready_rows(amp, rows_in)
    (acc,), ready0 = add_tiles(amp, left, [share, beside], None, False)
    (acc,), ready1 = add_tiles(amp, left, [near, near_beside], acc, False)
    far, acc = lax.optimization_barrier((far, acc))
    far_beside = shift(far, "c", 1)
    (acc,), ready2 = add_tiles(amp, left, [far], acc, False)
    sent, ready3 = add_tiles(amp, left, [far_beside], acc, True)
    arrived = [shift(part, "x", by) for part, by in zip(sent, (-1, 1, 2))]
    own = own_tiles(amp, own_left, [ready0, ready1, ready2])
    mine, theirs = own_last(amp, own_left, ready3, own, arrived)
    mine = mine + shift(theirs, "zl", 1)
    return mine.T + noise[0] * vectors.astype(F32)


def solution(mesh):
    fine = Mesh(mesh.devices.reshape(SIZES), NAMES)
    placed = (P(BLK, "zl"), P(BLK, "zl"), P(), P(), P())
    return jax.shard_map(
        per_device, mesh=fine, in_specs=placed, out_specs=P(BLK, "zl"), check_vma=False
    )
```

```python
import jax
import jax.numpy as jnp
from jax import lax
from jax.experimental import pallas as pl
from jax.experimental.pallas import tpu as pltpu
from jax.sharding import Mesh, PartitionSpec as P

SIZES = (2, 4, 4, 2, 2)
NAMES = ("zh", "x", "y", "c", "zl")
BLK = ("zh", "x", "y", "c")
TM = 512
TN = 1024
F32 = jnp.float32
BF16 = jnp.bfloat16
PARAMS = pltpu.CompilerParams(vmem_limit_bytes=48 << 20)


SCALE = 512


def cost(rows, cols):
    return pl.CostEstimate(flops=rows * cols * SCALE, transcendentals=0, bytes_accessed=cols * 384)


def three_parts(wide):
    hi = wide.astype(BF16).astype(F32)
    mid = (wide - hi).astype(BF16).astype(F32)
    return hi, mid, wide - hi - mid


def with_norms(wide, offset, first, other):
    lane = lax.broadcasted_iota(jnp.int32, wide.shape, 1)
    wide = jnp.where(lane < 64, wide, 0.0)
    half = offset - 0.5 * jnp.sum(wide * wide, axis=1, keepdims=True)
    hi, mid, low = three_parts(half)
    ones = (lane >= other) & (lane < other + 3)
    wide = jnp.where(ones, 1.0, wide)
    wide = jnp.where(lane == first, hi, wide)
    wide = jnp.where(lane == first + 1, mid, wide)
    wide = jnp.where(lane == first + 2, low, wide)
    return wide.astype(BF16)


def ready_rows(amp, mines, theirs):
    count = len(mines)

    def body(amp_ref, *refs):
        theirs_ref, out_ref = refs[count:]
        for k in range(count):
            for half in range(2):
                low = 32 * half
                mine = refs[k][low : low + 32, :].astype(F32)
                other = theirs_ref[64 * k + low : 64 * k + low + 32, :].astype(F32)
                wide = jnp.concatenate([mine, other, mine, other], axis=0).T
                out_ref[k, 512 * half : 512 * half + 512] = with_norms(wide, amp_ref[1], 67, 64)

    return pl.pallas_call(
        body,
        out_shape=jax.ShapeDtypeStruct((count, 1024, 128), BF16),
        in_specs=[pl.BlockSpec(memory_space=pltpu.SMEM)]
        + [pl.BlockSpec(memory_space=pltpu.VMEM)] * (count + 1),
        out_specs=pl.BlockSpec(memory_space=pltpu.VMEM),
        compiler_params=PARAMS,
        name="ready_rows",
    )(amp, *mines, theirs)


def first_pack(zl, points, vectors, lengthscale):
    def body(zl_ref, points_ref, vectors_ref, length_ref, out_ref, kept_ref):
        at = zl_ref[0]
        lane = lax.broadcasted_iota(jnp.int32, (32, 64), 1)
        row = lax.broadcasted_iota(jnp.int32, (32, 64), 0)
        column = jnp.sum(jnp.where(lane == row + 32 * at, length_ref[...], 0.0), axis=1, keepdims=True)
        scaled = (points_ref[...].astype(F32) / column).astype(BF16)
        out_ref[:32] = scaled[:, :512]
        out_ref[32:64] = scaled[:, 512:]
        given = vectors_ref[...].astype(F32)
        out_ref[64:] = jnp.where(at == 0, given[:, 512:], given[:, :512]).astype(BF16)
        kept_ref[...] = jnp.where(at == 0, given[:, :512], given[:, 512:]).astype(BF16)

    return pl.pallas_call(
        body,
        out_shape=[jax.ShapeDtypeStruct((n, 512), BF16) for n in (96, 32)],
        in_specs=[pl.BlockSpec(memory_space=pltpu.SMEM)] + [pl.BlockSpec(memory_space=pltpu.VMEM)] * 3,
        out_specs=[pl.BlockSpec(memory_space=pltpu.VMEM)] * 2,
        compiler_params=PARAMS,
        name="first_pack",
    )(zl, points, vectors, lengthscale.reshape(1, 64))


def copy_of(parts, rows, token, weight):
    def body(token_ref, *refs):
        at = 0
        for ref in refs[:-1]:
            refs[-1][at : at + rows] = ref[:rows]
            at += rows

    return pl.pallas_call(
        body,
        out_shape=jax.ShapeDtypeStruct((rows * len(parts), parts[0].shape[1]), BF16),
        in_specs=[pl.BlockSpec(memory_space=pl.ANY)]
        + [pl.BlockSpec(memory_space=pltpu.VMEM)] * len(parts),
        out_specs=pl.BlockSpec(memory_space=pltpu.VMEM),
        compiler_params=PARAMS,
        cost_estimate=cost(weight, 1024),
        name="copy_of",
    )(token, *parts)


def second_pack(zl, amp, half, got, kept):
    def body(zl_ref, amp_ref, half_ref, got_ref, kept_ref, rows_ref, share_ref):
        first = zl_ref[0] == 0
        mine = half_ref[...].astype(F32)
        theirs = got_ref[...].astype(F32)
        low = jnp.concatenate([mine[:32], theirs[:32]], axis=0)
        high = jnp.concatenate([mine[32:], theirs[32:64]], axis=0)
        picked = jnp.where(first, low, high)
        share_ref[...] = jnp.concatenate([picked, kept_ref[...].astype(F32), theirs[64:]], axis=0).T.astype(BF16)
        for k, wide in enumerate((low, high)):
            wide = jnp.concatenate([wide, wide], axis=0).T
            rows_ref[0, 512 * k : 512 * k + 512] = with_norms(wide, amp_ref[1], 67, 64)

    return pl.pallas_call(
        body,
        out_shape=[jax.ShapeDtypeStruct((1, 1024, 128), BF16), jax.ShapeDtypeStruct((512, 128), BF16)],
        in_specs=[pl.BlockSpec(memory_space=pltpu.SMEM)] * 2 + [pl.BlockSpec(memory_space=pltpu.VMEM)] * 3,
        out_specs=[pl.BlockSpec(memory_space=pltpu.VMEM)] * 2,
        compiler_params=PARAMS,
        name="second_pack",
    )(zl, amp, half, got, kept)


def one_block(left, right, vectors, top):
    exponent = lax.dot_general(right, left, (((1,), (1,)), ((), ())), preferred_element_type=F32)
    block = jnp.minimum(jnp.exp(exponent).astype(BF16), top)
    return jnp.dot(vectors, block, preferred_element_type=F32)


def ready_sum(left, pairs, top):
    result = jnp.zeros((64, left.shape[0]), F32)
    for right_ref, vectors_ref in pairs:
        total = right_ref.shape[0]
        for at in range(0, total, TN):
            part = slice(at, min(at + TN, total))
            result += one_block(left, right_ref[part, :], vectors_ref[:, part], top)
    return result


def raw_sum(left, raws, right_ref, vectors_ref, top):
    total = right_ref.shape[0]
    result = jnp.zeros((64, left.shape[0]), F32)
    at = back = 0
    for ref, start in raws:
        for sub in range(start, ref.shape[0], 512):
            wide = ref[sub : sub + 512, :].astype(F32)
            right_ref[at : at + 512, :] = with_norms(wide, 0.0, 64, 67)
            vectors_ref[:, at : at + 512] = wide.T[64:, :].astype(BF16)
            at += 512
            if at - back == TN or at == total:
                result += one_block(left, right_ref[back:at, :], vectors_ref[:, back:at], top)
                back = at
    return result


def add_tiles(amp, left, ready, raws, before=None, narrow=False, weight=1024):
    count = left.shape[0]
    flat = [part for pair in ready for part in pair]
    total = sum(raw.shape[0] - start for raw, start in raws)
    cols = total + sum(right.shape[0] for right, _ in ready)
    per = 1024 // TM
    old = [] if before is None else [before]
    sums = count if narrow else 1
    ends = [len(flat), len(raws), len(old), sums]

    def body(amp_ref, left_ref, *refs):
        groups = []
        for size in ends:
            groups.append(refs[:size])
            refs = refs[size:]
        flat_refs, raw_refs, before_refs, sum_refs = groups
        pairs = [(flat_refs[2 * k], flat_refs[2 * k + 1]) for k in range(len(ready))]
        step = pl.program_id(0)
        top = jnp.full((1, 1), amp_ref[0], F32).astype(BF16)

        def put(value):
            if before_refs:
                value += before_refs[0][0]
            if not narrow:
                sum_refs[0][0] = value
                return
            for k in range(count):

                @pl.when(step // per == k)
                def _():
                    sum_refs[k][...] = value.astype(BF16)

        def tiles(fresh):
            value = ready_sum(left_ref[0], pairs if fresh or not raws else pairs + [tuple(refs)], top)
            if fresh:
                starts = [(ref, start) for ref, (_, start) in zip(raw_refs, raws)]
                value += raw_sum(left_ref[0], starts, *refs, top)
            put(value)

        if not raws:
            tiles(False)
            return

        @pl.when(step == 0)
        def _():
            tiles(True)

        @pl.when(step > 0)
        def _():
            tiles(False)

    def place(k):
        return pl.BlockSpec((64, TM), lambda i: (0, jnp.clip(i - k * per, 0, per - 1)))

    def whole(array):
        return pl.BlockSpec(array.shape, lambda i: (0, 0))

    acc_spec = pl.BlockSpec((1, 64, TM), lambda i: (i // per, 0, i % per))
    if narrow:
        sum_shapes = [jax.ShapeDtypeStruct((64, 1024), BF16)] * count
        sum_specs = [place(k) for k in range(count)]
    else:
        sum_shapes = [jax.ShapeDtypeStruct((count, 64, 1024), F32)]
        sum_specs = [acc_spec]
    made = []
    if raws:
        made = [jax.ShapeDtypeStruct((total, 128), BF16), jax.ShapeDtypeStruct((64, total), BF16)]
    out = pl.pallas_call(
        body,
        grid=(count * per,),
        out_shape=sum_shapes + made,
        in_specs=[
            pl.BlockSpec(memory_space=pltpu.SMEM),
            pl.BlockSpec((1, TM, 128), lambda i: (i // per, i % per, 0)),
        ]
        + [whole(part) for part in flat]
        + [whole(raw) for raw, _ in raws]
        + [acc_spec] * len(old),
        out_specs=sum_specs + [whole(part) for part in made],
        compiler_params=PARAMS,
        cost_estimate=cost(weight * count, cols),
        name="add_tiles",
    )(amp, left, *flat, *[raw for raw, _ in raws], *old)
    return (out[:sums] if narrow else out[0]), tuple(out[sums:])


def shift(value, axis, by):
    size = SIZES[NAMES.index(axis)]
    return lax.ppermute(value, axis, [(i, (i + by) % size) for i in range(size)])


def per_device(points, vectors, lengthscale, outscale, noise):
    zl = lax.axis_index("zl").astype(jnp.int32).reshape(1)
    amp = jnp.concatenate([outscale, jnp.log(outscale)])

    given, kept = first_pack(zl, points.T, vectors.T, lengthscale)
    got = shift(given, "zl", 1)
    half = copy_of([given], 64, kept, 4096)
    mines = [shift(half, "x", by) for by in (1, -1, 2)]
    own_left, share = second_pack(zl, amp, half, got, kept)

    beside = shift(share, "c", 1)
    near = [shift(share, "y", by) for by in (1, -1, 2)]
    mined = copy_of(mines, 64, share, 16)
    mined, beside = lax.optimization_barrier((mined, beside))
    theirs = shift(mined, "zl", 1)
    own, ready0 = add_tiles(amp, own_left, [], [(share, 0), (beside, 0)], weight=4096)
    near[0], near[1], near[2], own = lax.optimization_barrier((near[0], near[1], near[2], own))
    merged = jnp.concatenate([share] + near, axis=0)
    far = shift(merged, "zh", 1)
    merged_beside = shift(merged, "c", 1)
    own, ready1 = add_tiles(amp, own_left, [], [(merged, 512)], own, weight=64)

    theirs, own = lax.optimization_barrier((theirs, own))
    left = ready_rows(amp, mines, theirs)
    acc, ready2 = add_tiles(amp, left, [ready0, ready1], [(merged_beside, 512)])
    far, acc = lax.optimization_barrier((far, acc))
    far_beside = shift(far, "c", 1)
    acc, ready3 = add_tiles(amp, left, [], [(far, 0)], acc)
    sent, ready4 = add_tiles(amp, left, [], [(far_beside, 0)], acc, narrow=True)
    arrived = [shift(part, "x", by) for part, by in zip(sent, (-1, 1, 2))]
    own, _ = add_tiles(amp, own_left, [ready2, ready3, ready4], [], own)
    own = own[0]
    for part in arrived:
        own = own + part.astype(F32)
    result = own[:32] + shift(own[32:], "zl", 1)
    return result.T + noise[0] * vectors.astype(F32)


def solution(mesh):
    fine = Mesh(mesh.devices.reshape(SIZES), NAMES)
    placed = (P(BLK, "zl"), P(BLK, "zl"), P(), P(), P())
    return jax.shard_map(
        per_device, mesh=fine, in_specs=placed, out_specs=P(BLK, "zl"), check_vma=False
    )
```

```python
import jax
import jax.numpy as jnp
from jax import lax
from jax.experimental import pallas as pl
from jax.experimental.pallas import tpu as pltpu
from jax.sharding import Mesh, PartitionSpec as P

SIZES = (2, 4, 4, 2, 2)
NAMES = ("zh", "x", "y", "c", "zl")
BLK = ("zh", "x", "y", "c")
TM = 512
TN = 1024
F32 = jnp.float32
BF16 = jnp.bfloat16
PARAMS = pltpu.CompilerParams(vmem_limit_bytes=48 << 20)


SCALE = 512


def cost(rows, cols):
    return pl.CostEstimate(flops=rows * cols * SCALE, transcendentals=0, bytes_accessed=cols * 384)


def three_parts(wide):
    hi = wide.astype(BF16).astype(F32)
    mid = (wide - hi).astype(BF16).astype(F32)
    return hi, mid, wide - hi - mid


def with_norms(wide, offset, first, other):
    lane = lax.broadcasted_iota(jnp.int32, wide.shape, 1)
    wide = jnp.where(lane < 64, wide, 0.0)
    half = offset - 0.5 * jnp.sum(wide * wide, axis=1, keepdims=True)
    hi, mid, low = three_parts(half)
    ones = (lane >= other) & (lane < other + 3)
    wide = jnp.where(ones, 1.0, wide)
    wide = jnp.where(lane == first, hi, wide)
    wide = jnp.where(lane == first + 1, mid, wide)
    wide = jnp.where(lane == first + 2, low, wide)
    return wide.astype(BF16)


def ready_rows(amp, mines, theirs):
    count = len(mines)

    def body(amp_ref, *refs):
        theirs_ref, out_ref = refs[count:]
        for k in range(count):
            for half in range(2):
                low = 32 * half
                mine = refs[k][low : low + 32, :].astype(F32)
                other = theirs_ref[64 * k + low : 64 * k + low + 32, :].astype(F32)
                wide = jnp.concatenate([mine, other, mine, other], axis=0).T
                out_ref[k, 512 * half : 512 * half + 512] = with_norms(wide, amp_ref[1], 67, 64)

    return pl.pallas_call(
        body,
        out_shape=jax.ShapeDtypeStruct((count, 1024, 128), BF16),
        in_specs=[pl.BlockSpec(memory_space=pltpu.SMEM)]
        + [pl.BlockSpec(memory_space=pltpu.VMEM)] * (count + 1),
        out_specs=pl.BlockSpec(memory_space=pltpu.VMEM),
        compiler_params=PARAMS,
        name="ready_rows",
    )(amp, *mines, theirs)


def first_pack(zl, points, vectors, lengthscale):
    def body(zl_ref, points_ref, vectors_ref, length_ref, out_ref, kept_ref):
        at = zl_ref[0]
        lane = lax.broadcasted_iota(jnp.int32, (32, 64), 1)
        row = lax.broadcasted_iota(jnp.int32, (32, 64), 0)
        column = jnp.sum(jnp.where(lane == row + 32 * at, length_ref[...], 0.0), axis=1, keepdims=True)
        scaled = (points_ref[...].astype(F32) / column).astype(BF16)
        out_ref[:32] = scaled[:, :512]
        out_ref[32:64] = scaled[:, 512:]
        given = vectors_ref[...].astype(F32)
        out_ref[64:] = jnp.where(at == 0, given[:, 512:], given[:, :512]).astype(BF16)
        kept_ref[...] = jnp.where(at == 0, given[:, :512], given[:, 512:]).astype(BF16)

    return pl.pallas_call(
        body,
        out_shape=[jax.ShapeDtypeStruct((n, 512), BF16) for n in (96, 32)],
        in_specs=[pl.BlockSpec(memory_space=pltpu.SMEM)] + [pl.BlockSpec(memory_space=pltpu.VMEM)] * 3,
        out_specs=[pl.BlockSpec(memory_space=pltpu.VMEM)] * 2,
        compiler_params=PARAMS,
        name="first_pack",
    )(zl, points, vectors, lengthscale.reshape(1, 64))


def copy_of(parts, rows, token, weight):
    def body(token_ref, *refs):
        at = 0
        for ref in refs[:-1]:
            refs[-1][at : at + rows] = ref[:rows]
            at += rows

    return pl.pallas_call(
        body,
        out_shape=jax.ShapeDtypeStruct((rows * len(parts), parts[0].shape[1]), BF16),
        in_specs=[pl.BlockSpec(memory_space=pl.ANY)]
        + [pl.BlockSpec(memory_space=pltpu.VMEM)] * len(parts),
        out_specs=pl.BlockSpec(memory_space=pltpu.VMEM),
        compiler_params=PARAMS,
        cost_estimate=cost(weight, 1024),
        name="copy_of",
    )(token, *parts)


def second_pack(zl, amp, half, got, kept):
    def body(zl_ref, amp_ref, half_ref, got_ref, kept_ref, rows_ref, share_ref):
        first = zl_ref[0] == 0
        mine = half_ref[...].astype(F32)
        theirs = got_ref[...].astype(F32)
        low = jnp.concatenate([mine[:32], theirs[:32]], axis=0)
        high = jnp.concatenate([mine[32:], theirs[32:64]], axis=0)
        picked = jnp.where(first, low, high)
        share_ref[...] = jnp.concatenate([picked, kept_ref[...].astype(F32), theirs[64:]], axis=0).T.astype(BF16)
        for k, wide in enumerate((low, high)):
            wide = jnp.concatenate([wide, wide], axis=0).T
            rows_ref[0, 512 * k : 512 * k + 512] = with_norms(wide, amp_ref[1], 67, 64)

    return pl.pallas_call(
        body,
        out_shape=[jax.ShapeDtypeStruct((1, 1024, 128), BF16), jax.ShapeDtypeStruct((512, 128), BF16)],
        in_specs=[pl.BlockSpec(memory_space=pltpu.SMEM)] * 2 + [pl.BlockSpec(memory_space=pltpu.VMEM)] * 3,
        out_specs=[pl.BlockSpec(memory_space=pltpu.VMEM)] * 2,
        compiler_params=PARAMS,
        name="second_pack",
    )(zl, amp, half, got, kept)


def one_block(left, right, vectors, top):
    exponent = lax.dot_general(right, left, (((1,), (1,)), ((), ())), preferred_element_type=F32)
    block = jnp.minimum(jnp.exp(exponent).astype(BF16), top)
    return jnp.dot(vectors, block, preferred_element_type=F32)


def ready_sum(left, pairs, top):
    result = jnp.zeros((64, left.shape[0]), F32)
    for right_ref, vectors_ref in pairs:
        total = right_ref.shape[0]
        for at in range(0, total, TN):
            part = slice(at, min(at + TN, total))
            result += one_block(left, right_ref[part, :], vectors_ref[:, part], top)
    return result


def raw_sum(left, raws, right_ref, vectors_ref, top):
    total = right_ref.shape[0]
    result = jnp.zeros((64, left.shape[0]), F32)
    at = 0
    rights, turned = [], []
    for ref, start in raws:
        for sub in range(start, ref.shape[0], 512):
            wide = ref[sub : sub + 512, :].astype(F32)
            rights.append(with_norms(wide, 0.0, 64, 67))
            turned.append(wide.T[64:, :].astype(BF16))
            right_ref[at : at + 512, :] = rights[-1]
            vectors_ref[:, at : at + 512] = turned[-1]
            at += 512
            if len(rights) * 512 == TN or at == total:
                right = jnp.concatenate(rights, axis=0)
                result += one_block(left, right, jnp.concatenate(turned, axis=1), top)
                rights, turned = [], []
    return result


def add_tiles(amp, left, ready, raws, before=None, narrow=False, weight=1024):
    count = left.shape[0]
    flat = [part for pair in ready for part in pair]
    total = sum(raw.shape[0] - start for raw, start in raws)
    cols = total + sum(right.shape[0] for right, _ in ready)
    per = 1024 // TM
    old = [] if before is None else [before]
    sums = count if narrow else 1
    ends = [len(flat), len(raws), len(old), sums]

    def body(amp_ref, left_ref, *refs):
        groups = []
        for size in ends:
            groups.append(refs[:size])
            refs = refs[size:]
        flat_refs, raw_refs, before_refs, sum_refs = groups
        pairs = [(flat_refs[2 * k], flat_refs[2 * k + 1]) for k in range(len(ready))]
        step = pl.program_id(0)
        top = jnp.full((1, 1), amp_ref[0], F32).astype(BF16)

        def put(value):
            if before_refs:
                value += before_refs[0][0]
            if not narrow:
                sum_refs[0][0] = value
                return
            for k in range(count):

                @pl.when(step // per == k)
                def _():
                    sum_refs[k][...] = value.astype(BF16)

        def tiles(fresh):
            value = ready_sum(left_ref[0], pairs if fresh or not raws else pairs + [tuple(refs)], top)
            if fresh:
                starts = [(ref, start) for ref, (_, start) in zip(raw_refs, raws)]
                value += raw_sum(left_ref[0], starts, *refs, top)
            put(value)

        if not raws:
            tiles(False)
            return

        @pl.when(step == 0)
        def _():
            tiles(True)

        @pl.when(step > 0)
        def _():
            tiles(False)

    def place(k):
        return pl.BlockSpec((64, TM), lambda i: (0, jnp.clip(i - k * per, 0, per - 1)))

    def whole(array):
        return pl.BlockSpec(array.shape, lambda i: (0, 0))

    acc_spec = pl.BlockSpec((1, 64, TM), lambda i: (i // per, 0, i % per))
    if narrow:
        sum_shapes = [jax.ShapeDtypeStruct((64, 1024), BF16)] * count
        sum_specs = [place(k) for k in range(count)]
    else:
        sum_shapes = [jax.ShapeDtypeStruct((count, 64, 1024), F32)]
        sum_specs = [acc_spec]
    made = []
    if raws:
        made = [jax.ShapeDtypeStruct((total, 128), BF16), jax.ShapeDtypeStruct((64, total), BF16)]
    out = pl.pallas_call(
        body,
        grid=(count * per,),
        out_shape=sum_shapes + made,
        in_specs=[
            pl.BlockSpec(memory_space=pltpu.SMEM),
            pl.BlockSpec((1, TM, 128), lambda i: (i // per, i % per, 0)),
        ]
        + [whole(part) for part in flat]
        + [whole(raw) for raw, _ in raws]
        + [acc_spec] * len(old),
        out_specs=sum_specs + [whole(part) for part in made],
        compiler_params=PARAMS,
        cost_estimate=cost(weight * count, cols),
        name="add_tiles",
    )(amp, left, *flat, *[raw for raw, _ in raws], *old)
    return (out[:sums] if narrow else out[0]), tuple(out[sums:])


def shift(value, axis, by):
    size = SIZES[NAMES.index(axis)]
    return lax.ppermute(value, axis, [(i, (i + by) % size) for i in range(size)])


def per_device(points, vectors, lengthscale, outscale, noise):
    zl = lax.axis_index("zl").astype(jnp.int32).reshape(1)
    amp = jnp.concatenate([outscale, jnp.log(outscale)])

    given, kept = first_pack(zl, points.T, vectors.T, lengthscale)
    got = shift(given, "zl", 1)
    half = copy_of([given], 64, kept, 4096)
    mines = [shift(half, "x", by) for by in (2, 1, -1)]
    own_left, share = second_pack(zl, amp, half, got, kept)

    beside = shift(share, "c", 1)
    near = [shift(share, "y", by) for by in (2, 1, -1)]
    mined = copy_of(mines, 64, share, 16)
    mined, beside = lax.optimization_barrier((mined, beside))
    theirs = shift(mined, "zl", 1)
    own, ready0 = add_tiles(amp, own_left, [], [(share, 0), (beside, 0)], weight=4096)
    near[0], near[1], near[2], own = lax.optimization_barrier((near[0], near[1], near[2], own))
    merged = jnp.concatenate([share] + near, axis=0)
    far = shift(merged, "zh", 1)
    merged_beside = shift(merged, "c", 1)
    own, ready1 = add_tiles(amp, own_left, [], [(merged, 512)], own, weight=64)

    theirs, own = lax.optimization_barrier((theirs, own))
    left = ready_rows(amp, mines, theirs)
    acc, ready2 = add_tiles(amp, left, [ready0, ready1], [(merged_beside, 512)])
    far, acc = lax.optimization_barrier((far, acc))
    far_beside = shift(far, "c", 1)
    acc, ready3 = add_tiles(amp, left, [], [(far, 0)], acc)
    sent, ready4 = add_tiles(amp, left, [], [(far_beside, 0)], acc, narrow=True)
    arrived = [shift(part, "x", by) for part, by in zip(sent, (2, -1, 1))]
    own, _ = add_tiles(amp, own_left, [ready2, ready3, ready4], [], own)
    own = own[0]
    for part in arrived:
        own = own + part.astype(F32)
    result = own[:32] + shift(own[32:], "zl", 1)
    return result.T + noise[0] * vectors.astype(F32)


def solution(mesh):
    fine = Mesh(mesh.devices.reshape(SIZES), NAMES)
    placed = (P(BLK, "zl"), P(BLK, "zl"), P(), P(), P())
    return jax.shard_map(
        per_device, mesh=fine, in_specs=placed, out_specs=P(BLK, "zl"), check_vma=False
    )
```

```python
import jax
import jax.numpy as jnp
from jax import lax
from jax.experimental import pallas as pl
from jax.experimental.pallas import tpu as pltpu
from jax.sharding import Mesh, PartitionSpec as P

SIZES = (2, 4, 4, 2, 2)
NAMES = ("zh", "x", "y", "c", "zl")
BLK = ("zh", "x", "y", "c")
TM = 512
TN = 1024
F32 = jnp.float32
BF16 = jnp.bfloat16
ALONE = pltpu.CompilerParams(vmem_limit_bytes=60 << 20)
PARAMS = pltpu.CompilerParams(vmem_limit_bytes=48 << 20)


SCALE = 512


def cost(rows, cols):
    return pl.CostEstimate(flops=rows * cols * SCALE, transcendentals=0, bytes_accessed=cols * 384)


def three_parts(wide):
    hi = wide.astype(BF16).astype(F32)
    mid = (wide - hi).astype(BF16).astype(F32)
    return hi, mid, wide - hi - mid


def with_norms(wide, offset, first, other):
    lane = lax.broadcasted_iota(jnp.int32, wide.shape, 1)
    wide = jnp.where(lane < 64, wide, 0.0)
    half = offset - 0.5 * jnp.sum(wide * wide, axis=1, keepdims=True)
    hi, mid, low = three_parts(half)
    ones = (lane >= other) & (lane < other + 3)
    wide = jnp.where(ones, 1.0, wide)
    wide = jnp.where(lane == first, hi, wide)
    wide = jnp.where(lane == first + 1, mid, wide)
    wide = jnp.where(lane == first + 2, low, wide)
    return wide.astype(BF16)


def ready_rows(amp, mines, theirs):
    count = len(mines)

    def body(amp_ref, *refs):
        theirs_ref, out_ref = refs[count:]
        for k in range(count):
            for half in range(2):
                low = 32 * half
                mine = refs[k][low : low + 32, :].astype(F32)
                other = theirs_ref[64 * k + low : 64 * k + low + 32, :].astype(F32)
                wide = jnp.concatenate([mine, other, mine, other], axis=0).T
                out_ref[k, 512 * half : 512 * half + 512] = with_norms(wide, amp_ref[1], 67, 64)

    return pl.pallas_call(
        body,
        out_shape=jax.ShapeDtypeStruct((count, 1024, 128), BF16),
        in_specs=[pl.BlockSpec(memory_space=pltpu.SMEM)]
        + [pl.BlockSpec(memory_space=pltpu.VMEM)] * (count + 1),
        out_specs=pl.BlockSpec(memory_space=pltpu.VMEM),
        compiler_params=PARAMS,
        name="ready_rows",
    )(amp, *mines, theirs)


def first_pack(zl, points, vectors, lengthscale):
    def body(zl_ref, points_in, vectors_in, length_in, out_ref, kept_ref, points_ref, vectors_ref, length_ref, sems):
        copies = [
            pltpu.make_async_copy(length_in, length_ref, sems.at[0]),
            pltpu.make_async_copy(points_in, points_ref, sems.at[1]),
            pltpu.make_async_copy(vectors_in, vectors_ref, sems.at[2]),
        ]
        for copy in copies:
            copy.start()
        for copy in copies:
            copy.wait()
        at = zl_ref[0]
        lane = lax.broadcasted_iota(jnp.int32, (32, 64), 1)
        row = lax.broadcasted_iota(jnp.int32, (32, 64), 0)
        column = jnp.sum(jnp.where(lane == row + 32 * at, length_ref[...], 0.0), axis=1, keepdims=True)
        scaled = (points_ref[...].astype(F32) / column).astype(BF16)
        out_ref[:32] = scaled[:, :512]
        out_ref[32:64] = scaled[:, 512:]
        given = vectors_ref[...].astype(F32)
        out_ref[64:] = jnp.where(at == 0, given[:, 512:], given[:, :512]).astype(BF16)
        kept_ref[...] = jnp.where(at == 0, given[:, :512], given[:, 512:]).astype(BF16)

    return pl.pallas_call(
        body,
        out_shape=(jax.ShapeDtypeStruct((96, 512), BF16), jax.ShapeDtypeStruct((32, 512), BF16)),
        in_specs=[pl.BlockSpec(memory_space=pltpu.SMEM)] + [pl.BlockSpec(memory_space=pltpu.HBM)] * 3,
        out_specs=(pl.BlockSpec(memory_space=pltpu.VMEM),) * 2,
        scratch_shapes=[
            pltpu.VMEM((32, 1024), BF16),
            pltpu.VMEM((32, 1024), BF16),
            pltpu.VMEM((1, 64), F32),
            pltpu.SemaphoreType.DMA((3,)),
        ],
        compiler_params=ALONE,
        name="first_pack",
    )(zl, points, vectors, lengthscale.reshape(1, 64))


def features_of(given):
    def body(given_ref, out_ref, sem):
        copy = pltpu.make_async_copy(given_ref.at[:64], out_ref, sem)
        copy.start()
        copy.wait()

    return pl.pallas_call(
        body,
        out_shape=jax.ShapeDtypeStruct((64, 512), BF16),
        in_specs=[pl.BlockSpec(memory_space=pltpu.HBM)],
        out_specs=pl.BlockSpec(memory_space=pltpu.HBM),
        scratch_shapes=[pltpu.SemaphoreType.DMA],
        compiler_params=ALONE,
        cost_estimate=cost(4096, 1024),
        name="features_of",
    )(given)


def copy_of(parts, rows, token, weight):
    def body(token_ref, *refs):
        at = 0
        for ref in refs[:-1]:
            refs[-1][at : at + rows] = ref[:rows]
            at += rows

    return pl.pallas_call(
        body,
        out_shape=jax.ShapeDtypeStruct((rows * len(parts), parts[0].shape[1]), BF16),
        in_specs=[pl.BlockSpec(memory_space=pl.ANY)]
        + [pl.BlockSpec(memory_space=pltpu.VMEM)] * len(parts),
        out_specs=pl.BlockSpec(memory_space=pltpu.VMEM),
        compiler_params=PARAMS,
        cost_estimate=cost(weight, 1024),
        name="copy_of",
    )(token, *parts)


def second_pack(zl, amp, half, got, kept):
    def body(zl_ref, amp_ref, half_ref, got_ref, kept_ref, rows_ref, share_ref):
        first = zl_ref[0] == 0
        mine = half_ref[:64].astype(F32)
        theirs = got_ref[...].astype(F32)
        low = jnp.concatenate([mine[:32], theirs[:32]], axis=0)
        high = jnp.concatenate([mine[32:], theirs[32:64]], axis=0)
        picked = jnp.where(first, low, high)
        share_ref[...] = jnp.concatenate([picked, kept_ref[...].astype(F32), theirs[64:]], axis=0).T.astype(BF16)
        for k, wide in enumerate((low, high)):
            wide = jnp.concatenate([wide, wide], axis=0).T
            rows_ref[0, 512 * k : 512 * k + 512] = with_norms(wide, amp_ref[1], 67, 64)

    return pl.pallas_call(
        body,
        out_shape=[jax.ShapeDtypeStruct((1, 1024, 128), BF16), jax.ShapeDtypeStruct((512, 128), BF16)],
        in_specs=[pl.BlockSpec(memory_space=pltpu.SMEM)] * 2 + [pl.BlockSpec(memory_space=pltpu.VMEM)] * 3,
        out_specs=[pl.BlockSpec(memory_space=pltpu.VMEM)] * 2,
        compiler_params=PARAMS,
        name="second_pack",
    )(zl, amp, half, got, kept)


def one_block(left, right, vectors, top):
    exponent = lax.dot_general(right, left, (((1,), (1,)), ((), ())), preferred_element_type=F32)
    block = jnp.minimum(jnp.exp(exponent).astype(BF16), top)
    return jnp.dot(vectors, block, preferred_element_type=F32)


def ready_sum(left, pairs, top):
    result = jnp.zeros((64, left.shape[0]), F32)
    for right_ref, vectors_ref in pairs:
        total = right_ref.shape[0]
        for at in range(0, total, TN):
            part = slice(at, min(at + TN, total))
            result += one_block(left, right_ref[part, :], vectors_ref[:, part], top)
    return result


def swapped(wide):
    lane = lax.broadcasted_iota(jnp.int32, wide.shape, 1)
    return jnp.where(lane % 64 < 32, pltpu.roll(wide, 96, 1), pltpu.roll(wide, 32, 1))


def raw_sum(left, raws, right_ref, vectors_ref, top):
    total = right_ref.shape[0]
    result = jnp.zeros((64, left.shape[0]), F32)
    at = 0
    rights, turned = [], []
    for ref, start, swap in raws:
        for sub in range(start, ref.shape[0], 512):
            wide = ref[sub : sub + 512, :].astype(F32)
            if swap:
                wide = swapped(wide)
            rights.append(with_norms(wide, 0.0, 64, 67))
            turned.append(wide.T[64:, :].astype(BF16))
            right_ref[at : at + 512, :] = rights[-1]
            vectors_ref[:, at : at + 512] = turned[-1]
            at += 512
            if len(rights) * 512 == TN or at == total:
                right = jnp.concatenate(rights, axis=0)
                result += one_block(left, right, jnp.concatenate(turned, axis=1), top)
                rights, turned = [], []
    return result


def add_tiles(amp, left, ready, raws, before=None, narrow=False, weight=1024, swap=False):
    count = left.shape[0]
    flat = [part for pair in ready for part in pair]
    total = sum(raw.shape[0] - start for raw, start in raws)
    cols = total + sum(right.shape[0] for right, _ in ready)
    per = 1024 // TM
    old = [] if before is None else [before]
    sums = count if narrow else 1
    ends = [len(flat), len(raws), len(old), sums]

    def body(amp_ref, left_ref, *refs):
        groups = []
        for size in ends:
            groups.append(refs[:size])
            refs = refs[size:]
        flat_refs, raw_refs, before_refs, sum_refs = groups
        pairs = [(flat_refs[2 * k], flat_refs[2 * k + 1]) for k in range(len(ready))]
        step = pl.program_id(0)
        top = jnp.full((1, 1), amp_ref[0], F32).astype(BF16)

        def put(value):
            if before_refs:
                value += before_refs[0][0]
            if not narrow:
                sum_refs[0][0] = value
                return
            for k in range(count):

                @pl.when(step // per == k)
                def _():
                    sum_refs[k][...] = value.astype(BF16)

        def tiles(fresh):
            value = ready_sum(left_ref[0], pairs if fresh or not raws else pairs + [tuple(refs)], top)
            if fresh:
                starts = [(ref, start, swap) for ref, (_, start) in zip(raw_refs, raws)]
                value += raw_sum(left_ref[0], starts, *refs, top)
            put(value)

        if not raws:
            tiles(False)
            return

        @pl.when(step == 0)
        def _():
            tiles(True)

        @pl.when(step > 0)
        def _():
            tiles(False)

    def place(k):
        return pl.BlockSpec((64, TM), lambda i: (0, jnp.clip(i - k * per, 0, per - 1)))

    def whole(array):
        return pl.BlockSpec(array.shape, lambda i: (0, 0))

    acc_spec = pl.BlockSpec((1, 64, TM), lambda i: (i // per, 0, i % per))
    if narrow:
        sum_shapes = [jax.ShapeDtypeStruct((64, 1024), BF16)] * count
        sum_specs = [place(k) for k in range(count)]
    else:
        sum_shapes = [jax.ShapeDtypeStruct((count, 64, 1024), F32)]
        sum_specs = [acc_spec]
    made = []
    if raws:
        made = [jax.ShapeDtypeStruct((total, 128), BF16), jax.ShapeDtypeStruct((64, total), BF16)]
    out = pl.pallas_call(
        body,
        grid=(count * per,),
        out_shape=sum_shapes + made,
        in_specs=[
            pl.BlockSpec(memory_space=pltpu.SMEM),
            pl.BlockSpec((1, TM, 128), lambda i: (i // per, i % per, 0)),
        ]
        + [whole(part) for part in flat]
        + [whole(raw) for raw, _ in raws]
        + [acc_spec] * len(old),
        out_specs=sum_specs + [whole(part) for part in made],
        compiler_params=PARAMS,
        cost_estimate=cost(weight * count, cols),
        name="add_tiles",
    )(amp, left, *flat, *[raw for raw, _ in raws], *old)
    return (out[:sums] if narrow else out[0]), tuple(out[sums:])


def shift(value, axis, by):
    size = SIZES[NAMES.index(axis)]
    return lax.ppermute(value, axis, [(i, (i + by) % size) for i in range(size)])


def cross(value):
    return lax.ppermute(value, ("zh", "zl"), [(i, 3 - i) for i in range(4)])


def per_device(points, vectors, lengthscale, outscale, noise):
    zl = lax.axis_index("zl").astype(jnp.int32).reshape(1)
    amp = jnp.concatenate([outscale, jnp.log(outscale)])

    given, kept = first_pack(zl, points.T, vectors.T, lengthscale)
    got = shift(given, "zl", 1)
    half = features_of(given)
    mines = [shift(half, "x", by) for by in (1, -1, 2)]
    own_left, share = second_pack(zl, amp, given, got, kept)

    beside = shift(share, "c", 1)
    near = [shift(share, "y", by) for by in (2, 1, -1)]
    mined = copy_of(mines, 64, share, 16)
    mined, beside = lax.optimization_barrier((mined, beside))
    theirs = shift(mined, "zl", 1)
    own, ready0 = add_tiles(amp, own_left, [], [(share, 0), (beside, 0)], weight=4096)
    near[0], near[1], near[2], own = lax.optimization_barrier((near[0], near[1], near[2], own))
    merged = jnp.concatenate([share] + near, axis=0)
    far = cross(merged)
    merged_beside = shift(merged, "c", 1)
    own, ready1 = add_tiles(amp, own_left, [], [(merged, 512)], own, weight=64)

    theirs, own = lax.optimization_barrier((theirs, own))
    left = ready_rows(amp, mines, theirs)
    acc, ready2 = add_tiles(amp, left, [ready0, ready1], [(merged_beside, 512)])
    far, acc = lax.optimization_barrier((far, acc))
    far_beside = shift(far, "c", 1)
    acc, ready3 = add_tiles(amp, left, [], [(far, 0)], acc, swap=True)
    sent, ready4 = add_tiles(amp, left, [], [(far_beside, 0)], acc, narrow=True, swap=True)
    arrived = [shift(part, "x", by) for part, by in zip(sent, (-1, 1, 2))]
    own, _ = add_tiles(amp, own_left, [ready2, ready3, ready4], [], own)
    own = own[0]
    for part in arrived:
        own = own + part.astype(F32)
    result = own[:32] + shift(own[32:], "zl", 1)
    return result.T + noise[0] * vectors.astype(F32)


def solution(mesh):
    fine = Mesh(mesh.devices.reshape(SIZES), NAMES)
    placed = (P(BLK, "zl"), P(BLK, "zl"), P(), P(), P())
    return jax.shard_map(
        per_device, mesh=fine, in_specs=placed, out_specs=P(BLK, "zl"), check_vma=False
    )
```

```python
import jax
import jax.numpy as jnp
from jax import lax
from jax.experimental import pallas as pl
from jax.experimental.pallas import tpu as pltpu
from jax.sharding import Mesh, PartitionSpec as P

SIZES = (2, 4, 4, 2, 2)
NAMES = ("zh", "x", "y", "c", "zl")
BLK = ("zh", "x", "y", "c")
TM = 512
TN = 1024
F32 = jnp.float32
BF16 = jnp.bfloat16
PARAMS = pltpu.CompilerParams(vmem_limit_bytes=48 << 20)


SCALE = 512


def cost(rows, cols):
    return pl.CostEstimate(flops=rows * cols * SCALE, transcendentals=0, bytes_accessed=cols * 384)


def three_parts(wide):
    hi = wide.astype(BF16).astype(F32)
    mid = (wide - hi).astype(BF16).astype(F32)
    return hi, mid, wide - hi - mid


def put_row(ref, k, at, wide, offset):
    lane = lax.broadcasted_iota(jnp.int32, wide.shape, 1)
    wide = jnp.where(lane < 64, wide, 0.0)
    half = offset - 0.5 * jnp.sum(wide * wide, axis=1, keepdims=True)
    for place, part in enumerate(three_parts(half)):
        wide = jnp.where(lane == 64 + place, part, wide)
    ref[k, at : at + 512, :128] = wide.astype(BF16)
    ref[k, at : at + 512, 128:] = jnp.full((512, 128), -0.5, BF16)


def column(raw):
    lane = lax.broadcasted_iota(jnp.int32, raw.shape, 1)
    wide = raw.astype(F32)
    square = wide * wide
    high = square.astype(BF16)
    low = square - high.astype(F32)
    second = jnp.where(lane < 64, high.astype(F32), pltpu.roll(low, 64, 1)).astype(BF16)
    first = jnp.where(lane < 64, wide, 1.0).astype(BF16)
    return jnp.concatenate([first, second], axis=1)


def ready_rows(amp, mines, theirs):
    count = len(mines)

    def body(amp_ref, *refs):
        theirs_ref, out_ref = refs[count:]
        for k in range(count):
            for half in range(2):
                low = 32 * half
                mine = refs[k][low : low + 32, :].astype(F32)
                other = theirs_ref[64 * k + low : 64 * k + low + 32, :].astype(F32)
                wide = jnp.concatenate([mine, other, mine, other], axis=0).T
                put_row(out_ref, k, 512 * half, wide, amp_ref[1])

    return pl.pallas_call(
        body,
        out_shape=jax.ShapeDtypeStruct((count, 1024, 256), BF16),
        in_specs=[pl.BlockSpec(memory_space=pltpu.SMEM)]
        + [pl.BlockSpec(memory_space=pltpu.VMEM)] * (count + 1),
        out_specs=pl.BlockSpec(memory_space=pltpu.VMEM),
        compiler_params=PARAMS,
        name="ready_rows",
    )(amp, *mines, theirs)


def kept_in_hbm(array):
    return pltpu.with_memory_space_constraint(array, pltpu.HBM)


def first_pack(zl, points, vectors, lengthscale):
    def body(zl_ref, points_in, vectors_in, length_in, out_ref, kept_ref, points_ref, vectors_ref, length_ref, sems):
        copies = [
            pltpu.make_async_copy(length_in, length_ref, sems.at[0]),
            pltpu.make_async_copy(points_in, points_ref, sems.at[1]),
            pltpu.make_async_copy(vectors_in, vectors_ref, sems.at[2]),
        ]
        for copy in copies:
            copy.start()
        for copy in copies:
            copy.wait()
        at = zl_ref[0]
        lane = lax.broadcasted_iota(jnp.int32, (32, 64), 1)
        row = lax.broadcasted_iota(jnp.int32, (32, 64), 0)
        column = jnp.sum(jnp.where(lane == row + 32 * at, length_ref[...], 0.0), axis=1, keepdims=True)
        scaled = (points_ref[...].astype(F32) / column).astype(BF16)
        out_ref[:32] = scaled[:, :512]
        out_ref[32:64] = scaled[:, 512:]
        given = vectors_ref[...].astype(F32)
        out_ref[64:] = jnp.where(at == 0, given[:, 512:], given[:, :512]).astype(BF16)
        kept_ref[...] = jnp.where(at == 0, given[:, :512], given[:, 512:]).astype(BF16)

    return pl.pallas_call(
        body,
        out_shape=(jax.ShapeDtypeStruct((96, 512), BF16), jax.ShapeDtypeStruct((32, 512), BF16)),
        in_specs=[pl.BlockSpec(memory_space=pltpu.SMEM)] + [pl.BlockSpec(memory_space=pltpu.HBM)] * 3,
        out_specs=(pl.BlockSpec(memory_space=pltpu.VMEM),) * 2,
        scratch_shapes=[
            pltpu.VMEM((32, 1024), BF16),
            pltpu.VMEM((32, 1024), BF16),
            pltpu.VMEM((1, 64), F32),
            pltpu.SemaphoreType.DMA((3,)),
        ],
        compiler_params=PARAMS,
        name="first_pack",
    )(zl, *(kept_in_hbm(a) for a in (points, vectors, lengthscale.reshape(1, 64))))


def copy_of(parts, rows, token, weight):
    def body(token_ref, *refs):
        at = 0
        for ref in refs[:-1]:
            refs[-1][at : at + rows] = ref[:rows]
            at += rows

    return pl.pallas_call(
        body,
        out_shape=jax.ShapeDtypeStruct((rows * len(parts), parts[0].shape[1]), BF16),
        in_specs=[pl.BlockSpec(memory_space=pl.ANY)]
        + [pl.BlockSpec(memory_space=pltpu.VMEM)] * len(parts),
        out_specs=pl.BlockSpec(memory_space=pltpu.VMEM),
        compiler_params=PARAMS,
        cost_estimate=cost(weight, 1024),
        name="copy_of",
    )(token, *parts)


def second_pack(zl, amp, half, got, kept):
    def body(zl_ref, amp_ref, half_ref, got_ref, kept_ref, rows_ref, share_ref):
        first = zl_ref[0] == 0
        mine = half_ref[...].astype(F32)
        theirs = got_ref[...].astype(F32)
        low = jnp.concatenate([mine[:32], theirs[:32]], axis=0)
        high = jnp.concatenate([mine[32:], theirs[32:64]], axis=0)
        picked = jnp.where(first, low, high)
        share_ref[...] = jnp.concatenate([picked, kept_ref[...].astype(F32), theirs[64:]], axis=0).T.astype(BF16)
        for k, wide in enumerate((low, high)):
            wide = jnp.concatenate([wide, wide], axis=0).T
            put_row(rows_ref, 0, 512 * k, wide, amp_ref[1])

    return pl.pallas_call(
        body,
        out_shape=[jax.ShapeDtypeStruct((1, 1024, 256), BF16), jax.ShapeDtypeStruct((512, 128), BF16)],
        in_specs=[pl.BlockSpec(memory_space=pltpu.SMEM)] * 2 + [pl.BlockSpec(memory_space=pltpu.VMEM)] * 3,
        out_specs=[pl.BlockSpec(memory_space=pltpu.VMEM)] * 2,
        compiler_params=PARAMS,
        name="second_pack",
    )(zl, amp, half, got, kept)


def one_block(left, right, vectors, top):
    exponent = lax.dot_general(right, left, (((1,), (1,)), ((), ())), preferred_element_type=F32)
    block = jnp.minimum(jnp.exp(exponent).astype(BF16), top)
    return jnp.dot(vectors, block, preferred_element_type=F32)


def ready_sum(left, pairs, top):
    result = jnp.zeros((64, left.shape[0]), F32)
    for right_ref, vectors_ref in pairs:
        total = right_ref.shape[0]
        for at in range(0, total, TN):
            part = slice(at, min(at + TN, total))
            result += one_block(left, right_ref[part, :], vectors_ref[:, part], top)
    return result


def raw_sum(left, raws, right_ref, vectors_ref, top):
    total = right_ref.shape[0]
    result = jnp.zeros((64, left.shape[0]), F32)
    at = 0
    rights, turned = [], []
    for ref, start in raws:
        for sub in range(start, ref.shape[0], 512):
            raw = ref[sub : sub + 512, :]
            rights.append(column(raw))
            turned.append(raw.astype(F32).T[64:, :].astype(BF16))
            right_ref[at : at + 512, :] = rights[-1]
            vectors_ref[:, at : at + 512] = turned[-1]
            at += 512
            if len(rights) * 512 == TN or at == total:
                right = jnp.concatenate(rights, axis=0)
                result += one_block(left, right, jnp.concatenate(turned, axis=1), top)
                rights, turned = [], []
    return result


def add_tiles(amp, left, ready, raws, before=None, narrow=False, weight=1024):
    count = left.shape[0]
    flat = [part for pair in ready for part in pair]
    total = sum(raw.shape[0] - start for raw, start in raws)
    cols = total + sum(right.shape[0] for right, _ in ready)
    per = 1024 // TM
    old = [] if before is None else [before]
    sums = count if narrow else 1
    ends = [len(flat), len(raws), len(old), sums]

    def body(amp_ref, left_ref, *refs):
        groups = []
        for size in ends:
            groups.append(refs[:size])
            refs = refs[size:]
        flat_refs, raw_refs, before_refs, sum_refs = groups
        pairs = [(flat_refs[2 * k], flat_refs[2 * k + 1]) for k in range(len(ready))]
        step = pl.program_id(0)
        top = jnp.full((1, 1), amp_ref[0], F32).astype(BF16)

        def put(value):
            if before_refs:
                value += before_refs[0][0]
            if not narrow:
                sum_refs[0][0] = value
                return
            for k in range(count):

                @pl.when(step // per == k)
                def _():
                    sum_refs[k][...] = value.astype(BF16)

        def tiles(fresh):
            value = ready_sum(left_ref[0], pairs if fresh or not raws else pairs + [tuple(refs)], top)
            if fresh:
                starts = [(ref, start) for ref, (_, start) in zip(raw_refs, raws)]
                value += raw_sum(left_ref[0], starts, *refs, top)
            put(value)

        if not raws:
            tiles(False)
            return

        @pl.when(step == 0)
        def _():
            tiles(True)

        @pl.when(step > 0)
        def _():
            tiles(False)

    def place(k):
        return pl.BlockSpec((64, TM), lambda i: (0, jnp.clip(i - k * per, 0, per - 1)))

    def whole(array):
        return pl.BlockSpec(array.shape, lambda i: (0, 0))

    acc_spec = pl.BlockSpec((1, 64, TM), lambda i: (i // per, 0, i % per))
    if narrow:
        sum_shapes = [jax.ShapeDtypeStruct((64, 1024), BF16)] * count
        sum_specs = [place(k) for k in range(count)]
    else:
        sum_shapes = [jax.ShapeDtypeStruct((count, 64, 1024), F32)]
        sum_specs = [acc_spec]
    made = []
    if raws:
        made = [jax.ShapeDtypeStruct((total, 256), BF16), jax.ShapeDtypeStruct((64, total), BF16)]
    out = pl.pallas_call(
        body,
        grid=(count * per,),
        out_shape=sum_shapes + made,
        in_specs=[
            pl.BlockSpec(memory_space=pltpu.SMEM),
            pl.BlockSpec((1, TM, 256), lambda i: (i // per, i % per, 0)),
        ]
        + [whole(part) for part in flat]
        + [whole(raw) for raw, _ in raws]
        + [acc_spec] * len(old),
        out_specs=sum_specs + [whole(part) for part in made],
        compiler_params=PARAMS,
        cost_estimate=cost(weight * count, cols),
        name="add_tiles",
    )(amp, left, *flat, *[raw for raw, _ in raws], *old)
    return (out[:sums] if narrow else out[0]), tuple(out[sums:])


def shift(value, axis, by):
    size = SIZES[NAMES.index(axis)]
    return lax.ppermute(value, axis, [(i, (i + by) % size) for i in range(size)])


def per_device(points, vectors, lengthscale, outscale, noise):
    zl = lax.axis_index("zl").astype(jnp.int32).reshape(1)
    amp = jnp.concatenate([outscale, jnp.log(outscale)])

    given, kept = first_pack(zl, points.T, vectors.T, lengthscale)
    got = shift(given, "zl", 1)
    half = copy_of([given], 64, kept, 4096)
    mines = [shift(half, "x", by) for by in (2, 1, -1)]
    own_left, share = second_pack(zl, amp, half, got, kept)

    beside = shift(share, "c", 1)
    near = [shift(share, "y", by) for by in (2, 1, -1)]
    mined = copy_of(mines, 64, share, 16)
    mined, beside = lax.optimization_barrier((mined, beside))
    theirs = shift(mined, "zl", 1)
    own, ready0 = add_tiles(amp, own_left, [], [(share, 0), (beside, 0)], weight=4096)
    near[0], near[1], near[2], own = lax.optimization_barrier((near[0], near[1], near[2], own))
    merged = jnp.concatenate([share] + near, axis=0)
    far = shift(merged, "zh", 1)
    merged_beside = shift(merged, "c", 1)
    own, ready1 = add_tiles(amp, own_left, [], [(merged, 512)], own, weight=64)

    theirs, own = lax.optimization_barrier((theirs, own))
    left = ready_rows(amp, mines, theirs)
    acc, ready2 = add_tiles(amp, left, [ready0, ready1], [(merged_beside, 512)])
    far, acc = lax.optimization_barrier((far, acc))
    far_beside = shift(far, "c", 1)
    acc, ready3 = add_tiles(amp, left, [], [(far, 0)], acc)
    sent, ready4 = add_tiles(amp, left, [], [(far_beside, 0)], acc, narrow=True)
    arrived = [shift(part, "x", by) for part, by in zip(sent, (2, -1, 1))]
    own, _ = add_tiles(amp, own_left, [ready2, ready3, ready4], [], own)
    own = own[0]
    for part in arrived:
        own = own + part.astype(F32)
    result = own[:32] + shift(own[32:], "zl", 1)
    return result.T + noise[0] * vectors.astype(F32)


def solution(mesh):
    fine = Mesh(mesh.devices.reshape(SIZES), NAMES)
    placed = (P(BLK, "zl"), P(BLK, "zl"), P(), P(), P())
    return jax.shard_map(
        per_device, mesh=fine, in_specs=placed, out_specs=P(BLK, "zl"), check_vma=False
    )
```

```python
import jax
import jax.numpy as jnp
from jax import lax
from jax.experimental import pallas as pl
from jax.experimental.pallas import tpu as pltpu
from jax.sharding import Mesh, PartitionSpec as P

SIZES = (2, 4, 4, 2, 2)
NAMES = ("zh", "x", "y", "c", "zl")
BLK = ("zh", "x", "y", "c")
TM = 512
TN = 1024
F32 = jnp.float32
BF16 = jnp.bfloat16
PARAMS = pltpu.CompilerParams(vmem_limit_bytes=48 << 20)


SCALE = 512


def cost(rows, cols):
    return pl.CostEstimate(flops=rows * cols * SCALE, transcendentals=0, bytes_accessed=cols * 384)


def three_parts(wide):
    hi = wide.astype(BF16).astype(F32)
    mid = (wide - hi).astype(BF16).astype(F32)
    return hi, mid, wide - hi - mid


def with_parts(features, offset, first):
    half = offset - 0.5 * jnp.sum(features * features, axis=0, keepdims=True)
    shape = (8, features.shape[1])
    row = lax.broadcasted_iota(jnp.int32, shape, 0)
    tail = jnp.where(row < 6, 1.0, 0.0)
    for place, part in enumerate(three_parts(half)):
        tail = jnp.where(row == first + place, part, tail)
    return jnp.concatenate([features, tail, jnp.zeros((56, features.shape[1]), F32)], axis=0)


def ready_rows(amp, mines, theirs):
    count = len(mines)

    def body(amp_ref, *refs):
        theirs_ref, out_ref = refs[count:]
        for k in range(count):
            for half in range(2):
                low = 32 * half
                mine = refs[k][low : low + 32, :].astype(F32)
                other = theirs_ref[64 * k + low : 64 * k + low + 32, :].astype(F32)
                features = jnp.concatenate([mine, other], axis=0)
                out_ref[k, :, 512 * half : 512 * half + 512] = with_parts(features, amp_ref[1], 3).astype(BF16)

    return pl.pallas_call(
        body,
        out_shape=jax.ShapeDtypeStruct((count, 128, 1024), BF16),
        in_specs=[pl.BlockSpec(memory_space=pltpu.SMEM)]
        + [pl.BlockSpec(memory_space=pltpu.VMEM)] * (count + 1),
        out_specs=pl.BlockSpec(memory_space=pltpu.VMEM),
        compiler_params=PARAMS,
        name="ready_rows",
    )(amp, *mines, theirs)


def kept_in_hbm(array):
    return pltpu.with_memory_space_constraint(array, pltpu.HBM)


def first_pack(zl, points, vectors, lengthscale):
    def body(zl_ref, points_in, vectors_in, length_in, out_ref, kept_ref, points_ref, vectors_ref, length_ref, sems):
        copies = [
            pltpu.make_async_copy(length_in, length_ref, sems.at[0]),
            pltpu.make_async_copy(points_in, points_ref, sems.at[1]),
            pltpu.make_async_copy(vectors_in, vectors_ref, sems.at[2]),
        ]
        for copy in copies:
            copy.start()
        for copy in copies:
            copy.wait()
        at = zl_ref[0]
        lane = lax.broadcasted_iota(jnp.int32, (32, 64), 1)
        row = lax.broadcasted_iota(jnp.int32, (32, 64), 0)
        column = jnp.sum(jnp.where(lane == row + 32 * at, length_ref[...], 0.0), axis=1, keepdims=True)
        scaled = (points_ref[...].astype(F32) / column).astype(BF16)
        out_ref[:32] = scaled[:, :512]
        out_ref[32:64] = scaled[:, 512:]
        given = vectors_ref[...].astype(F32)
        out_ref[64:] = jnp.where(at == 0, given[:, 512:], given[:, :512]).astype(BF16)
        kept_ref[...] = jnp.where(at == 0, given[:, :512], given[:, 512:]).astype(BF16)

    return pl.pallas_call(
        body,
        out_shape=(jax.ShapeDtypeStruct((96, 512), BF16), jax.ShapeDtypeStruct((32, 512), BF16)),
        in_specs=[pl.BlockSpec(memory_space=pltpu.SMEM)] + [pl.BlockSpec(memory_space=pltpu.HBM)] * 3,
        out_specs=(pl.BlockSpec(memory_space=pltpu.VMEM),) * 2,
        scratch_shapes=[
            pltpu.VMEM((32, 1024), BF16),
            pltpu.VMEM((32, 1024), BF16),
            pltpu.VMEM((1, 64), F32),
            pltpu.SemaphoreType.DMA((3,)),
        ],
        compiler_params=PARAMS,
        name="first_pack",
    )(zl, *(kept_in_hbm(a) for a in (points, vectors, lengthscale.reshape(1, 64))))


def copy_of(parts, rows, token, weight):
    def body(token_ref, *refs):
        at = 0
        for ref in refs[:-1]:
            refs[-1][at : at + rows] = ref[:rows]
            at += rows

    return pl.pallas_call(
        body,
        out_shape=jax.ShapeDtypeStruct((rows * len(parts), parts[0].shape[1]), BF16),
        in_specs=[pl.BlockSpec(memory_space=pl.ANY)]
        + [pl.BlockSpec(memory_space=pltpu.VMEM)] * len(parts),
        out_specs=pl.BlockSpec(memory_space=pltpu.VMEM),
        compiler_params=PARAMS,
        cost_estimate=cost(weight, 1024),
        name="copy_of",
    )(token, *parts)


def second_pack(zl, amp, half, got, kept):
    def body(zl_ref, amp_ref, half_ref, got_ref, kept_ref, rows_ref, share_ref):
        first = zl_ref[0] == 0
        mine = half_ref[...].astype(F32)
        theirs = got_ref[...].astype(F32)
        low = jnp.concatenate([mine[:32], theirs[:32]], axis=0)
        high = jnp.concatenate([mine[32:], theirs[32:64]], axis=0)
        picked = jnp.where(first, low, high)
        share_ref[...] = jnp.concatenate([picked, kept_ref[...].astype(F32), theirs[64:]], axis=0).astype(BF16)
        for k, features in enumerate((low, high)):
            rows_ref[0, :, 512 * k : 512 * k + 512] = with_parts(features, amp_ref[1], 3).astype(BF16)

    return pl.pallas_call(
        body,
        out_shape=[jax.ShapeDtypeStruct((1, 128, 1024), BF16), jax.ShapeDtypeStruct((128, 512), BF16)],
        in_specs=[pl.BlockSpec(memory_space=pltpu.SMEM)] * 2 + [pl.BlockSpec(memory_space=pltpu.VMEM)] * 3,
        out_specs=[pl.BlockSpec(memory_space=pltpu.VMEM)] * 2,
        compiler_params=PARAMS,
        name="second_pack",
    )(zl, amp, half, got, kept)


def one_block(left, right, vectors, top):
    exponent = jnp.dot(right, left, preferred_element_type=F32)
    block = jnp.minimum(jnp.exp(exponent).astype(BF16), top)
    return jnp.dot(vectors, block, preferred_element_type=F32)


def ready_sum(left, pairs, top):
    result = jnp.zeros((64, left.shape[1]), F32)
    for right_ref, vectors_ref in pairs:
        total = right_ref.shape[0]
        for at in range(0, total, TN):
            part = slice(at, min(at + TN, total))
            result += one_block(left, right_ref[part, :], vectors_ref[:, part], top)
    return result


def raw_sum(left, raws, right_ref, vectors_ref, top):
    total = right_ref.shape[0]
    result = jnp.zeros((64, left.shape[1]), F32)
    at = 0
    rights, turned = [], []
    for ref, start in raws:
        for sub in range(128 * start, ref.shape[0], 128):
            features = ref[sub : sub + 64, :].astype(F32)
            rights.append(with_parts(features, 0.0, 0).T.astype(BF16))
            turned.append(ref[sub + 64 : sub + 128, :])
            right_ref[at : at + 512, :] = rights[-1]
            vectors_ref[:, at : at + 512] = turned[-1]
            at += 512
            if len(rights) * 512 == TN or at == total:
                right = jnp.concatenate(rights, axis=0)
                result += one_block(left, right, jnp.concatenate(turned, axis=1), top)
                rights, turned = [], []
    return result


def add_tiles(amp, left, ready, raws, before=None, narrow=False, weight=1024):
    count = left.shape[0]
    flat = [part for pair in ready for part in pair]
    total = sum(4 * raw.shape[0] - 512 * start for raw, start in raws)
    cols = total + sum(right.shape[0] for right, _ in ready)
    per = 1024 // TM
    old = [] if before is None else [before]
    sums = count if narrow else 1
    ends = [len(flat), len(raws), len(old), sums]

    def body(amp_ref, left_ref, *refs):
        groups = []
        for size in ends:
            groups.append(refs[:size])
            refs = refs[size:]
        flat_refs, raw_refs, before_refs, sum_refs = groups
        pairs = [(flat_refs[2 * k], flat_refs[2 * k + 1]) for k in range(len(ready))]
        step = pl.program_id(0)
        top = jnp.full((1, 1), amp_ref[0], F32).astype(BF16)

        def put(value):
            if before_refs:
                value += before_refs[0][0]
            if not narrow:
                sum_refs[0][0] = value
                return
            for k in range(count):

                @pl.when(step // per == k)
                def _():
                    sum_refs[k][...] = value.astype(BF16)

        def tiles(fresh):
            value = ready_sum(left_ref[0], pairs if fresh or not raws else pairs + [tuple(refs)], top)
            if fresh:
                starts = [(ref, start) for ref, (_, start) in zip(raw_refs, raws)]
                value += raw_sum(left_ref[0], starts, *refs, top)
            put(value)

        if not raws:
            tiles(False)
            return

        @pl.when(step == 0)
        def _():
            tiles(True)

        @pl.when(step > 0)
        def _():
            tiles(False)

    def place(k):
        return pl.BlockSpec((64, TM), lambda i: (0, jnp.clip(i - k * per, 0, per - 1)))

    def whole(array):
        return pl.BlockSpec(array.shape, lambda i: (0, 0))

    acc_spec = pl.BlockSpec((1, 64, TM), lambda i: (i // per, 0, i % per))
    if narrow:
        sum_shapes = [jax.ShapeDtypeStruct((64, 1024), BF16)] * count
        sum_specs = [place(k) for k in range(count)]
    else:
        sum_shapes = [jax.ShapeDtypeStruct((count, 64, 1024), F32)]
        sum_specs = [acc_spec]
    made = []
    if raws:
        made = [jax.ShapeDtypeStruct((total, 128), BF16), jax.ShapeDtypeStruct((64, total), BF16)]
    out = pl.pallas_call(
        body,
        grid=(count * per,),
        out_shape=sum_shapes + made,
        in_specs=[
            pl.BlockSpec(memory_space=pltpu.SMEM),
            pl.BlockSpec((1, 128, TM), lambda i: (i // per, 0, i % per)),
        ]
        + [whole(part) for part in flat]
        + [whole(raw) for raw, _ in raws]
        + [acc_spec] * len(old),
        out_specs=sum_specs + [whole(part) for part in made],
        compiler_params=PARAMS,
        cost_estimate=cost(weight * count, cols),
        name="add_tiles",
    )(amp, left, *flat, *[raw for raw, _ in raws], *old)
    return (out[:sums] if narrow else out[0]), tuple(out[sums:])


def shift(value, axis, by):
    size = SIZES[NAMES.index(axis)]
    return lax.ppermute(value, axis, [(i, (i + by) % size) for i in range(size)])


def per_device(points, vectors, lengthscale, outscale, noise):
    zl = lax.axis_index("zl").astype(jnp.int32).reshape(1)
    amp = jnp.concatenate([outscale, jnp.log(outscale)])

    given, kept = first_pack(zl, points.T, vectors.T, lengthscale)
    got = shift(given, "zl", 1)
    half = copy_of([given], 64, kept, 4096)
    mines = [shift(half, "x", by) for by in (2, 1, -1)]
    own_left, share = second_pack(zl, amp, half, got, kept)

    beside = shift(share, "c", 1)
    near = [shift(share, "y", by) for by in (2, 1, -1)]
    mined = copy_of(mines, 64, share, 16)
    mined, beside = lax.optimization_barrier((mined, beside))
    theirs = shift(mined, "zl", 1)
    own, ready0 = add_tiles(amp, own_left, [], [(share, 0), (beside, 0)], weight=4096)
    near[0], near[1], near[2], own = lax.optimization_barrier((near[0], near[1], near[2], own))
    merged = jnp.concatenate([share] + near, axis=0)
    far = shift(merged, "zh", 1)
    merged_beside = shift(merged, "c", 1)
    own, ready1 = add_tiles(amp, own_left, [], [(merged, 1)], own, weight=64)

    theirs, own = lax.optimization_barrier((theirs, own))
    left = ready_rows(amp, mines, theirs)
    acc, ready2 = add_tiles(amp, left, [ready0, ready1], [(merged_beside, 1)])
    far, acc = lax.optimization_barrier((far, acc))
    far_beside = shift(far, "c", 1)
    acc, ready3 = add_tiles(amp, left, [], [(far, 0)], acc)
    sent, ready4 = add_tiles(amp, left, [], [(far_beside, 0)], acc, narrow=True)
    arrived = [shift(part, "x", by) for part, by in zip(sent, (2, -1, 1))]
    own, _ = add_tiles(amp, own_left, [ready2, ready3, ready4], [], own)
    mine, theirs = own[0, :32], own[0, 32:]
    for part in arrived:
        theirs = theirs + part[32:].astype(F32)
    for part in arrived:
        mine = mine + part[:32].astype(F32)
    result = mine + shift(theirs, "zl", 1)
    return result.T + noise[0] * vectors.astype(F32)


def solution(mesh):
    fine = Mesh(mesh.devices.reshape(SIZES), NAMES)
    placed = (P(BLK, "zl"), P(BLK, "zl"), P(), P(), P())
    return jax.shard_map(
        per_device, mesh=fine, in_specs=placed, out_specs=P(BLK, "zl"), check_vma=False
    )
```

```python
import jax
import jax.numpy as jnp
from jax import lax
from jax.experimental import pallas as pl
from jax.experimental.pallas import tpu as pltpu
from jax.sharding import Mesh, PartitionSpec as P

SIZES = (2, 4, 4, 2, 2)
NAMES = ("zh", "x", "y", "c", "zl")
BLK = ("zh", "x", "y", "c")
TM = 512
TN = 1024
F32 = jnp.float32
BF16 = jnp.bfloat16
PARAMS = pltpu.CompilerParams(vmem_limit_bytes=48 << 20)


SCALE = 512


def cost(rows, cols):
    return pl.CostEstimate(flops=rows * cols * SCALE, transcendentals=0, bytes_accessed=cols * 384)


def three_parts(wide):
    hi = wide.astype(BF16).astype(F32)
    mid = (wide - hi).astype(BF16).astype(F32)
    return hi, mid, wide - hi - mid


def with_parts(features, offset, first):
    half = offset - 0.5 * jnp.sum(features * features, axis=0, keepdims=True)
    shape = (8, features.shape[1])
    row = lax.broadcasted_iota(jnp.int32, shape, 0)
    tail = jnp.where(row < 6, 1.0, 0.0)
    for place, part in enumerate(three_parts(half)):
        tail = jnp.where(row == first + place, part, tail)
    return jnp.concatenate([features, tail, jnp.zeros((56, features.shape[1]), F32)], axis=0)


def ready_rows(amp, mines, theirs):
    count = len(mines)

    def body(amp_ref, *refs):
        theirs_ref, out_ref = refs[count:]
        for k in range(count):
            for half in range(2):
                low = 32 * half
                mine = refs[k][low : low + 32, :].astype(F32)
                other = theirs_ref[64 * k + low : 64 * k + low + 32, :].astype(F32)
                features = jnp.concatenate([mine, other], axis=0)
                out_ref[k, :, 512 * half : 512 * half + 512] = with_parts(features, amp_ref[1], 3).astype(BF16)

    return pl.pallas_call(
        body,
        out_shape=jax.ShapeDtypeStruct((count, 128, 1024), BF16),
        in_specs=[pl.BlockSpec(memory_space=pltpu.SMEM)]
        + [pl.BlockSpec(memory_space=pltpu.VMEM)] * (count + 1),
        out_specs=pl.BlockSpec(memory_space=pltpu.VMEM),
        compiler_params=PARAMS,
        name="ready_rows",
    )(amp, *mines, theirs)


def kept_in_hbm(array):
    return pltpu.with_memory_space_constraint(array, pltpu.HBM)


def first_pack(zl, points, vectors, lengthscale):
    def body(zl_ref, points_in, vectors_in, length_in, out_ref, kept_ref, points_ref, vectors_ref, length_ref, sems):
        copies = [
            pltpu.make_async_copy(length_in, length_ref, sems.at[0]),
            pltpu.make_async_copy(points_in, points_ref, sems.at[1]),
            pltpu.make_async_copy(vectors_in, vectors_ref, sems.at[2]),
        ]
        for copy in copies:
            copy.start()
        for copy in copies:
            copy.wait()
        at = zl_ref[0]
        lane = lax.broadcasted_iota(jnp.int32, (32, 64), 1)
        row = lax.broadcasted_iota(jnp.int32, (32, 64), 0)
        column = jnp.sum(jnp.where(lane == row + 32 * at, length_ref[...], 0.0), axis=1, keepdims=True)
        scaled = (points_ref[...].astype(F32) / column).astype(BF16)
        out_ref[:32] = scaled[:, :512]
        out_ref[32:64] = scaled[:, 512:]
        given = vectors_ref[...].astype(F32)
        out_ref[64:] = jnp.where(at == 0, given[:, 512:], given[:, :512]).astype(BF16)
        kept_ref[...] = jnp.where(at == 0, given[:, :512], given[:, 512:]).astype(BF16)

    return pl.pallas_call(
        body,
        out_shape=(jax.ShapeDtypeStruct((96, 512), BF16), jax.ShapeDtypeStruct((32, 512), BF16)),
        in_specs=[pl.BlockSpec(memory_space=pltpu.SMEM)] + [pl.BlockSpec(memory_space=pltpu.HBM)] * 3,
        out_specs=(pl.BlockSpec(memory_space=pltpu.VMEM),) * 2,
        scratch_shapes=[
            pltpu.VMEM((32, 1024), BF16),
            pltpu.VMEM((32, 1024), BF16),
            pltpu.VMEM((1, 64), F32),
            pltpu.SemaphoreType.DMA((3,)),
        ],
        compiler_params=PARAMS,
        name="first_pack",
    )(zl, *(kept_in_hbm(a) for a in (points, vectors, lengthscale.reshape(1, 64))))


def copy_of(parts, rows, token, weight):
    def body(token_ref, *refs):
        at = 0
        for ref in refs[:-1]:
            refs[-1][at : at + rows] = ref[:rows]
            at += rows

    return pl.pallas_call(
        body,
        out_shape=jax.ShapeDtypeStruct((rows * len(parts), parts[0].shape[1]), BF16),
        in_specs=[pl.BlockSpec(memory_space=pl.ANY)]
        + [pl.BlockSpec(memory_space=pltpu.VMEM)] * len(parts),
        out_specs=pl.BlockSpec(memory_space=pltpu.VMEM),
        compiler_params=PARAMS,
        cost_estimate=cost(weight, 1024),
        name="copy_of",
    )(token, *parts)


def second_pack(zl, amp, half, got, kept):
    def body(zl_ref, amp_ref, half_ref, got_ref, kept_ref, rows_ref, share_ref):
        first = zl_ref[0] == 0
        mine = half_ref[...].astype(F32)
        theirs = got_ref[...].astype(F32)
        low = jnp.concatenate([mine[:32], theirs[:32]], axis=0)
        high = jnp.concatenate([mine[32:], theirs[32:64]], axis=0)
        picked = jnp.where(first, low, high)
        share_ref[...] = jnp.concatenate([picked, kept_ref[...].astype(F32), theirs[64:]], axis=0).astype(BF16)
        for k, features in enumerate((low, high)):
            rows_ref[0, :, 512 * k : 512 * k + 512] = with_parts(features, amp_ref[1], 3).astype(BF16)

    return pl.pallas_call(
        body,
        out_shape=[jax.ShapeDtypeStruct((1, 128, 1024), BF16), jax.ShapeDtypeStruct((128, 512), BF16)],
        in_specs=[pl.BlockSpec(memory_space=pltpu.SMEM)] * 2 + [pl.BlockSpec(memory_space=pltpu.VMEM)] * 3,
        out_specs=[pl.BlockSpec(memory_space=pltpu.VMEM)] * 2,
        compiler_params=PARAMS,
        name="second_pack",
    )(zl, amp, half, got, kept)


def one_block(left, right, vectors, top):
    exponent = jnp.dot(right, left, preferred_element_type=F32)
    block = jnp.minimum(jnp.exp(exponent).astype(BF16), top)
    return jnp.dot(vectors, block, preferred_element_type=F32)


def ready_sum(lefts, pairs, top):
    sums = [jnp.zeros((64, TM), F32) for _ in lefts]
    for right_ref, vectors_ref in pairs:
        total = right_ref.shape[0]
        for at in range(0, total, TN):
            part = slice(at, min(at + TN, total))
            for k, left in enumerate(lefts):
                sums[k] += one_block(left, right_ref[part, :], vectors_ref[:, part], top)
    return sums


def raw_sum(lefts, raws, right_ref, vectors_ref, top):
    total = right_ref.shape[0]
    sums = [jnp.zeros((64, TM), F32) for _ in lefts]
    at = 0
    rights, turned = [], []
    for ref, start in raws:
        for sub in range(128 * start, ref.shape[0], 128):
            features = ref[sub : sub + 64, :].astype(F32)
            rights.append(with_parts(features, 0.0, 0).T.astype(BF16))
            turned.append(ref[sub + 64 : sub + 128, :])
            right_ref[at : at + 512, :] = rights[-1]
            vectors_ref[:, at : at + 512] = turned[-1]
            at += 512
            if len(rights) * 512 == TN or at == total:
                right = jnp.concatenate(rights, axis=0)
                vectors = jnp.concatenate(turned, axis=1)
                for k, left in enumerate(lefts):
                    sums[k] += one_block(left, right, vectors, top)
                rights, turned = [], []
    return sums


def add_tiles(amp, left, ready, raws, before=None, narrow=False, weight=1024):
    count = left.shape[0]
    flat = [part for pair in ready for part in pair]
    total = sum(4 * raw.shape[0] - 512 * start for raw, start in raws)
    cols = total + sum(right.shape[0] for right, _ in ready)
    old = [] if before is None else [before]
    sums = count if narrow else 1
    ends = [len(flat), len(raws), len(old), sums]

    def body(amp_ref, left_ref, *refs):
        groups = []
        for size in ends:
            groups.append(refs[:size])
            refs = refs[size:]
        flat_refs, raw_refs, before_refs, sum_refs = groups
        pairs = [(flat_refs[2 * k], flat_refs[2 * k + 1]) for k in range(len(ready))]
        step = pl.program_id(0)
        top = jnp.full((1, 1), amp_ref[0], F32).astype(BF16)

        def put(value):
            if before_refs:
                value += before_refs[0][0]
            if not narrow:
                sum_refs[0][0] = value
                return
            for k in range(count):

                @pl.when(step == k)
                def _():
                    sum_refs[k][...] = value.astype(BF16)

        def tiles(fresh):
            lefts = [left_ref[0, :, at : at + TM] for at in range(0, 1024, TM)]
            sums = ready_sum(lefts, pairs if fresh or not raws else pairs + [tuple(refs)], top)
            if fresh:
                starts = [(ref, start) for ref, (_, start) in zip(raw_refs, raws)]
                sums = [a + b for a, b in zip(sums, raw_sum(lefts, starts, *refs, top))]
            put(jnp.concatenate(sums, axis=1))

        if not raws:
            tiles(False)
            return

        @pl.when(step == 0)
        def _():
            tiles(True)

        @pl.when(step > 0)
        def _():
            tiles(False)


    def whole(array):
        return pl.BlockSpec(array.shape, lambda i: (0, 0))

    acc_spec = pl.BlockSpec((1, 64, 1024), lambda i: (i, 0, 0))
    if narrow:
        sum_shapes = [jax.ShapeDtypeStruct((64, 1024), BF16)] * count
        sum_specs = [whole(part) for part in sum_shapes]
    else:
        sum_shapes = [jax.ShapeDtypeStruct((count, 64, 1024), F32)]
        sum_specs = [acc_spec]
    made = []
    if raws:
        made = [jax.ShapeDtypeStruct((total, 128), BF16), jax.ShapeDtypeStruct((64, total), BF16)]
    out = pl.pallas_call(
        body,
        grid=(count,),
        out_shape=sum_shapes + made,
        in_specs=[
            pl.BlockSpec(memory_space=pltpu.SMEM),
            pl.BlockSpec((1, 128, 1024), lambda i: (i, 0, 0)),
        ]
        + [whole(part) for part in flat]
        + [whole(raw) for raw, _ in raws]
        + [acc_spec] * len(old),
        out_specs=sum_specs + [whole(part) for part in made],
        compiler_params=PARAMS,
        cost_estimate=cost(weight * count, cols),
        name="add_tiles",
    )(amp, left, *flat, *[raw for raw, _ in raws], *old)
    return (out[:sums] if narrow else out[0]), tuple(out[sums:])


def shift(value, axis, by):
    size = SIZES[NAMES.index(axis)]
    return lax.ppermute(value, axis, [(i, (i + by) % size) for i in range(size)])


def per_device(points, vectors, lengthscale, outscale, noise):
    zl = lax.axis_index("zl").astype(jnp.int32).reshape(1)
    amp = jnp.concatenate([outscale, jnp.log(outscale)])

    given, kept = first_pack(zl, points.T, vectors.T, lengthscale)
    got = shift(given, "zl", 1)
    half = copy_of([given], 64, kept, 4096)
    mines = [shift(half, "x", by) for by in (1, -1, 2)]
    own_left, share = second_pack(zl, amp, half, got, kept)

    beside = shift(share, "c", 1)
    near = [shift(share, "y", by) for by in (2, 1, -1)]
    mined = copy_of(mines, 64, share, 16)
    mined, beside = lax.optimization_barrier((mined, beside))
    theirs = shift(mined, "zl", 1)
    own, ready0 = add_tiles(amp, own_left, [], [(share, 0), (beside, 0)], weight=4096)
    near[0], near[1], near[2], own = lax.optimization_barrier((near[0], near[1], near[2], own))
    merged = jnp.concatenate([share] + near, axis=0)
    far = shift(merged, "zh", 1)
    merged_beside = shift(merged, "c", 1)
    own, ready1 = add_tiles(amp, own_left, [], [(merged, 1)], own, weight=64)

    theirs, own = lax.optimization_barrier((theirs, own))
    left = ready_rows(amp, mines, theirs)
    acc, ready2 = add_tiles(amp, left, [ready0, ready1], [(merged_beside, 1)])
    far, acc = lax.optimization_barrier((far, acc))
    far_beside = shift(far, "c", 1)
    acc, ready3 = add_tiles(amp, left, [], [(far, 0)], acc)
    sent, ready4 = add_tiles(amp, left, [], [(far_beside, 0)], acc, narrow=True)
    arrived = [shift(sent[k], "x", by) for k, by in ((2, 2), (0, -1), (1, 1))]
    own, _ = add_tiles(amp, own_left, [ready2, ready3, ready4], [], own)
    mine, theirs = own[0, :32], own[0, 32:]
    for part in arrived:
        theirs = theirs + part[32:].astype(F32)
    for part in arrived:
        mine = mine + part[:32].astype(F32)
    result = mine + shift(theirs, "zl", 1)
    return result.T + noise[0] * vectors.astype(F32)


def solution(mesh):
    fine = Mesh(mesh.devices.reshape(SIZES), NAMES)
    placed = (P(BLK, "zl"), P(BLK, "zl"), P(), P(), P())
    return jax.shard_map(
        per_device, mesh=fine, in_specs=placed, out_specs=P(BLK, "zl"), check_vma=False
    )
```

```python
import jax
import jax.numpy as jnp
from jax import lax
from jax.experimental import pallas as pl
from jax.experimental.pallas import tpu as pltpu
from jax.sharding import Mesh, PartitionSpec as P

SIZES = (2, 4, 4, 2, 2)
NAMES = ("zh", "x", "y", "c", "zl")
BLK = ("zh", "x", "y", "c")
TM = 512
TN = 1024
F32 = jnp.float32
BF16 = jnp.bfloat16
PARAMS = pltpu.CompilerParams(vmem_limit_bytes=48 << 20)


SCALE = 512


def cost(rows, cols):
    return pl.CostEstimate(flops=rows * cols * SCALE, transcendentals=0, bytes_accessed=cols * 384)


def three_parts(wide):
    hi = wide.astype(BF16).astype(F32)
    mid = (wide - hi).astype(BF16).astype(F32)
    return hi, mid, wide - hi - mid


def with_parts(features, offset, first):
    half = offset - 0.5 * jnp.sum(features * features, axis=0, keepdims=True)
    shape = (8, features.shape[1])
    row = lax.broadcasted_iota(jnp.int32, shape, 0)
    tail = jnp.where(row < 6, 1.0, 0.0)
    for place, part in enumerate(three_parts(half)):
        tail = jnp.where(row == first + place, part, tail)
    return jnp.concatenate([features, tail, jnp.zeros((56, features.shape[1]), F32)], axis=0)


def ready_rows(amp, mines, theirs):
    count = len(mines)

    def body(amp_ref, *refs):
        theirs_ref, out_ref = refs[count:]
        for k in range(count):
            for half in range(2):
                low = 32 * half
                mine = refs[k][low : low + 32, :].astype(F32)
                other = theirs_ref[64 * k + low : 64 * k + low + 32, :].astype(F32)
                features = jnp.concatenate([mine, other], axis=0)
                out_ref[k, :, 512 * half : 512 * half + 512] = with_parts(features, amp_ref[1], 3).astype(BF16)

    return pl.pallas_call(
        body,
        out_shape=jax.ShapeDtypeStruct((count, 128, 1024), BF16),
        in_specs=[pl.BlockSpec(memory_space=pltpu.SMEM)]
        + [pl.BlockSpec(memory_space=pltpu.VMEM)] * (count + 1),
        out_specs=pl.BlockSpec(memory_space=pltpu.VMEM),
        compiler_params=PARAMS,
        name="ready_rows",
    )(amp, *mines, theirs)


def kept_in_hbm(array):
    return pltpu.with_memory_space_constraint(array, pltpu.HBM)


def first_pack(zl, points, vectors, lengthscale):
    def body(zl_ref, points_in, vectors_in, length_in, out_ref, kept_ref, points_ref, vectors_ref, length_ref, sems):
        copies = [
            pltpu.make_async_copy(length_in, length_ref, sems.at[0]),
            pltpu.make_async_copy(points_in, points_ref, sems.at[1]),
            pltpu.make_async_copy(vectors_in, vectors_ref, sems.at[2]),
        ]
        for copy in copies:
            copy.start()
        for copy in copies:
            copy.wait()
        at = zl_ref[0]
        lane = lax.broadcasted_iota(jnp.int32, (32, 64), 1)
        row = lax.broadcasted_iota(jnp.int32, (32, 64), 0)
        column = jnp.sum(jnp.where(lane == row + 32 * at, length_ref[...], 0.0), axis=1, keepdims=True)
        scaled = (points_ref[...].astype(F32) / column).astype(BF16)
        out_ref[:32] = scaled[:, :512]
        out_ref[32:64] = scaled[:, 512:]
        given = vectors_ref[...].astype(F32)
        out_ref[64:] = jnp.where(at == 0, given[:, 512:], given[:, :512]).astype(BF16)
        kept_ref[...] = jnp.where(at == 0, given[:, :512], given[:, 512:]).astype(BF16)

    return pl.pallas_call(
        body,
        out_shape=(jax.ShapeDtypeStruct((96, 512), BF16), jax.ShapeDtypeStruct((32, 512), BF16)),
        in_specs=[pl.BlockSpec(memory_space=pltpu.SMEM)] + [pl.BlockSpec(memory_space=pltpu.HBM)] * 3,
        out_specs=(pl.BlockSpec(memory_space=pltpu.VMEM),) * 2,
        scratch_shapes=[
            pltpu.VMEM((32, 1024), BF16),
            pltpu.VMEM((32, 1024), BF16),
            pltpu.VMEM((1, 64), F32),
            pltpu.SemaphoreType.DMA((3,)),
        ],
        compiler_params=PARAMS,
        name="first_pack",
    )(zl, *(kept_in_hbm(a) for a in (points, vectors, lengthscale.reshape(1, 64))))


def copy_of(parts, rows, token, weight):
    def body(token_ref, *refs):
        at = 0
        for ref in refs[:-1]:
            refs[-1][at : at + rows] = ref[:rows]
            at += rows

    return pl.pallas_call(
        body,
        out_shape=jax.ShapeDtypeStruct((rows * len(parts), parts[0].shape[1]), BF16),
        in_specs=[pl.BlockSpec(memory_space=pl.ANY)]
        + [pl.BlockSpec(memory_space=pltpu.VMEM)] * len(parts),
        out_specs=pl.BlockSpec(memory_space=pltpu.VMEM),
        compiler_params=PARAMS,
        cost_estimate=cost(weight, 1024),
        name="copy_of",
    )(token, *parts)


def second_pack(zl, amp, half, got, kept):
    def body(zl_ref, amp_ref, half_ref, got_ref, kept_ref, rows_ref, share_ref):
        first = zl_ref[0] == 0
        mine = half_ref[...].astype(F32)
        theirs = got_ref[...].astype(F32)
        low = jnp.concatenate([mine[:32], theirs[:32]], axis=0)
        high = jnp.concatenate([mine[32:], theirs[32:64]], axis=0)
        picked = jnp.where(first, low, high)
        share_ref[...] = jnp.concatenate([picked, kept_ref[...].astype(F32), theirs[64:]], axis=0).astype(BF16)
        for k, features in enumerate((low, high)):
            rows_ref[0, :, 512 * k : 512 * k + 512] = with_parts(features, amp_ref[1], 3).astype(BF16)

    return pl.pallas_call(
        body,
        out_shape=[jax.ShapeDtypeStruct((1, 128, 1024), BF16), jax.ShapeDtypeStruct((128, 512), BF16)],
        in_specs=[pl.BlockSpec(memory_space=pltpu.SMEM)] * 2 + [pl.BlockSpec(memory_space=pltpu.VMEM)] * 3,
        out_specs=[pl.BlockSpec(memory_space=pltpu.VMEM)] * 2,
        compiler_params=PARAMS,
        name="second_pack",
    )(zl, amp, half, got, kept)


def one_block(left, right, vectors, top):
    exponent = jnp.dot(right, left, preferred_element_type=F32)
    block = jnp.minimum(jnp.exp(exponent).astype(BF16), top)
    return jnp.dot(vectors, block, preferred_element_type=F32)


def ready_sum(lefts, pairs, top):
    sums = [jnp.zeros((64, TM), F32) for _ in lefts]
    for right_ref, vectors_ref in pairs:
        total = right_ref.shape[0]
        for at in range(0, total, TN):
            part = slice(at, min(at + TN, total))
            for k, left in enumerate(lefts):
                sums[k] += one_block(left, right_ref[part, :], vectors_ref[:, part], top)
    return sums


def raw_sum(lefts, raws, right_ref, vectors_ref, top):
    total = right_ref.shape[0]
    sums = [jnp.zeros((64, TM), F32) for _ in lefts]
    at = 0
    rights, turned = [], []
    for ref, start in raws:
        for sub in range(128 * start, ref.shape[0], 128):
            features = ref[sub : sub + 64, :].astype(F32)
            rights.append(with_parts(features, 0.0, 0).T.astype(BF16))
            turned.append(ref[sub + 64 : sub + 128, :])
            right_ref[at : at + 512, :] = rights[-1]
            vectors_ref[:, at : at + 512] = turned[-1]
            at += 512
            if len(rights) * 512 == TN or at == total:
                right = jnp.concatenate(rights, axis=0)
                vectors = jnp.concatenate(turned, axis=1)
                for k, left in enumerate(lefts):
                    sums[k] += one_block(left, right, vectors, top)
                rights, turned = [], []
    return sums


def add_tiles(amp, left, ready, raws, before=None, narrow=False, weight=1024):
    count = left.shape[0]
    flat = [part for pair in ready for part in pair]
    total = sum(4 * raw.shape[0] - 512 * start for raw, start in raws)
    cols = total + sum(right.shape[0] for right, _ in ready)
    old = [] if before is None else [before]
    sums = count if narrow else 1
    ends = [len(flat), len(raws), len(old), sums]

    def body(amp_ref, left_ref, *refs):
        groups = []
        for size in ends:
            groups.append(refs[:size])
            refs = refs[size:]
        flat_refs, raw_refs, before_refs, sum_refs = groups
        pairs = [(flat_refs[2 * k], flat_refs[2 * k + 1]) for k in range(len(ready))]
        step = pl.program_id(0)
        top = jnp.full((1, 1), amp_ref[0], F32).astype(BF16)

        def put(value):
            if before_refs:
                value += before_refs[0][0]
            if not narrow:
                sum_refs[0][0] = value
                return
            for k in range(count):

                @pl.when(step == k)
                def _():
                    sum_refs[k][...] = value.astype(BF16)

        def tiles(fresh):
            lefts = [left_ref[0, :, at : at + TM] for at in range(0, 1024, TM)]
            sums = ready_sum(lefts, pairs if fresh or not raws else pairs + [tuple(refs)], top)
            if fresh:
                starts = [(ref, start) for ref, (_, start) in zip(raw_refs, raws)]
                sums = [a + b for a, b in zip(sums, raw_sum(lefts, starts, *refs, top))]
            put(jnp.concatenate(sums, axis=1))

        if not raws:
            tiles(False)
            return

        @pl.when(step == 0)
        def _():
            tiles(True)

        @pl.when(step > 0)
        def _():
            tiles(False)


    def whole(array):
        return pl.BlockSpec(array.shape, lambda i: (0, 0))

    acc_spec = pl.BlockSpec((1, 64, 1024), lambda i: (i, 0, 0))
    if narrow:
        sum_shapes = [jax.ShapeDtypeStruct((64, 1024), BF16)] * count
        sum_specs = [whole(part) for part in sum_shapes]
    else:
        sum_shapes = [jax.ShapeDtypeStruct((count, 64, 1024), F32)]
        sum_specs = [acc_spec]
    made = []
    if raws:
        made = [jax.ShapeDtypeStruct((total, 128), BF16), jax.ShapeDtypeStruct((64, total), BF16)]
    out = pl.pallas_call(
        body,
        grid=(count,),
        out_shape=sum_shapes + made,
        in_specs=[
            pl.BlockSpec(memory_space=pltpu.SMEM),
            pl.BlockSpec((1, 128, 1024), lambda i: (i, 0, 0)),
        ]
        + [whole(part) for part in flat]
        + [whole(raw) for raw, _ in raws]
        + [acc_spec] * len(old),
        out_specs=sum_specs + [whole(part) for part in made],
        compiler_params=PARAMS,
        cost_estimate=cost(weight * count, cols),
        name="add_tiles",
    )(amp, left, *flat, *[raw for raw, _ in raws], *old)
    return (out[:sums] if narrow else out[0]), tuple(out[sums:])


def shift(value, axis, by):
    size = SIZES[NAMES.index(axis)]
    return lax.ppermute(value, axis, [(i, (i + by) % size) for i in range(size)])


def per_device(points, vectors, lengthscale, outscale, noise):
    zl = lax.axis_index("zl").astype(jnp.int32).reshape(1)
    amp = jnp.concatenate([outscale, jnp.log(outscale)])

    given, kept = first_pack(zl, points.T, vectors.T, lengthscale)
    got = shift(given, "zl", 1)
    half = copy_of([given], 64, kept, 4096)
    mines = [shift(half, "x", by) for by in (1, -1, 2)]
    own_left, share = second_pack(zl, amp, half, got, kept)

    beside = shift(share, "c", 1)
    near = [shift(share, "y", by) for by in (2, 1, -1)]
    mined = copy_of(mines, 64, share, 16)
    mined, beside = lax.optimization_barrier((mined, beside))
    theirs = shift(mined, "zl", 1)
    own, ready0 = add_tiles(amp, own_left, [], [(share, 0), (beside, 0)], weight=4096)
    near[0], near[1], near[2], own = lax.optimization_barrier((near[0], near[1], near[2], own))
    merged = jnp.concatenate([share] + near, axis=0)
    far = shift(merged, "zh", 1)
    merged_beside = shift(merged, "c", 1)
    own, ready1 = add_tiles(amp, own_left, [], [(merged, 1)], own, weight=64)

    theirs, own = lax.optimization_barrier((theirs, own))
    left = ready_rows(amp, mines, theirs)
    acc, ready2 = add_tiles(amp, left, [ready0, ready1], [(merged_beside, 1)])
    far, acc = lax.optimization_barrier((far, acc))
    far_beside = shift(far, "c", 1)
    acc, ready3 = add_tiles(amp, left, [], [(far, 0)], acc)
    sent, ready4 = add_tiles(amp, left, [], [(far_beside, 0)], acc, narrow=True)
    arrived = [shift(sent[k], "x", by) for k, by in ((2, 2), (0, -1), (1, 1))]
    own, _ = add_tiles(amp, own_left, [ready2, ready3, ready4], [], own)
    mine, theirs = own[0, :32], own[0, 32:]
    for part in arrived:
        theirs = theirs + part[32:].astype(F32)
    for part in arrived:
        mine = mine + part[:32].astype(F32)
    result = mine + shift(theirs.astype(BF16), "zl", 1).astype(F32)
    return result.T + noise[0] * vectors.astype(F32)


def solution(mesh):
    fine = Mesh(mesh.devices.reshape(SIZES), NAMES)
    placed = (P(BLK, "zl"), P(BLK, "zl"), P(), P(), P())
    return jax.shard_map(
        per_device, mesh=fine, in_specs=placed, out_specs=P(BLK, "zl"), check_vma=False
    )
```

```python
import jax
import jax.numpy as jnp
from jax import lax
from jax.experimental import pallas as pl
from jax.experimental.pallas import tpu as pltpu
from jax.sharding import Mesh, PartitionSpec as P

SIZES = (2, 4, 4, 2, 2)
NAMES = ("zh", "x", "y", "c", "zl")
BLK = ("zh", "x", "y", "c")
TM = 512
TN = 1024
F32 = jnp.float32
BF16 = jnp.bfloat16
PARAMS = pltpu.CompilerParams(vmem_limit_bytes=48 << 20)


SCALE = 512


def cost(rows, cols):
    return pl.CostEstimate(flops=rows * cols * SCALE, transcendentals=0, bytes_accessed=cols * 384)


def three_parts(wide):
    hi = wide.astype(BF16).astype(F32)
    mid = (wide - hi).astype(BF16).astype(F32)
    return hi, mid, wide - hi - mid


def with_parts(features, offset, first):
    half = offset - 0.5 * jnp.sum(features * features, axis=0, keepdims=True)
    shape = (8, features.shape[1])
    row = lax.broadcasted_iota(jnp.int32, shape, 0)
    tail = jnp.where(row < 6, 1.0, 0.0)
    for place, part in enumerate(three_parts(half)):
        tail = jnp.where(row == first + place, part, tail)
    return jnp.concatenate([features, tail, jnp.zeros((56, features.shape[1]), F32)], axis=0)


def ready_rows(amp, mines, theirs, entire):
    count = len(mines)

    def body(amp_ref, *refs):
        theirs_ref, entire_ref, out_ref = refs[count:]
        for half in range(2):
            features = entire_ref[64 * half : 64 * half + 64, :].astype(F32)
            out_ref[count, :, 512 * half : 512 * half + 512] = with_parts(features, amp_ref[1], 3).astype(BF16)
        for k in range(count):
            for half in range(2):
                low = 32 * half
                mine = refs[k][low : low + 32, :].astype(F32)
                other = theirs_ref[64 * k + low : 64 * k + low + 32, :].astype(F32)
                features = jnp.concatenate([mine, other], axis=0)
                out_ref[k, :, 512 * half : 512 * half + 512] = with_parts(features, amp_ref[1], 3).astype(BF16)

    return pl.pallas_call(
        body,
        out_shape=jax.ShapeDtypeStruct((count + 1, 128, 1024), BF16),
        in_specs=[pl.BlockSpec(memory_space=pltpu.SMEM)]
        + [pl.BlockSpec(memory_space=pltpu.VMEM)] * (count + 2),
        out_specs=pl.BlockSpec(memory_space=pltpu.VMEM),
        compiler_params=PARAMS,
        name="ready_rows",
    )(amp, *mines, theirs, entire)


def kept_in_hbm(array):
    return pltpu.with_memory_space_constraint(array, pltpu.HBM)


def first_pack(zl, points, vectors, lengthscale):
    def body(zl_ref, points_in, vectors_in, length_in, out_ref, kept_ref, points_ref, vectors_ref, length_ref, sems):
        copies = [
            pltpu.make_async_copy(length_in, length_ref, sems.at[0]),
            pltpu.make_async_copy(points_in, points_ref, sems.at[1]),
            pltpu.make_async_copy(vectors_in, vectors_ref, sems.at[2]),
        ]
        for copy in copies:
            copy.start()
        for copy in copies:
            copy.wait()
        at = zl_ref[0]
        lane = lax.broadcasted_iota(jnp.int32, (32, 64), 1)
        row = lax.broadcasted_iota(jnp.int32, (32, 64), 0)
        column = jnp.sum(jnp.where(lane == row + 32 * at, length_ref[...], 0.0), axis=1, keepdims=True)
        scaled = (points_ref[...].astype(F32) / column).astype(BF16)
        out_ref[:32] = scaled[:, :512]
        out_ref[32:64] = scaled[:, 512:]
        given = vectors_ref[...].astype(F32)
        out_ref[64:] = jnp.where(at == 0, given[:, 512:], given[:, :512]).astype(BF16)
        kept_ref[...] = jnp.where(at == 0, given[:, :512], given[:, 512:]).astype(BF16)

    return pl.pallas_call(
        body,
        out_shape=(jax.ShapeDtypeStruct((96, 512), BF16), jax.ShapeDtypeStruct((32, 512), BF16)),
        in_specs=[pl.BlockSpec(memory_space=pltpu.SMEM)] + [pl.BlockSpec(memory_space=pltpu.HBM)] * 3,
        out_specs=(pl.BlockSpec(memory_space=pltpu.VMEM),) * 2,
        scratch_shapes=[
            pltpu.VMEM((32, 1024), BF16),
            pltpu.VMEM((32, 1024), BF16),
            pltpu.VMEM((1, 64), F32),
            pltpu.SemaphoreType.DMA((3,)),
        ],
        compiler_params=PARAMS,
        name="first_pack",
    )(zl, *(kept_in_hbm(a) for a in (points, vectors, lengthscale.reshape(1, 64))))


def copy_of(parts, rows, token, weight):
    def body(token_ref, *refs):
        at = 0
        for ref in refs[:-1]:
            refs[-1][at : at + rows] = ref[:rows]
            at += rows

    return pl.pallas_call(
        body,
        out_shape=jax.ShapeDtypeStruct((rows * len(parts), parts[0].shape[1]), BF16),
        in_specs=[pl.BlockSpec(memory_space=pl.ANY)]
        + [pl.BlockSpec(memory_space=pltpu.VMEM)] * len(parts),
        out_specs=pl.BlockSpec(memory_space=pltpu.VMEM),
        compiler_params=PARAMS,
        cost_estimate=cost(weight, 1024),
        name="copy_of",
    )(token, *parts)


def second_pack(zl, amp, half, got, kept):
    def body(zl_ref, amp_ref, half_ref, got_ref, kept_ref, rows_ref, share_ref, entire_ref):
        first = zl_ref[0] == 0
        mine = half_ref[...].astype(F32)
        theirs = got_ref[...].astype(F32)
        low = jnp.concatenate([mine[:32], theirs[:32]], axis=0)
        high = jnp.concatenate([mine[32:], theirs[32:64]], axis=0)
        entire_ref[...] = jnp.concatenate([low, high], axis=0).astype(BF16)
        picked = jnp.where(first, low, high)
        share_ref[...] = jnp.concatenate([picked, kept_ref[...].astype(F32), theirs[64:]], axis=0).astype(BF16)
        for k, features in enumerate((low, high)):
            rows_ref[0, :, 512 * k : 512 * k + 512] = with_parts(features, amp_ref[1], 3).astype(BF16)

    return pl.pallas_call(
        body,
        out_shape=[jax.ShapeDtypeStruct((1, 128, 1024), BF16)] + [jax.ShapeDtypeStruct((128, 512), BF16)] * 2,
        in_specs=[pl.BlockSpec(memory_space=pltpu.SMEM)] * 2 + [pl.BlockSpec(memory_space=pltpu.VMEM)] * 3,
        out_specs=[pl.BlockSpec(memory_space=pltpu.VMEM)] * 3,
        compiler_params=PARAMS,
        name="second_pack",
    )(zl, amp, half, got, kept)


def one_block(left, right, vectors, top):
    exponent = jnp.dot(right, left, preferred_element_type=F32)
    block = jnp.minimum(jnp.exp(exponent).astype(BF16), top)
    return jnp.dot(vectors, block, preferred_element_type=F32)


def ready_sum(lefts, pairs, top):
    sums = [jnp.zeros((64, TM), F32) for _ in lefts]
    for right_ref, vectors_ref in pairs:
        total = right_ref.shape[0]
        for at in range(0, total, TN):
            part = slice(at, min(at + TN, total))
            for k, left in enumerate(lefts):
                sums[k] += one_block(left, right_ref[part, :], vectors_ref[:, part], top)
    return sums


def raw_sum(lefts, raws, right_ref, vectors_ref, top):
    total = right_ref.shape[0]
    sums = [jnp.zeros((64, TM), F32) for _ in lefts]
    at = 0
    rights, turned = [], []
    for ref, start in raws:
        for sub in range(128 * start, ref.shape[0], 128):
            features = ref[sub : sub + 64, :].astype(F32)
            rights.append(with_parts(features, 0.0, 0).T.astype(BF16))
            turned.append(ref[sub + 64 : sub + 128, :])
            right_ref[at : at + 512, :] = rights[-1]
            vectors_ref[:, at : at + 512] = turned[-1]
            at += 512
            if len(rights) * 512 == TN or at == total:
                right = jnp.concatenate(rights, axis=0)
                vectors = jnp.concatenate(turned, axis=1)
                for k, left in enumerate(lefts):
                    sums[k] += one_block(left, right, vectors, top)
                rights, turned = [], []
    return sums


def add_tiles(amp, left, ready, raws, before=None, narrow=False, weight=1024):
    count = left.shape[0]
    flat = [part for pair in ready for part in pair]
    total = sum(4 * raw.shape[0] - 512 * start for raw, start in raws)
    cols = total + sum(right.shape[0] for right, _ in ready)
    old = [] if before is None else [before]
    sums = count if narrow else 1
    ends = [len(flat), len(raws), len(old), sums]

    def body(amp_ref, left_ref, *refs):
        groups = []
        for size in ends:
            groups.append(refs[:size])
            refs = refs[size:]
        flat_refs, raw_refs, before_refs, sum_refs = groups
        pairs = [(flat_refs[2 * k], flat_refs[2 * k + 1]) for k in range(len(ready))]
        step = pl.program_id(0)
        top = jnp.full((1, 1), amp_ref[0], F32).astype(BF16)

        def put(value):
            if before_refs:
                value += before_refs[0][0]
            if not narrow:
                sum_refs[0][0] = value
                return
            for k in range(count):

                @pl.when(step == k)
                def _():
                    sum_refs[k][...] = value.astype(BF16)

        def tiles(fresh):
            lefts = [left_ref[0, :, at : at + TM] for at in range(0, 1024, TM)]
            sums = ready_sum(lefts, pairs if fresh or not raws else pairs + [tuple(refs)], top)
            if fresh:
                starts = [(ref, start) for ref, (_, start) in zip(raw_refs, raws)]
                sums = [a + b for a, b in zip(sums, raw_sum(lefts, starts, *refs, top))]
            put(jnp.concatenate(sums, axis=1))

        if not raws:
            tiles(False)
            return

        @pl.when(step == 0)
        def _():
            tiles(True)

        @pl.when(step > 0)
        def _():
            tiles(False)


    def whole(array):
        return pl.BlockSpec(array.shape, lambda i: (0, 0))

    acc_spec = pl.BlockSpec((1, 64, 1024), lambda i: (i, 0, 0))
    if narrow:
        sum_shapes = [jax.ShapeDtypeStruct((64, 1024), BF16)] * count
        sum_specs = [whole(part) for part in sum_shapes]
    else:
        sum_shapes = [jax.ShapeDtypeStruct((count, 64, 1024), F32)]
        sum_specs = [acc_spec]
    made = []
    if raws:
        made = [jax.ShapeDtypeStruct((total, 128), BF16), jax.ShapeDtypeStruct((64, total), BF16)]
    out = pl.pallas_call(
        body,
        grid=(count,),
        out_shape=sum_shapes + made,
        in_specs=[
            pl.BlockSpec(memory_space=pltpu.SMEM),
            pl.BlockSpec((1, 128, 1024), lambda i: (i, 0, 0)),
        ]
        + [whole(part) for part in flat]
        + [whole(raw) for raw, _ in raws]
        + [acc_spec] * len(old),
        out_specs=sum_specs + [whole(part) for part in made],
        compiler_params=PARAMS,
        cost_estimate=cost(weight * count, cols),
        name="add_tiles",
    )(amp, left, *flat, *[raw for raw, _ in raws], *old)
    return (out[:sums] if narrow else out[0]), tuple(out[sums:])


def shift(value, axis, by):
    size = SIZES[NAMES.index(axis)]
    return lax.ppermute(value, axis, [(i, (i + by) % size) for i in range(size)])


def per_device(points, vectors, lengthscale, outscale, noise):
    zl = lax.axis_index("zl").astype(jnp.int32).reshape(1)
    amp = jnp.concatenate([outscale, jnp.log(outscale)])

    given, kept = first_pack(zl, points.T, vectors.T, lengthscale)
    got = shift(given, "zl", 1)
    half = copy_of([given], 64, kept, 4096)
    mines = [shift(half, "x", by) for by in (1, -1)]
    own_left, share, entire = second_pack(zl, amp, half, got, kept)

    beside = shift(share, "c", 1)
    near = [shift(share, "y", by) for by in (2, 1, -1)]
    entire = shift(entire, "x", 2)
    mined = copy_of(mines, 64, share, 16)
    mined, beside, entire = lax.optimization_barrier((mined, beside, entire))
    theirs = shift(mined, "zl", 1)
    own, ready0 = add_tiles(amp, own_left, [], [(share, 0), (beside, 0)], weight=4096)
    near[0], near[1], near[2], own = lax.optimization_barrier((near[0], near[1], near[2], own))
    merged = jnp.concatenate([share] + near, axis=0)
    far = shift(merged, "zh", 1)
    merged_beside = shift(merged, "c", 1)
    own, ready1 = add_tiles(amp, own_left, [], [(merged, 1)], own, weight=64)

    theirs, own = lax.optimization_barrier((theirs, own))
    left = ready_rows(amp, mines, theirs, entire)
    acc, ready2 = add_tiles(amp, left, [ready0, ready1], [(merged_beside, 1)])
    far, acc = lax.optimization_barrier((far, acc))
    far_beside = shift(far, "c", 1)
    acc, ready3 = add_tiles(amp, left, [], [(far, 0)], acc)
    sent, ready4 = add_tiles(amp, left, [], [(far_beside, 0)], acc, narrow=True)
    arrived = [shift(sent[k], "x", by) for k, by in ((2, 2), (0, -1), (1, 1))]
    own, _ = add_tiles(amp, own_left, [ready2, ready3, ready4], [], own)
    mine, theirs = own[0, :32], own[0, 32:]
    for part in arrived:
        theirs = theirs + part[32:].astype(F32)
    for part in arrived:
        mine = mine + part[:32].astype(F32)
    result = mine + shift(theirs, "zl", 1)
    return result.T + noise[0] * vectors.astype(F32)


def solution(mesh):
    fine = Mesh(mesh.devices.reshape(SIZES), NAMES)
    placed = (P(BLK, "zl"), P(BLK, "zl"), P(), P(), P())
    return jax.shard_map(
        per_device, mesh=fine, in_specs=placed, out_specs=P(BLK, "zl"), check_vma=False
    )
```

```python
import jax
import jax.numpy as jnp
from jax import lax
from jax.experimental import pallas as pl
from jax.experimental.pallas import tpu as pltpu
from jax.sharding import Mesh, PartitionSpec as P

SIZES = (2, 4, 4, 2, 2)
NAMES = ("zh", "x", "y", "c", "zl")
BLK = ("zh", "x", "y", "c")
TM = 512
TN = 1024
F32 = jnp.float32
BF16 = jnp.bfloat16
PARAMS = pltpu.CompilerParams(vmem_limit_bytes=48 << 20)


SCALE = 512


def cost(rows, cols):
    return pl.CostEstimate(flops=rows * cols * SCALE, transcendentals=0, bytes_accessed=cols * 384)


def three_parts(wide):
    hi = wide.astype(BF16).astype(F32)
    mid = (wide - hi).astype(BF16).astype(F32)
    return hi, mid, wide - hi - mid


def with_parts(features, offset, first):
    half = offset - 0.5 * jnp.sum(features * features, axis=0, keepdims=True)
    shape = (8, features.shape[1])
    row = lax.broadcasted_iota(jnp.int32, shape, 0)
    tail = jnp.where(row < 6, 1.0, 0.0)
    for place, part in enumerate(three_parts(half)):
        tail = jnp.where(row == first + place, part, tail)
    return jnp.concatenate([features, tail, jnp.zeros((56, features.shape[1]), F32)], axis=0)


def ready_rows(amp, mines, theirs, entire):
    count = len(mines)

    def body(amp_ref, *refs):
        theirs_ref, entire_ref, out_ref = refs[count:]
        for half in range(2):
            features = entire_ref[64 * half : 64 * half + 64, :].astype(F32)
            out_ref[count, :, 512 * half : 512 * half + 512] = with_parts(features, amp_ref[1], 3).astype(BF16)
        for k in range(count):
            for half in range(2):
                low = 32 * half
                mine = refs[k][low : low + 32, :].astype(F32)
                other = theirs_ref[64 * k + low : 64 * k + low + 32, :].astype(F32)
                features = jnp.concatenate([mine, other], axis=0)
                out_ref[k, :, 512 * half : 512 * half + 512] = with_parts(features, amp_ref[1], 3).astype(BF16)

    return pl.pallas_call(
        body,
        out_shape=jax.ShapeDtypeStruct((count + 1, 128, 1024), BF16),
        in_specs=[pl.BlockSpec(memory_space=pltpu.SMEM)]
        + [pl.BlockSpec(memory_space=pltpu.VMEM)] * (count + 2),
        out_specs=pl.BlockSpec(memory_space=pltpu.VMEM),
        compiler_params=PARAMS,
        name="ready_rows",
    )(amp, *mines, theirs, entire)


def kept_in_hbm(array):
    return pltpu.with_memory_space_constraint(array, pltpu.HBM)


def first_pack(zl, points, vectors, lengthscale):
    def body(zl_ref, points_in, vectors_in, length_in, out_ref, kept_ref, points_ref, vectors_ref, length_ref, sems):
        copies = [
            pltpu.make_async_copy(length_in, length_ref, sems.at[0]),
            pltpu.make_async_copy(points_in, points_ref, sems.at[1]),
            pltpu.make_async_copy(vectors_in, vectors_ref, sems.at[2]),
        ]
        for copy in copies:
            copy.start()
        for copy in copies:
            copy.wait()
        at = zl_ref[0]
        lane = lax.broadcasted_iota(jnp.int32, (32, 64), 1)
        row = lax.broadcasted_iota(jnp.int32, (32, 64), 0)
        column = jnp.sum(jnp.where(lane == row + 32 * at, length_ref[...], 0.0), axis=1, keepdims=True)
        scaled = (points_ref[...].astype(F32) / column).astype(BF16)
        out_ref[:32] = scaled[:, :512]
        out_ref[32:64] = scaled[:, 512:]
        given = vectors_ref[...].astype(F32)
        out_ref[64:] = jnp.where(at == 0, given[:, 512:], given[:, :512]).astype(BF16)
        kept_ref[...] = jnp.where(at == 0, given[:, :512], given[:, 512:]).astype(BF16)

    return pl.pallas_call(
        body,
        out_shape=(jax.ShapeDtypeStruct((96, 512), BF16), jax.ShapeDtypeStruct((32, 512), BF16)),
        in_specs=[pl.BlockSpec(memory_space=pltpu.SMEM)] + [pl.BlockSpec(memory_space=pltpu.HBM)] * 3,
        out_specs=(pl.BlockSpec(memory_space=pltpu.VMEM),) * 2,
        scratch_shapes=[
            pltpu.VMEM((32, 1024), BF16),
            pltpu.VMEM((32, 1024), BF16),
            pltpu.VMEM((1, 64), F32),
            pltpu.SemaphoreType.DMA((3,)),
        ],
        compiler_params=PARAMS,
        name="first_pack",
    )(zl, *(kept_in_hbm(a) for a in (points, vectors, lengthscale.reshape(1, 64))))


def copy_of(parts, rows, token, weight):
    def body(token_ref, *refs):
        at = 0
        for ref in refs[:-1]:
            refs[-1][at : at + rows] = ref[:rows]
            at += rows

    return pl.pallas_call(
        body,
        out_shape=jax.ShapeDtypeStruct((rows * len(parts), parts[0].shape[1]), BF16),
        in_specs=[pl.BlockSpec(memory_space=pl.ANY)]
        + [pl.BlockSpec(memory_space=pltpu.VMEM)] * len(parts),
        out_specs=pl.BlockSpec(memory_space=pltpu.VMEM),
        compiler_params=PARAMS,
        cost_estimate=cost(weight, 1024),
        name="copy_of",
    )(token, *parts)


def second_pack(zl, amp, half, got, kept):
    def body(zl_ref, amp_ref, half_ref, got_ref, kept_ref, rows_ref, share_ref, entire_ref):
        first = zl_ref[0] == 0
        mine = half_ref[...].astype(F32)
        theirs = got_ref[...].astype(F32)
        low = jnp.concatenate([mine[:32], theirs[:32]], axis=0)
        high = jnp.concatenate([mine[32:], theirs[32:64]], axis=0)
        entire_ref[...] = jnp.concatenate([low, high], axis=0).astype(BF16)
        picked = jnp.where(first, low, high)
        share_ref[...] = jnp.concatenate([picked, kept_ref[...].astype(F32), theirs[64:]], axis=0).astype(BF16)
        for k, features in enumerate((low, high)):
            rows_ref[0, :, 512 * k : 512 * k + 512] = with_parts(features, amp_ref[1], 3).astype(BF16)

    return pl.pallas_call(
        body,
        out_shape=[jax.ShapeDtypeStruct((1, 128, 1024), BF16)] + [jax.ShapeDtypeStruct((128, 512), BF16)] * 2,
        in_specs=[pl.BlockSpec(memory_space=pltpu.SMEM)] * 2 + [pl.BlockSpec(memory_space=pltpu.VMEM)] * 3,
        out_specs=[pl.BlockSpec(memory_space=pltpu.VMEM)] * 3,
        compiler_params=PARAMS,
        name="second_pack",
    )(zl, amp, half, got, kept)


def one_block(left, right, vectors, top):
    exponent = jnp.dot(right, left, preferred_element_type=F32)
    block = jnp.minimum(jnp.exp(exponent).astype(BF16), top)
    return jnp.dot(vectors, block, preferred_element_type=F32)


def ready_sum(lefts, pairs, top):
    sums = [jnp.zeros((64, TM), F32) for _ in lefts]
    for right_ref, vectors_ref in pairs:
        total = right_ref.shape[0]
        for at in range(0, total, TN):
            part = slice(at, min(at + TN, total))
            for k, left in enumerate(lefts):
                sums[k] += one_block(left, right_ref[part, :], vectors_ref[:, part], top)
    return sums


def raw_sum(lefts, raws, right_ref, vectors_ref, top):
    total = right_ref.shape[0]
    sums = [jnp.zeros((64, TM), F32) for _ in lefts]
    at = 0
    rights, turned = [], []
    for ref, start in raws:
        for sub in range(128 * start, ref.shape[0], 128):
            features = ref[sub : sub + 64, :].astype(F32)
            rights.append(with_parts(features, 0.0, 0).T.astype(BF16))
            turned.append(ref[sub + 64 : sub + 128, :])
            right_ref[at : at + 512, :] = rights[-1]
            vectors_ref[:, at : at + 512] = turned[-1]
            at += 512
            if len(rights) * 512 == TN or at == total:
                right = jnp.concatenate(rights, axis=0)
                vectors = jnp.concatenate(turned, axis=1)
                for k, left in enumerate(lefts):
                    sums[k] += one_block(left, right, vectors, top)
                rights, turned = [], []
    return sums


def add_tiles(amp, left, ready, raws, before=None, narrow=False, weight=1024):
    count = left.shape[0]
    flat = [part for pair in ready for part in pair]
    total = sum(4 * raw.shape[0] - 512 * start for raw, start in raws)
    cols = total + sum(right.shape[0] for right, _ in ready)
    old = [] if before is None else [before]
    sums = count if narrow else 1
    ends = [len(flat), len(raws), len(old), sums]

    def body(amp_ref, left_ref, *refs):
        groups = []
        for size in ends:
            groups.append(refs[:size])
            refs = refs[size:]
        flat_refs, raw_refs, before_refs, sum_refs = groups
        pairs = [(flat_refs[2 * k], flat_refs[2 * k + 1]) for k in range(len(ready))]
        step = pl.program_id(0)
        top = jnp.full((1, 1), amp_ref[0], F32).astype(BF16)

        def put(value):
            if before_refs:
                value += before_refs[0][0]
            if not narrow:
                sum_refs[0][0] = value
                return
            for k in range(count):

                @pl.when(step == k)
                def _():
                    sum_refs[k][...] = value.astype(BF16)

        def tiles(fresh):
            lefts = [left_ref[0, :, at : at + TM] for at in range(0, 1024, TM)]
            sums = ready_sum(lefts, pairs if fresh or not raws else pairs + [tuple(refs)], top)
            if fresh:
                starts = [(ref, start) for ref, (_, start) in zip(raw_refs, raws)]
                sums = [a + b for a, b in zip(sums, raw_sum(lefts, starts, *refs, top))]
            put(jnp.concatenate(sums, axis=1))

        if not raws:
            tiles(False)
            return

        @pl.when(step == 0)
        def _():
            tiles(True)

        @pl.when(step > 0)
        def _():
            tiles(False)


    def whole(array):
        return pl.BlockSpec(array.shape, lambda i: (0, 0))

    acc_spec = pl.BlockSpec((1, 64, 1024), lambda i: (i, 0, 0))
    if narrow:
        sum_shapes = [jax.ShapeDtypeStruct((64, 1024), BF16)] * count
        sum_specs = [whole(part) for part in sum_shapes]
    else:
        sum_shapes = [jax.ShapeDtypeStruct((count, 64, 1024), F32)]
        sum_specs = [acc_spec]
    made = []
    if raws:
        made = [jax.ShapeDtypeStruct((total, 128), BF16), jax.ShapeDtypeStruct((64, total), BF16)]
    out = pl.pallas_call(
        body,
        grid=(count,),
        out_shape=sum_shapes + made,
        in_specs=[
            pl.BlockSpec(memory_space=pltpu.SMEM),
            pl.BlockSpec((1, 128, 1024), lambda i: (i, 0, 0)),
        ]
        + [whole(part) for part in flat]
        + [whole(raw) for raw, _ in raws]
        + [acc_spec] * len(old),
        out_specs=sum_specs + [whole(part) for part in made],
        compiler_params=PARAMS,
        cost_estimate=cost(weight * count, cols),
        name="add_tiles",
    )(amp, left, *flat, *[raw for raw, _ in raws], *old)
    return (out[:sums] if narrow else out[0]), tuple(out[sums:])


def shift(value, axis, by):
    size = SIZES[NAMES.index(axis)]
    return lax.ppermute(value, axis, [(i, (i + by) % size) for i in range(size)])


def per_device(points, vectors, lengthscale, outscale, noise):
    zl = lax.axis_index("zl").astype(jnp.int32).reshape(1)
    amp = jnp.concatenate([outscale, jnp.log(outscale)])

    given, kept = first_pack(zl, points.T, vectors.T, lengthscale)
    got = shift(given, "zl", 1)
    half = copy_of([given], 64, kept, 4096)
    mines = [shift(half, "x", by) for by in (1, -1)]
    own_left, share, entire = second_pack(zl, amp, half, got, kept)

    beside = shift(share, "c", 1)
    near = [shift(share, "y", by) for by in (2, 1, -1)]
    entire = shift(entire, "x", 2)
    mined = copy_of(mines, 64, share, 16)
    mined, beside, entire = lax.optimization_barrier((mined, beside, entire))
    theirs = shift(mined, "zl", 1)
    own, ready0 = add_tiles(amp, own_left, [], [(share, 0), (beside, 0)], weight=4096)
    near[0], near[1], near[2], own = lax.optimization_barrier((near[0], near[1], near[2], own))
    merged = jnp.concatenate([share] + near, axis=0)
    far = shift(merged, "zh", 1)
    merged_beside = shift(merged, "c", 1)
    left = ready_rows(amp, mines, theirs, entire)
    acc, ready2 = add_tiles(amp, left, [ready0], [(merged, 1), (merged_beside, 1)])
    far, acc = lax.optimization_barrier((far, acc))
    far_beside = shift(far, "c", 1)
    acc, ready3 = add_tiles(amp, left, [], [(far, 0)], acc)
    sent, ready4 = add_tiles(amp, left, [], [(far_beside, 0)], acc, narrow=True)
    arrived = [shift(sent[k], "x", by) for k, by in ((2, 2), (0, -1), (1, 1))]
    own, _ = add_tiles(amp, own_left, [ready2, ready3, ready4], [], own)
    mine, theirs = own[0, :32], own[0, 32:]
    for part in arrived:
        theirs = theirs + part[32:].astype(F32)
    for part in arrived:
        mine = mine + part[:32].astype(F32)
    result = mine + shift(theirs, "zl", 1)
    return result.T + noise[0] * vectors.astype(F32)


def solution(mesh):
    fine = Mesh(mesh.devices.reshape(SIZES), NAMES)
    placed = (P(BLK, "zl"), P(BLK, "zl"), P(), P(), P())
    return jax.shard_map(
        per_device, mesh=fine, in_specs=placed, out_specs=P(BLK, "zl"), check_vma=False
    )
```

```python
import jax
import jax.numpy as jnp
from jax import lax
from jax.experimental import pallas as pl
from jax.experimental.pallas import tpu as pltpu
from jax.sharding import Mesh, PartitionSpec as P

SIZES = (2, 4, 4, 2, 2)
NAMES = ("zh", "x", "y", "c", "zl")
BLK = ("zh", "x", "y", "c")
TM = 512
TN = 1024
F32 = jnp.float32
BF16 = jnp.bfloat16
PARAMS = pltpu.CompilerParams(vmem_limit_bytes=48 << 20)


SCALE = 512


def cost(rows, cols):
    return pl.CostEstimate(flops=rows * cols * SCALE, transcendentals=0, bytes_accessed=cols * 384)


def three_parts(wide):
    hi = wide.astype(BF16).astype(F32)
    mid = (wide - hi).astype(BF16).astype(F32)
    return hi, mid, wide - hi - mid


def with_parts(features, offset, first):
    half = offset - 0.5 * jnp.sum(features * features, axis=0, keepdims=True)
    shape = (8, features.shape[1])
    row = lax.broadcasted_iota(jnp.int32, shape, 0)
    tail = jnp.where(row < 6, 1.0, 0.0)
    for place, part in enumerate(three_parts(half)):
        tail = jnp.where(row == first + place, part, tail)
    return jnp.concatenate([features, tail, jnp.zeros((56, features.shape[1]), F32)], axis=0)


def ready_rows(amp, mines, theirs, entire):
    count = len(mines)

    def body(amp_ref, *refs):
        theirs_ref, entire_ref, out_ref = refs[count:]
        for half in range(2):
            features = entire_ref[64 * half : 64 * half + 64, :].astype(F32)
            out_ref[count, :, 512 * half : 512 * half + 512] = with_parts(features, amp_ref[1], 3).astype(BF16)
        for k in range(count):
            for half in range(2):
                low = 32 * half
                mine = refs[k][low : low + 32, :].astype(F32)
                other = theirs_ref[64 * k + low : 64 * k + low + 32, :].astype(F32)
                features = jnp.concatenate([mine, other], axis=0)
                out_ref[k, :, 512 * half : 512 * half + 512] = with_parts(features, amp_ref[1], 3).astype(BF16)

    return pl.pallas_call(
        body,
        out_shape=jax.ShapeDtypeStruct((count + 1, 128, 1024), BF16),
        in_specs=[pl.BlockSpec(memory_space=pltpu.SMEM)]
        + [pl.BlockSpec(memory_space=pltpu.VMEM)] * (count + 2),
        out_specs=pl.BlockSpec(memory_space=pltpu.VMEM),
        compiler_params=PARAMS,
        name="ready_rows",
    )(amp, *mines, theirs, entire)


def kept_in_hbm(array):
    return pltpu.with_memory_space_constraint(array, pltpu.HBM)


def first_pack(zl, points, vectors, lengthscale):
    def body(zl_ref, points_in, vectors_in, length_in, out_ref, kept_ref, points_ref, vectors_ref, length_ref, sems):
        copies = [
            pltpu.make_async_copy(length_in, length_ref, sems.at[0]),
            pltpu.make_async_copy(points_in, points_ref, sems.at[1]),
            pltpu.make_async_copy(vectors_in, vectors_ref, sems.at[2]),
        ]
        for copy in copies:
            copy.start()
        for copy in copies:
            copy.wait()
        at = zl_ref[0]
        lane = lax.broadcasted_iota(jnp.int32, (32, 64), 1)
        row = lax.broadcasted_iota(jnp.int32, (32, 64), 0)
        column = jnp.sum(jnp.where(lane == row + 32 * at, length_ref[...], 0.0), axis=1, keepdims=True)
        scaled = (points_ref[...].astype(F32) / column).astype(BF16)
        out_ref[:32] = scaled[:, :512]
        out_ref[32:64] = scaled[:, 512:]
        given = vectors_ref[...].astype(F32)
        out_ref[64:] = jnp.where(at == 0, given[:, 512:], given[:, :512]).astype(BF16)
        kept_ref[...] = jnp.where(at == 0, given[:, :512], given[:, 512:]).astype(BF16)

    return pl.pallas_call(
        body,
        out_shape=(jax.ShapeDtypeStruct((96, 512), BF16), jax.ShapeDtypeStruct((32, 512), BF16)),
        in_specs=[pl.BlockSpec(memory_space=pltpu.SMEM)] + [pl.BlockSpec(memory_space=pltpu.HBM)] * 3,
        out_specs=(pl.BlockSpec(memory_space=pltpu.VMEM),) * 2,
        scratch_shapes=[
            pltpu.VMEM((32, 1024), BF16),
            pltpu.VMEM((32, 1024), BF16),
            pltpu.VMEM((1, 64), F32),
            pltpu.SemaphoreType.DMA((3,)),
        ],
        compiler_params=PARAMS,
        name="first_pack",
    )(zl, *(kept_in_hbm(a) for a in (points, vectors, lengthscale.reshape(1, 64))))


def copy_of(parts, rows, token, weight):
    def body(token_ref, *refs):
        at = 0
        for ref in refs[:-1]:
            refs[-1][at : at + rows] = ref[:rows]
            at += rows

    return pl.pallas_call(
        body,
        out_shape=jax.ShapeDtypeStruct((rows * len(parts), parts[0].shape[1]), BF16),
        in_specs=[pl.BlockSpec(memory_space=pl.ANY)]
        + [pl.BlockSpec(memory_space=pltpu.VMEM)] * len(parts),
        out_specs=pl.BlockSpec(memory_space=pltpu.VMEM),
        compiler_params=PARAMS,
        cost_estimate=cost(weight, 1024),
        name="copy_of",
    )(token, *parts)


def second_pack(zl, amp, half, got, kept):
    def body(zl_ref, amp_ref, half_ref, got_ref, kept_ref, rows_ref, share_ref, entire_ref):
        first = zl_ref[0] == 0
        mine = half_ref[...].astype(F32)
        theirs = got_ref[...].astype(F32)
        low = jnp.concatenate([mine[:32], theirs[:32]], axis=0)
        high = jnp.concatenate([mine[32:], theirs[32:64]], axis=0)
        entire_ref[...] = jnp.concatenate([low, high], axis=0).astype(BF16)
        picked = jnp.where(first, low, high)
        share_ref[...] = jnp.concatenate([picked, kept_ref[...].astype(F32), theirs[64:]], axis=0).astype(BF16)
        for k, features in enumerate((low, high)):
            rows_ref[0, :, 512 * k : 512 * k + 512] = with_parts(features, amp_ref[1], 3).astype(BF16)

    return pl.pallas_call(
        body,
        out_shape=[jax.ShapeDtypeStruct((1, 128, 1024), BF16)] + [jax.ShapeDtypeStruct((128, 512), BF16)] * 2,
        in_specs=[pl.BlockSpec(memory_space=pltpu.SMEM)] * 2 + [pl.BlockSpec(memory_space=pltpu.VMEM)] * 3,
        out_specs=[pl.BlockSpec(memory_space=pltpu.VMEM)] * 3,
        compiler_params=PARAMS,
        name="second_pack",
    )(zl, amp, half, got, kept)


def one_block(left, right, vectors, top):
    exponent = jnp.dot(right, left, preferred_element_type=F32)
    block = jnp.minimum(jnp.exp(exponent).astype(BF16), top)
    return jnp.dot(vectors, block, preferred_element_type=F32)


def ready_sum(lefts, pairs, top):
    sums = [jnp.zeros((64, TM), F32) for _ in lefts]
    for right_ref, vectors_ref, low, total in pairs:
        for at in range(low, total, TN):
            part = slice(at, min(at + TN, total))
            for k, left in enumerate(lefts):
                sums[k] += one_block(left, right_ref[part, :], vectors_ref[:, part], top)
    return sums


def raw_sum(lefts, raws, right_ref, vectors_ref, top):
    total = right_ref.shape[0]
    sums = [jnp.zeros((64, TM), F32) for _ in lefts]
    at = 0
    rights, turned = [], []
    for ref, start in raws:
        for sub in range(128 * start, ref.shape[0], 128):
            features = ref[sub : sub + 64, :].astype(F32)
            rights.append(with_parts(features, 0.0, 0).T.astype(BF16))
            turned.append(ref[sub + 64 : sub + 128, :])
            right_ref[at : at + 512, :] = rights[-1]
            vectors_ref[:, at : at + 512] = turned[-1]
            at += 512
            if len(rights) * 512 == TN or at == total:
                right = jnp.concatenate(rights, axis=0)
                vectors = jnp.concatenate(turned, axis=1)
                for k, left in enumerate(lefts):
                    sums[k] += one_block(left, right, vectors, top)
                rights, turned = [], []
    return sums


def add_tiles(amp, left, ready, raws, before=None, narrow=False, weight=1024):
    count = left.shape[0]
    flat = [part for pair in ready for part in pair[:2]]
    ranges = [pair[2:] or (0, pair[0].shape[0]) for pair in ready]
    total = sum(4 * raw.shape[0] - 512 * start for raw, start in raws)
    cols = total + sum(stop - low for low, stop in ranges)
    old = [] if before is None else [before]
    sums = count if narrow else 1
    ends = [len(flat), len(raws), len(old), sums]

    def body(amp_ref, left_ref, *refs):
        groups = []
        for size in ends:
            groups.append(refs[:size])
            refs = refs[size:]
        flat_refs, raw_refs, before_refs, sum_refs = groups
        pairs = [(flat_refs[2 * k], flat_refs[2 * k + 1], *ranges[k]) for k in range(len(ready))]
        step = pl.program_id(0)
        top = jnp.full((1, 1), amp_ref[0], F32).astype(BF16)

        def put(value):
            if before_refs:
                value += before_refs[0][0]
            if not narrow:
                sum_refs[0][0] = value
                return
            for k in range(count):

                @pl.when(step == k)
                def _():
                    sum_refs[k][...] = value.astype(BF16)

        def tiles(fresh):
            lefts = [left_ref[0, :, at : at + TM] for at in range(0, 1024, TM)]
            sums = ready_sum(lefts, pairs if fresh or not raws else pairs + [(*refs, 0, total)], top)
            if fresh:
                starts = [(ref, start) for ref, (_, start) in zip(raw_refs, raws)]
                sums = [a + b for a, b in zip(sums, raw_sum(lefts, starts, *refs, top))]
            put(jnp.concatenate(sums, axis=1))

        if not raws:
            tiles(False)
            return

        @pl.when(step == 0)
        def _():
            tiles(True)

        @pl.when(step > 0)
        def _():
            tiles(False)


    def whole(array):
        return pl.BlockSpec(array.shape, lambda i: (0, 0))

    acc_spec = pl.BlockSpec((1, 64, 1024), lambda i: (i, 0, 0))
    if narrow:
        sum_shapes = [jax.ShapeDtypeStruct((64, 1024), BF16)] * count
        sum_specs = [whole(part) for part in sum_shapes]
    else:
        sum_shapes = [jax.ShapeDtypeStruct((count, 64, 1024), F32)]
        sum_specs = [acc_spec]
    made = []
    if raws:
        made = [jax.ShapeDtypeStruct((total, 128), BF16), jax.ShapeDtypeStruct((64, total), BF16)]
    out = pl.pallas_call(
        body,
        grid=(count,),
        out_shape=sum_shapes + made,
        in_specs=[
            pl.BlockSpec(memory_space=pltpu.SMEM),
            pl.BlockSpec((1, 128, 1024), lambda i: (i, 0, 0)),
        ]
        + [whole(part) for part in flat]
        + [whole(raw) for raw, _ in raws]
        + [acc_spec] * len(old),
        out_specs=sum_specs + [whole(part) for part in made],
        compiler_params=PARAMS,
        cost_estimate=cost(weight * count, cols),
        name="add_tiles",
    )(amp, left, *flat, *[raw for raw, _ in raws], *old)
    return (out[:sums] if narrow else out[0]), tuple(out[sums:])


def shift(value, axis, by):
    size = SIZES[NAMES.index(axis)]
    return lax.ppermute(value, axis, [(i, (i + by) % size) for i in range(size)])


def per_device(points, vectors, lengthscale, outscale, noise):
    zl = lax.axis_index("zl").astype(jnp.int32).reshape(1)
    amp = jnp.concatenate([outscale, jnp.log(outscale)])

    given, kept = first_pack(zl, points.T, vectors.T, lengthscale)
    got = shift(given, "zl", 1)
    half = copy_of([given], 64, kept, 4096)
    mines = [shift(half, "x", by) for by in (1, -1)]
    own_left, share, entire = second_pack(zl, amp, half, got, kept)

    beside = shift(share, "c", 1)
    near = [shift(share, "y", by) for by in (2, 1, -1)]
    entire = shift(entire, "x", 2)
    mined = copy_of(mines, 64, share, 16)
    mined, beside, entire = lax.optimization_barrier((mined, beside, entire))
    theirs = shift(mined, "zl", 1)
    own, ready0 = add_tiles(amp, own_left, [], [(share, 0), (beside, 0)], weight=4096)
    near[0], near[1], near[2], own = lax.optimization_barrier((near[0], near[1], near[2], own))
    merged = jnp.concatenate([share] + near, axis=0)
    far = shift(merged, "zh", 1)
    merged_beside = shift(merged, "c", 1)
    left = ready_rows(amp, mines, theirs, entire)
    acc, ready2 = add_tiles(amp, left, [ready0], [(merged, 1), (merged_beside, 1)])
    own, _ = add_tiles(amp, own_left, [(*ready2, 0, 1536)], [], own)
    far, acc, own = lax.optimization_barrier((far, acc, own))
    far_beside = shift(far, "c", 1)
    acc, ready3 = add_tiles(amp, left, [], [(far, 0)], acc)
    sent, ready4 = add_tiles(amp, left, [], [(far_beside, 0)], acc, narrow=True)
    arrived = [shift(sent[k], "x", by) for k, by in ((2, 2), (0, -1), (1, 1))]
    own, _ = add_tiles(amp, own_left, [(*ready2, 1536, 3072), ready3, ready4], [], own)
    mine, theirs = own[0, :32], own[0, 32:]
    for part in arrived:
        theirs = theirs + part[32:].astype(F32)
    for part in arrived:
        mine = mine + part[:32].astype(F32)
    result = mine + shift(theirs, "zl", 1)
    return result.T + noise[0] * vectors.astype(F32)


def solution(mesh):
    fine = Mesh(mesh.devices.reshape(SIZES), NAMES)
    placed = (P(BLK, "zl"), P(BLK, "zl"), P(), P(), P())
    return jax.shard_map(
        per_device, mesh=fine, in_specs=placed, out_specs=P(BLK, "zl"), check_vma=False
    )
```

```python
import jax
import jax.numpy as jnp
from jax import lax
from jax.experimental import pallas as pl
from jax.experimental.pallas import tpu as pltpu
from jax.sharding import Mesh, PartitionSpec as P

SIZES = (2, 4, 4, 2, 2)
NAMES = ("zh", "x", "y", "c", "zl")
BLK = ("zh", "x", "y", "c")
TM = 512
TN = 1024
F32 = jnp.float32
BF16 = jnp.bfloat16
PARAMS = pltpu.CompilerParams(vmem_limit_bytes=48 << 20)


SCALE = 512


def cost(rows, cols):
    return pl.CostEstimate(flops=rows * cols * SCALE, transcendentals=0, bytes_accessed=cols * 384)


def three_parts(wide):
    hi = wide.astype(BF16).astype(F32)
    mid = (wide - hi).astype(BF16).astype(F32)
    return hi, mid, wide - hi - mid


def with_parts(features, offset, first):
    half = offset - 0.5 * jnp.sum(features * features, axis=0, keepdims=True)
    shape = (8, features.shape[1])
    row = lax.broadcasted_iota(jnp.int32, shape, 0)
    tail = jnp.where(row < 6, 1.0, 0.0)
    for place, part in enumerate(three_parts(half)):
        tail = jnp.where(row == first + place, part, tail)
    return jnp.concatenate([features, tail, jnp.zeros((56, features.shape[1]), F32)], axis=0)


def ready_rows(amp, mines, theirs, entire):
    count = len(mines)

    def body(amp_ref, *refs):
        theirs_ref, entire_ref, out_ref = refs[count:]
        for half in range(2):
            features = entire_ref[64 * half : 64 * half + 64, :].astype(F32)
            out_ref[count, :, 512 * half : 512 * half + 512] = with_parts(features, amp_ref[1], 3).astype(BF16)
        for k in range(count):
            for half in range(2):
                low = 32 * half
                mine = refs[k][low : low + 32, :].astype(F32)
                other = theirs_ref[64 * k + low : 64 * k + low + 32, :].astype(F32)
                features = jnp.concatenate([mine, other], axis=0)
                out_ref[k, :, 512 * half : 512 * half + 512] = with_parts(features, amp_ref[1], 3).astype(BF16)

    return pl.pallas_call(
        body,
        out_shape=jax.ShapeDtypeStruct((count + 1, 128, 1024), BF16),
        in_specs=[pl.BlockSpec(memory_space=pltpu.SMEM)]
        + [pl.BlockSpec(memory_space=pltpu.VMEM)] * (count + 2),
        out_specs=pl.BlockSpec(memory_space=pltpu.VMEM),
        compiler_params=PARAMS,
        name="ready_rows",
    )(amp, *mines, theirs, entire)


def kept_in_hbm(array):
    return pltpu.with_memory_space_constraint(array, pltpu.HBM)


def first_pack(zl, points, vectors, lengthscale):
    def body(zl_ref, points_in, vectors_in, length_in, out_ref, kept_ref, points_ref, vectors_ref, length_ref, sems):
        copies = [
            pltpu.make_async_copy(length_in, length_ref, sems.at[0]),
            pltpu.make_async_copy(points_in, points_ref, sems.at[1]),
            pltpu.make_async_copy(vectors_in, vectors_ref, sems.at[2]),
        ]
        for copy in copies:
            copy.start()
        for copy in copies:
            copy.wait()
        at = zl_ref[0]
        lane = lax.broadcasted_iota(jnp.int32, (32, 64), 1)
        row = lax.broadcasted_iota(jnp.int32, (32, 64), 0)
        column = jnp.sum(jnp.where(lane == row + 32 * at, length_ref[...], 0.0), axis=1, keepdims=True)
        scaled = (points_ref[...].astype(F32) / column).astype(BF16)
        out_ref[:32] = scaled[:, :512]
        out_ref[32:64] = scaled[:, 512:]
        given = vectors_ref[...].astype(F32)
        out_ref[64:] = jnp.where(at == 0, given[:, 512:], given[:, :512]).astype(BF16)
        kept_ref[...] = jnp.where(at == 0, given[:, :512], given[:, 512:]).astype(BF16)

    return pl.pallas_call(
        body,
        out_shape=(jax.ShapeDtypeStruct((96, 512), BF16), jax.ShapeDtypeStruct((32, 512), BF16)),
        in_specs=[pl.BlockSpec(memory_space=pltpu.SMEM)] + [pl.BlockSpec(memory_space=pltpu.HBM)] * 3,
        out_specs=(pl.BlockSpec(memory_space=pltpu.VMEM),) * 2,
        scratch_shapes=[
            pltpu.VMEM((32, 1024), BF16),
            pltpu.VMEM((32, 1024), BF16),
            pltpu.VMEM((1, 64), F32),
            pltpu.SemaphoreType.DMA((3,)),
        ],
        compiler_params=PARAMS,
        name="first_pack",
    )(zl, *(kept_in_hbm(a) for a in (points, vectors, lengthscale.reshape(1, 64))))


def copy_of(parts, rows, token, weight):
    def body(token_ref, *refs):
        at = 0
        for ref in refs[:-1]:
            refs[-1][at : at + rows] = ref[:rows]
            at += rows

    return pl.pallas_call(
        body,
        out_shape=jax.ShapeDtypeStruct((rows * len(parts), parts[0].shape[1]), BF16),
        in_specs=[pl.BlockSpec(memory_space=pl.ANY)]
        + [pl.BlockSpec(memory_space=pltpu.VMEM)] * len(parts),
        out_specs=pl.BlockSpec(memory_space=pltpu.VMEM),
        compiler_params=PARAMS,
        cost_estimate=cost(weight, 1024),
        name="copy_of",
    )(token, *parts)


def second_pack(zl, amp, half, got, kept):
    def body(zl_ref, amp_ref, half_ref, got_ref, kept_ref, rows_ref, share_ref, entire_ref):
        first = zl_ref[0] == 0
        mine = half_ref[...].astype(F32)
        theirs = got_ref[...].astype(F32)
        low = jnp.concatenate([mine[:32], theirs[:32]], axis=0)
        high = jnp.concatenate([mine[32:], theirs[32:64]], axis=0)
        entire_ref[...] = jnp.concatenate([low, high], axis=0).astype(BF16)
        picked = jnp.where(first, low, high)
        share_ref[...] = jnp.concatenate([picked, kept_ref[...].astype(F32), theirs[64:]], axis=0).astype(BF16)
        for k, features in enumerate((low, high)):
            rows_ref[0, :, 512 * k : 512 * k + 512] = with_parts(features, amp_ref[1], 3).astype(BF16)

    return pl.pallas_call(
        body,
        out_shape=[jax.ShapeDtypeStruct((1, 128, 1024), BF16)] + [jax.ShapeDtypeStruct((128, 512), BF16)] * 2,
        in_specs=[pl.BlockSpec(memory_space=pltpu.SMEM)] * 2 + [pl.BlockSpec(memory_space=pltpu.VMEM)] * 3,
        out_specs=[pl.BlockSpec(memory_space=pltpu.VMEM)] * 3,
        compiler_params=PARAMS,
        name="second_pack",
    )(zl, amp, half, got, kept)


def one_block(left, right, vectors, top):
    exponent = jnp.dot(right, left, preferred_element_type=F32)
    block = jnp.minimum(jnp.exp(exponent).astype(BF16), top)
    return jnp.dot(vectors, block, preferred_element_type=F32)


def ready_sum(lefts, pairs, top):
    sums = [jnp.zeros((64, TM), F32) for _ in lefts]
    for right_ref, vectors_ref in pairs:
        total = right_ref.shape[0]
        for at in range(0, total, TN):
            part = slice(at, min(at + TN, total))
            for k, left in enumerate(lefts):
                sums[k] += one_block(left, right_ref[part, :], vectors_ref[:, part], top)
    return sums


def raw_sum(lefts, raws, right_ref, vectors_ref, top):
    total = right_ref.shape[0]
    sums = [jnp.zeros((64, TM), F32) for _ in lefts]
    at = 0
    rights, turned = [], []
    for ref, start in raws:
        for sub in range(128 * start, ref.shape[0], 128):
            features = ref[sub : sub + 64, :].astype(F32)
            rights.append(with_parts(features, 0.0, 0).T.astype(BF16))
            turned.append(ref[sub + 64 : sub + 128, :])
            right_ref[at : at + 512, :] = rights[-1]
            vectors_ref[:, at : at + 512] = turned[-1]
            at += 512
            if len(rights) * 512 == TN or at == total:
                right = jnp.concatenate(rights, axis=0)
                vectors = jnp.concatenate(turned, axis=1)
                for k, left in enumerate(lefts):
                    sums[k] += one_block(left, right, vectors, top)
                rights, turned = [], []
    return sums


def add_tiles(amp, left, ready, raws, before=None, narrow=False, weight=1024):
    count = left.shape[0]
    flat = [part for pair in ready for part in pair]
    total = sum(4 * raw.shape[0] - 512 * start for raw, start in raws)
    cols = total + sum(right.shape[0] for right, _ in ready)
    old = [] if before is None else [before]
    sums = count if narrow else 1
    ends = [len(flat), len(raws), len(old), sums]

    def body(amp_ref, left_ref, *refs):
        groups = []
        for size in ends:
            groups.append(refs[:size])
            refs = refs[size:]
        flat_refs, raw_refs, before_refs, sum_refs = groups
        pairs = [(flat_refs[2 * k], flat_refs[2 * k + 1]) for k in range(len(ready))]
        step = pl.program_id(0)
        top = jnp.full((1, 1), amp_ref[0], F32).astype(BF16)

        def put(value):
            if before_refs:
                value += before_refs[0][0]
            if not narrow:
                sum_refs[0][0] = value
                return
            for k in range(count):

                @pl.when(step == k)
                def _():
                    sum_refs[k][...] = value.astype(BF16)

        def tiles(fresh):
            lefts = [left_ref[0, :, at : at + TM] for at in range(0, 1024, TM)]
            sums = ready_sum(lefts, pairs if fresh or not raws else pairs + [tuple(refs)], top)
            if fresh:
                starts = [(ref, start) for ref, (_, start) in zip(raw_refs, raws)]
                sums = [a + b for a, b in zip(sums, raw_sum(lefts, starts, *refs, top))]
            put(jnp.concatenate(sums, axis=1))

        if not raws:
            tiles(False)
            return

        @pl.when(step == 0)
        def _():
            tiles(True)

        @pl.when(step > 0)
        def _():
            tiles(False)


    def whole(array):
        return pl.BlockSpec(array.shape, lambda i: (0, 0))

    acc_spec = pl.BlockSpec((1, 64, 1024), lambda i: (i, 0, 0))
    if narrow:
        sum_shapes = [jax.ShapeDtypeStruct((64, 1024), BF16)] * count
        sum_specs = [whole(part) for part in sum_shapes]
    else:
        sum_shapes = [jax.ShapeDtypeStruct((count, 64, 1024), F32)]
        sum_specs = [acc_spec]
    made = []
    if raws:
        made = [jax.ShapeDtypeStruct((total, 128), BF16), jax.ShapeDtypeStruct((64, total), BF16)]
    out = pl.pallas_call(
        body,
        grid=(count,),
        out_shape=sum_shapes + made,
        in_specs=[
            pl.BlockSpec(memory_space=pltpu.SMEM),
            pl.BlockSpec((1, 128, 1024), lambda i: (i, 0, 0)),
        ]
        + [whole(part) for part in flat]
        + [whole(raw) for raw, _ in raws]
        + [acc_spec] * len(old),
        out_specs=sum_specs + [whole(part) for part in made],
        compiler_params=PARAMS,
        cost_estimate=cost(weight * count, cols),
        name="add_tiles",
    )(amp, left, *flat, *[raw for raw, _ in raws], *old)
    return (out[:sums] if narrow else out[0]), tuple(out[sums:])


def shift(value, axis, by):
    size = SIZES[NAMES.index(axis)]
    return lax.ppermute(value, axis, [(i, (i + by) % size) for i in range(size)])


def per_device(points, vectors, lengthscale, outscale, noise):
    zl = lax.axis_index("zl").astype(jnp.int32).reshape(1)
    amp = jnp.concatenate([outscale, jnp.log(outscale)])

    given, kept = first_pack(zl, points.T, vectors.T, lengthscale)
    got = shift(given, "zl", 1)
    half = copy_of([given], 64, kept, 4096)
    mines = [shift(half, "x", by) for by in (1, -1)]
    own_left, share, entire = second_pack(zl, amp, half, got, kept)

    beside = shift(share, "c", 1)
    near = [shift(share, "y", by) for by in (1, 2, -1)]
    entire = shift(entire, "x", 2)
    mined = copy_of(mines, 64, share, 16)
    mined, beside, entire = lax.optimization_barrier((mined, beside, entire))
    theirs = shift(mined, "zl", 1)
    own, ready0 = add_tiles(amp, own_left, [], [(share, 0), (beside, 0)], weight=4096)
    near[0], near[1], near[2], own = lax.optimization_barrier((near[0], near[1], near[2], own))
    merged = jnp.concatenate([share] + near, axis=0)
    far = shift(merged, "zh", 1)
    merged_beside = shift(merged, "c", 1)
    left = ready_rows(amp, mines, theirs, entire)
    acc, ready2 = add_tiles(amp, left, [ready0], [(merged, 1), (merged_beside, 1)])
    far, acc = lax.optimization_barrier((far, acc))
    far_beside = shift(far, "c", 1)
    acc, ready3 = add_tiles(amp, left, [], [(far, 0)], acc)
    sent, ready4 = add_tiles(amp, left, [], [(far_beside, 0)], acc, narrow=True)
    arrived = [shift(sent[k], "x", by) for k, by in ((2, 2), (0, -1), (1, 1))]
    own, _ = add_tiles(amp, own_left, [ready2, ready3, ready4], [], own)
    mine, theirs = own[0, :32], own[0, 32:]
    for part in arrived:
        theirs = theirs + part[32:].astype(F32)
    for part in arrived:
        mine = mine + part[:32].astype(F32)
    result = mine + shift(theirs, "zl", 1)
    return result.T + noise[0] * vectors.astype(F32)


def solution(mesh):
    fine = Mesh(mesh.devices.reshape(SIZES), NAMES)
    placed = (P(BLK, "zl"), P(BLK, "zl"), P(), P(), P())
    return jax.shard_map(
        per_device, mesh=fine, in_specs=placed, out_specs=P(BLK, "zl"), check_vma=False
    )
```
